32 devices in a mesh: fsdp: 8 (over y, x, core), tp: 4 (over z).
Axes of the slice: x: 2, y: 2, z: 4, core: 2. Of those that a mesh axis runs over, the one named last changes fastest.
Arguments:
- tokens: bfloat16 [16384, 1024], P(('fsdp', 'tp')), may hold values from -6 to 6
- lengths: int32 [8, 4], P('fsdp'), may hold values from 1 to 1024, 2048 in all within a row
- rates: float32 [8], P('tp'), may hold values from 0.00012207031 to 0.03
- w_query: bfloat16 [1024, 1024], P('fsdp', 'tp'), may hold values from -0.1875 to 0.1875
- w_key: bfloat16 [1024, 1024], P('fsdp', 'tp'), may hold values from -0.1875 to 0.1875
- w_value: bfloat16 [1024, 1024], P('fsdp', 'tp'), may hold values from -0.1875 to 0.1875
- w_update: bfloat16 [1024, 1024], P('fsdp', 'tp'), may hold values from -0.1875 to 0.1875
- w_output: bfloat16 [1024, 1024], P('tp', 'fsdp'), may hold values from -0.25 to 0.25
- w_gate: bfloat16 [1024, 2816], P('fsdp', 'tp'), may hold values from -0.1875 to 0.1875
- w_up: bfloat16 [1024, 2816], P('fsdp', 'tp'), may hold values from -0.1875 to 0.1875
- w_down: bfloat16 [2816, 1024], P('tp', 'fsdp'), may hold values from -0.109375 to 0.109375
- out_grad: bfloat16 [16384, 1024], P(('fsdp', 'tp')), may hold values from -6 to 6
Outputs:
- result: bfloat16 [16384, 1024], P(('fsdp', 'tp'))
- d_tokens: float32 [16384, 1024], P(('fsdp', 'tp'))
- g_query: float32 [1024, 1024], P('fsdp', 'tp')
- g_key: float32 [1024, 1024], P('fsdp', 'tp')
- g_value: float32 [1024, 1024], P('fsdp', 'tp')
- g_update: float32 [1024, 1024], P('fsdp', 'tp')
- g_output: float32 [1024, 1024], P('tp', 'fsdp')
- g_gate: float32 [1024, 2816], P('fsdp', 'tp')
- g_up: float32 [1024, 2816], P('fsdp', 'tp')
- g_down: float32 [2816, 1024], P('tp', 'fsdp')
The draws below stay inside these ranges and needn't reach their ends.
Inputs may be any that keep to these rules, and one draw needn't show every extreme that they name: Each row of lengths sums to 2048; its largest entry is 1024 exactly; the last entry counts padded slots.
All inputs are finite; a program needn't handle non-finite values.
Results may differ from the reference program's by a relative error of at most 0.015.
Values may be sent and summed in bfloat16 or wider, within the bound.
A program may use at most 192 MiB of HBM per device.

```python
import math
import jax
import jax.numpy as jnp
import numpy as np
from jax import lax

D = 1024
HEADS = 8
HEAD_DIM = 128
FF = 2816
SLOTS = 4
GROUP = 2048
TOKENS = 16384
N_FSDP = 8


def levels(stream_key, dims, split, smallest, largest):
    level = 1.0
    for dim, blocks in split:
        heights = jax.random.uniform(jax.random.fold_in(jax.random.fold_in(stream_key, 6), dim), (blocks,), jnp.float32, smallest / len(split), largest / len(split))
        level = level * jnp.repeat(jnp.exp(heights), dims[dim] // blocks).reshape((-1,) + (1,) * (len(dims) - 1 - dim))
    return level


def length_profile(count, total, reach, slope):
    weights = [(1 << 20) // math.isqrt(grade ** slope) + 1 for grade in range(2, count + 1)]
    rest, given = total - reach - (count - 1), [1] * (count - 1)
    while rest > 0:
        movable = [i for i in range(count - 1) if given[i] < reach]
        pool, budget = sum([weights[i] for i in movable]), rest
        for i in movable:
            addition = min(reach - given[i], max(1, budget * weights[i] // pool), rest)
            given[i] = given[i] + addition
            rest = rest - addition
    return np.array([reach] + given)


def uneven_parts(stream_key, amount, total, most, lean):
    if amount == 2:
        one = jax.random.randint(stream_key, (), max(1, total - most), min(most, total - 1) + 1)
        return jnp.stack([one, total - one])
    tallies = jnp.asarray(length_profile(amount, total, most, lean), jnp.int32)
    couples = (amount - 1) // 2
    source_of, taker = tallies[1:1 + 2 * couples:2], tallies[2:2 + 2 * couples:2]
    margin = jnp.minimum(source_of - 1, most - taker)
    passed = jax.random.randint(jax.random.fold_in(stream_key, 1), (couples,), 0, 1 << 20) % (margin + 1)
    tallies = tallies.at[1:1 + 2 * couples:2].set(source_of - passed).at[2:2 + 2 * couples:2].set(taker + passed)
    return tallies[jax.random.permutation(jax.random.fold_in(stream_key, 2), amount)]


def gaussian(rng, shape, spread, limit, cuts=(), held_as=jnp.bfloat16):
    result = spread * jax.random.normal(rng, shape, jnp.float32)
    if cuts:
        result = result * levels(rng, shape, cuts, -0.22, 0.18)
    return jnp.clip(result, -limit, limit).astype(held_as)


def setup_inputs(seed: int = 0) -> dict:
    splits = jax.random.split(jax.random.key(seed), 13)
    return {
        "tokens": gaussian(splits[0], (TOKENS, D), 1.0, 6.0, ((0, 32),)),
        "lengths": jax.vmap(lambda own: uneven_parts(own, SLOTS, GROUP, GROUP // 2, 1))(jax.random.split(splits[1], N_FSDP)).reshape((N_FSDP, SLOTS)).astype(jnp.int32),
        "rates": jnp.clip(jnp.exp(math.log(0.03) - 5.5043554 * jax.random.uniform(splits[2], (HEADS,), jnp.float32) ** levels(splits[2], (HEADS,), ((0, 4),), -0.2, 0.2)), 0.00012207031, 0.03),
        "w_query": gaussian(splits[3], (D, D), D ** -0.5, 0.1875, ((0, 8), (1, 4))),
        "w_key": gaussian(splits[4], (D, D), D ** -0.5, 0.1875, ((0, 8), (1, 4))),
        "w_value": gaussian(splits[5], (D, D), D ** -0.5, 0.1875, ((0, 8), (1, 4))),
        "w_update": gaussian(splits[6], (D, D), D ** -0.5, 0.1875, ((0, 8), (1, 4))),
        "w_output": gaussian(splits[7], (D, D), (D // 2) ** -0.5, 0.25, ((0, 4), (1, 8))),
        "w_gate": gaussian(splits[8], (D, FF), D ** -0.5, 0.1875, ((0, 8), (1, 4))),
        "w_up": gaussian(splits[9], (D, FF), D ** -0.5, 0.1875, ((0, 8), (1, 4))),
        "w_down": gaussian(splits[10], (FF, D), FF ** -0.5, 0.109375, ((0, 4), (1, 8))),
        "out_grad": gaussian(splits[11], (TOKENS, D), 1.0, 6.0, ((0, 32),)),
    }


epsilon = 1e-06
head_floor = 1.0
highest = lax.Precision.HIGHEST

@jax.custom_vjp
def low(v):
    return lax.optimization_barrier(v.astype(jnp.bfloat16)).astype(jnp.float32)

@jax.custom_vjp
def low_back(v):
    return v

def low_keep(v):
    return (low(v), None)

def low_pass(kept, grad):
    return (grad,)

def back_keep(v):
    return (v, None)

def back_low(kept, grad):
    return (low(grad),)
low.defvjp(low_keep, low_pass)
low_back.defvjp(back_keep, back_low)

def swish(values):
    return values * jax.nn.sigmoid(values)

def rms_scale(values, offset=epsilon):
    return lax.rsqrt(lax.optimization_barrier(jnp.mean(values * values, axis=-1, keepdims=True)) + offset)

def layout(lengths_row, group_rows):
    lengths_int = lengths_row.astype(jnp.int32)
    ends = jnp.cumsum(lengths_int, dtype=jnp.int32).astype(jnp.int32)
    places = jnp.arange(group_rows, dtype=jnp.int32)
    segment_ids = lax.optimization_barrier(jnp.sum((places[:, None] >= ends[None, :]).astype(jnp.int32), axis=1, dtype=jnp.int32)).astype(jnp.int32)
    starts = (ends - lengths_int).astype(jnp.int32)
    slot_ids = jnp.arange(SLOTS, dtype=jnp.int32)
    zero_int = jnp.zeros((), jnp.int32)
    first_place = lax.optimization_barrier(jnp.sum(jnp.where(segment_ids[:, None] == slot_ids[None, :], starts[None, :], zero_int), axis=1, dtype=jnp.int32)).astype(jnp.int32)
    positions = (places - first_place).astype(jnp.float32)
    live_rows = (segment_ids < SLOTS - 1).astype(jnp.float32)
    return (segment_ids, places, positions, live_rows)

def angles(positions, head_width):
    half_width = head_width // 2
    frequency = 10000.0 ** (-2.0 * jnp.arange(half_width, dtype=jnp.float32) / head_width)
    turned = positions[:, None] * frequency[None, :]
    return (jnp.cos(turned)[:, None, :], jnp.sin(turned)[:, None, :])

def rotate(values, cos_table, sin_table):
    half_width = values.shape[-1] // 2
    front_half = values[..., :half_width]
    back_half = values[..., half_width:]
    return jnp.concatenate([front_half * cos_table - back_half * sin_table, front_half * sin_table + back_half * cos_table], axis=-1)

def decay_table(rates, seg_block, segment_ids, place_block, places):
    rates_f = rates.astype(jnp.float32)
    gaps = (place_block[:, None] - places[None, :]).astype(jnp.int32)
    allowed = (seg_block[:, None] == segment_ids[None, :]) & (gaps >= 0)
    spans = jnp.maximum(gaps, 0).astype(jnp.float32)
    factors = jnp.exp(-rates_f[:, None, None] * spans[None, :, :])
    return jnp.where(allowed[None, :, :], factors, jnp.zeros_like(factors))

def attend(query, key_rows, value_rows, rates, segment_ids, places):
    group_rows = query.shape[0]
    block_rows = min(512, group_rows)

    def one_block(block_index):
        first_row = (block_index * block_rows).astype(jnp.int32)
        query_block = lax.dynamic_slice_in_dim(query, first_row, block_rows, 0)
        seg_block = lax.dynamic_slice_in_dim(segment_ids, first_row, block_rows, 0)
        place_block = lax.dynamic_slice_in_dim(places, first_row, block_rows, 0)
        raw_scores = low_back(jnp.einsum('thd,shd->hts', query_block, key_rows, precision=highest))
        decay = decay_table(rates, seg_block, segment_ids, place_block, places)
        weights = low(raw_scores * decay)
        return jnp.einsum('hts,shd->thd', weights, value_rows, precision=highest)
    blocks = lax.map(jax.checkpoint(one_block), jnp.arange(group_rows // block_rows, dtype=jnp.int32))
    return blocks.reshape(query.shape)

def layer(tokens_f, lengths_row, rates, w_query, w_key, w_value, w_update, w_output, w_gate, w_up, w_down):
    group_rows = tokens_f.shape[0]
    segment_ids, places, positions, live_rows = layout(lengths_row, group_rows)
    cos_table, sin_table = angles(positions, HEAD_DIM)
    shape_heads = (group_rows, HEADS, HEAD_DIM)
    normed1 = low(tokens_f * rms_scale(tokens_f))
    query_pre = low_back(jnp.dot(normed1, w_query, precision=highest))
    key_pre = low_back(jnp.dot(normed1, w_key, precision=highest))
    value_pre = low_back(jnp.dot(normed1, w_value, precision=highest))
    update_pre = low_back(jnp.dot(normed1, w_update, precision=highest))
    query = low(rotate(swish(query_pre).reshape(shape_heads), cos_table, sin_table))
    key_rows = low(rotate(swish(key_pre).reshape(shape_heads), cos_table, sin_table))
    value_rows = low(value_pre).reshape(shape_heads)
    update = swish(update_pre)
    attn = low_back(attend(query, key_rows, value_rows, rates, segment_ids, places))
    normed_attn = (attn * rms_scale(attn, head_floor)).reshape(group_rows, HEADS * HEAD_DIM)
    mixed = low(normed_attn * update)
    branch = low_back(jnp.dot(mixed, w_output, precision=highest))
    middle = tokens_f + branch
    normed2 = low(middle * rms_scale(middle))
    gate_rows = low_back(jnp.dot(normed2, w_gate, precision=highest))
    up_rows = low_back(jnp.dot(normed2, w_up, precision=highest))
    hidden = low(gate_rows * up_rows)
    second = low_back(jnp.dot(hidden, w_down, precision=highest))
    return middle + second

def reference(tokens, lengths, rates, w_query, w_key, w_value, w_update, w_output, w_gate, w_up, w_down, out_grad):
    weights = (w_query, w_key, w_value, w_update, w_output, w_gate, w_up, w_down)
    weights = tuple((weight.astype(jnp.float32) for weight in weights))
    rates_f = rates.astype(jnp.float32)
    token_groups = tokens.astype(jnp.float32).reshape(N_FSDP, GROUP, D)
    grad_groups = out_grad.astype(jnp.float32).reshape(N_FSDP, GROUP, D)
    lengths_int = lengths.astype(jnp.int32)

    def one_group(totals, item):
        group_tokens, group_grad, lengths_row = item
        live_rows = layout(lengths_row, GROUP)[3]
        cotangent = group_grad * live_rows[:, None]

        def forward(tokens_f, *weight_args):
            return layer(tokens_f, lengths_row, rates_f, *weight_args)
        output, pull_back = jax.vjp(forward, group_tokens, *weights)
        grads = pull_back(cotangent)
        totals = tuple((total + grad for total, grad in zip(totals, grads[1:])))
        return (totals, (output, grads[0]))
    start_totals = tuple((jnp.zeros(weight.shape, jnp.float32) for weight in weights))
    totals, (outputs, input_grads) = lax.scan(one_group, start_totals, (token_groups, grad_groups, lengths_int))
    return (outputs.reshape(TOKENS, D).astype(jnp.bfloat16), input_grads.reshape(TOKENS, D), totals[0], totals[1], totals[2], totals[3], totals[4], totals[5], totals[6], totals[7])
```

```python
import jax
import jax.numpy as jnp
from jax import lax
from jax.sharding import PartitionSpec as P

HEAD_DIM = 128
SLOTS = 4

epsilon = 1e-06
head_floor = 1.0
AXES = ("fsdp", "tp")


def swish(values):
    return values * jax.nn.sigmoid(values)


def swish_slope(values):
    sigma = jax.nn.sigmoid(values)
    return sigma * (1.0 + values * (1.0 - sigma))


def rms_scale(values, offset=epsilon):
    return lax.rsqrt(jnp.mean(values * values, axis=-1, keepdims=True) + offset)


def norm_back(values, scale, grads):
    normed = values * scale
    return scale * (grads - normed * jnp.mean(grads * normed, axis=-1, keepdims=True))


def segment_of(places, ends):
    return jnp.sum((places[..., None] >= ends).astype(jnp.int32), axis=-1, dtype=jnp.int32)


def rotate(values, cos_table, sin_table):
    half = values.shape[-1] // 2
    front, back = values[..., :half], values[..., half:]
    return jnp.concatenate(
        [front * cos_table - back * sin_table, front * sin_table + back * cos_table], axis=-1
    )


def rotate_back(values, cos_table, sin_table):
    return rotate(values, cos_table, -sin_table)


def mm(left, right):
    return jnp.dot(left, right, preferred_element_type=jnp.float32)


def mm_trans(left, right):
    return lax.dot_general(
        left, right, (((1,), (1,)), ((), ())), preferred_element_type=jnp.float32
    )


def mm_inner(left, right):
    return lax.dot_general(
        left, right, (((0,), (0,)), ((), ())), preferred_element_type=jnp.float32
    )


def heads_dot(spec, left, right):
    return jnp.einsum(spec, left, right, preferred_element_type=jnp.float32)


def gather_full(shard, row_axis, column_axis):
    part = lax.all_gather(shard, "tp", axis=0 if row_axis == "tp" else 1, tiled=True)
    return lax.all_gather(part, "fsdp", axis=0 if row_axis == "fsdp" else 1, tiled=True)


def scatter_grad(grad, row_axis, column_axis):
    part = grad.astype(jnp.bfloat16)
    part = lax.psum_scatter(
        part, "fsdp", scatter_dimension=0 if row_axis == "fsdp" else 1, tiled=True
    )
    part = lax.psum_scatter(part, "tp", scatter_dimension=0 if row_axis == "tp" else 1, tiled=True)
    return part.astype(jnp.float32)


def body(
    tokens,
    lengths,
    rates,
    w_query,
    w_key,
    w_value,
    w_update,
    w_output,
    w_gate,
    w_up,
    w_down,
    out_grad,
):
    tp_count = lax.axis_size("tp")
    tp_index = lax.axis_index("tp")
    rows, width = tokens.shape
    head_width = HEAD_DIM
    all_rates = lax.all_gather(rates, "tp", axis=0, tiled=True)
    heads = all_rates.shape[0]
    ends = jnp.cumsum(lengths[0], dtype=jnp.int32)
    first = tp_index * rows
    places = first + jnp.arange(rows, dtype=jnp.int32)
    segments = segment_of(places, ends)
    starts = ends - lengths[0]
    slots = jnp.arange(SLOTS, dtype=jnp.int32)
    positions = (
        places - jnp.sum(jnp.where(segments[:, None] == slots, starts, 0), axis=1)
    ).astype(jnp.float32)
    live = (segments < SLOTS - 1).astype(jnp.float32)
    frequency = 10000.0 ** (-2.0 * jnp.arange(head_width // 2, dtype=jnp.float32) / head_width)
    turned = positions[:, None] * frequency[None, :]
    cos_table, sin_table = jnp.cos(turned)[:, None, :], jnp.sin(turned)[:, None, :]

    gaps = places[:, None] - places[None, :]
    allowed = (segments[:, None] == segments[None, :]) & (gaps >= 0)
    spans = jnp.maximum(gaps, 0).astype(jnp.float32)
    decay = jnp.where(
        allowed[None], jnp.exp(-all_rates[:, None, None] * spans[None]), 0.0
    )
    blocks = jnp.arange(tp_count, dtype=jnp.int32)
    seg_before = segment_of(first - 1, ends)
    seg_after = segment_of(first + rows, ends)
    seg_last = segment_of(blocks * rows + rows - 1, ends)
    seg_first = segment_of(blocks * rows, ends)
    offsets = jnp.arange(rows, dtype=jnp.float32)

    def row_decay(distance, mask):
        return jnp.where(mask[:, None], jnp.exp(-distance[:, None] * all_rates[None]), 0.0)[
            :, :, None
        ]

    to_end = row_decay(rows - 1 - offsets, segments == segments[rows - 1])
    from_start = row_decay(offsets, segments == segments[0])
    into = row_decay(offsets + 1.0, segments == seg_before)
    out_of = row_decay(rows - offsets, segments == seg_after)

    def block_weights(mask, distance):
        distance = jnp.maximum(distance, 0).astype(jnp.float32)
        return jnp.where(mask[:, None], jnp.exp(-distance[:, None] * all_rates[None]), 0.0)

    before_weights = block_weights(
        (blocks < tp_index) & (seg_last == seg_before), (tp_index - blocks - 1) * rows
    )
    after_weights = block_weights(
        (blocks > tp_index) & (seg_first == seg_after), (blocks - tp_index - 1) * rows
    )

    tokens_f = tokens.astype(jnp.float32)
    scale1 = rms_scale(tokens_f)
    normed1 = (tokens_f * scale1).astype(jnp.bfloat16)
    query_full, key_full, value_full, update_full = (
        gather_full(w, "fsdp", "tp") for w in (w_query, w_key, w_value, w_update)
    )
    output_full = gather_full(w_output, "tp", "fsdp")
    gate_full, up_full = (gather_full(w, "fsdp", "tp") for w in (w_gate, w_up))
    down_full = gather_full(w_down, "tp", "fsdp")
    shape_heads = (rows, heads, head_width)
    query_pre = mm(normed1, query_full)
    key_pre = mm(normed1, key_full)
    value_rows = mm(normed1, value_full).astype(jnp.bfloat16).reshape(shape_heads)
    update_pre = mm(normed1, update_full)
    query = rotate(swish(query_pre).reshape(shape_heads), cos_table, sin_table).astype(jnp.bfloat16)
    key_rows = rotate(swish(key_pre).reshape(shape_heads), cos_table, sin_table).astype(
        jnp.bfloat16
    )
    update = swish(update_pre)
    key_state = heads_dot(
        "shc,shd->hcd", (key_rows * to_end).astype(jnp.bfloat16), value_rows
    ).astype(jnp.bfloat16)
    key_states = lax.all_gather(key_state, "tp", axis=0, tiled=False)
    state_in = jnp.sum(
        key_states.astype(jnp.float32) * before_weights[:, :, None, None], axis=0
    ).astype(jnp.bfloat16)
    weights = (heads_dot("thc,shc->hts", query, key_rows) * decay).astype(jnp.bfloat16)
    attn = heads_dot("hts,shd->thd", weights, value_rows) + into * heads_dot(
        "thc,hcd->thd", query, state_in
    )
    scale_attn = rms_scale(attn, head_floor)
    normed_attn = (attn * scale_attn).reshape(rows, width)
    mixed = (normed_attn * update).astype(jnp.bfloat16)
    middle = tokens_f + mm(mixed, output_full)
    scale2 = rms_scale(middle)
    normed2 = (middle * scale2).astype(jnp.bfloat16)
    gate_rows = mm(normed2, gate_full)
    up_rows = mm(normed2, up_full)
    hidden = (gate_rows * up_rows).astype(jnp.bfloat16)
    result = (middle + mm(hidden, down_full)).astype(jnp.bfloat16)

    cotangent = out_grad.astype(jnp.float32) * live[:, None]
    cot_rows = cotangent.astype(jnp.bfloat16)
    grad_down = mm_inner(hidden, cot_rows)
    d_hidden = mm_trans(cot_rows, down_full)
    d_gate = (d_hidden * up_rows).astype(jnp.bfloat16)
    d_up = (d_hidden * gate_rows).astype(jnp.bfloat16)
    grad_gate = mm_inner(normed2, d_gate)
    grad_up = mm_inner(normed2, d_up)
    d_normed2 = mm_trans(d_gate, gate_full) + mm_trans(d_up, up_full)
    d_middle = cotangent + norm_back(middle, scale2, d_normed2)
    mid_rows = d_middle.astype(jnp.bfloat16)
    d_mixed = mm_trans(mid_rows, output_full)
    grad_output = mm_inner(mixed, mid_rows)
    d_update_pre = (d_mixed * normed_attn * swish_slope(update_pre)).astype(jnp.bfloat16)
    d_attn = norm_back(attn, scale_attn, (d_mixed * update).reshape(shape_heads)).astype(
        jnp.bfloat16
    )
    query_state = heads_dot(
        "thc,thd->hcd", (query * from_start).astype(jnp.bfloat16), d_attn
    ).astype(jnp.bfloat16)
    query_states = lax.all_gather(query_state, "tp", axis=0, tiled=False)
    state_back = jnp.sum(
        query_states.astype(jnp.float32) * after_weights[:, :, None, None], axis=0
    ).astype(jnp.bfloat16)
    d_raw = (heads_dot("thd,shd->hts", d_attn, value_rows) * decay).astype(jnp.bfloat16)
    d_value = heads_dot("hts,thd->shd", weights, d_attn) + out_of * heads_dot(
        "shc,hcd->shd", key_rows, state_back
    )
    d_query = heads_dot("hts,shc->thc", d_raw, key_rows) + into * heads_dot(
        "thd,hcd->thc", d_attn, state_in
    )
    d_key = heads_dot("hts,thc->shc", d_raw, query) + out_of * heads_dot(
        "shd,hcd->shc", value_rows, state_back
    )
    d_query_pre = (
        swish_slope(query_pre) * rotate_back(d_query, cos_table, sin_table).reshape(rows, width)
    ).astype(jnp.bfloat16)
    d_key_pre = (
        swish_slope(key_pre) * rotate_back(d_key, cos_table, sin_table).reshape(rows, width)
    ).astype(jnp.bfloat16)
    d_value_pre = d_value.reshape(rows, width).astype(jnp.bfloat16)
    grads = [mm_inner(normed1, d) for d in (d_query_pre, d_key_pre, d_value_pre, d_update_pre)]
    d_normed1 = (
        mm_trans(d_query_pre, query_full)
        + mm_trans(d_key_pre, key_full)
        + mm_trans(d_value_pre, value_full)
        + mm_trans(d_update_pre, update_full)
    )
    d_tokens = d_middle + norm_back(tokens_f, scale1, d_normed1)
    return (
        result,
        d_tokens,
        *(scatter_grad(g, "fsdp", "tp") for g in grads),
        scatter_grad(grad_output, "tp", "fsdp"),
        scatter_grad(grad_gate, "fsdp", "tp"),
        scatter_grad(grad_up, "fsdp", "tp"),
        scatter_grad(grad_down, "tp", "fsdp"),
    )


def solution(mesh):
    rows = P(AXES, None)
    inner, outer = P("fsdp", "tp"), P("tp", "fsdp")
    return jax.shard_map(
        body,
        mesh=mesh,
        in_specs=(
            rows,
            P("fsdp", None),
            P("tp"),
            inner,
            inner,
            inner,
            inner,
            outer,
            inner,
            inner,
            outer,
            rows,
        ),
        out_specs=(rows, rows, inner, inner, inner, inner, outer, inner, inner, outer),
        check_vma=False,
    )
```

```python
import functools

import jax
import jax.numpy as jnp
from jax import lax
from jax.experimental import pallas as pl
from jax.experimental.pallas import tpu as pltpu
from jax.sharding import PartitionSpec as P

HEAD_DIM = 128
SLOTS = 4

epsilon = 1e-06
head_floor = 1.0
AXES = ("fsdp", "tp")


def swish(values):
    return values * jax.nn.sigmoid(values)


def swish_slope(values):
    sigma = jax.nn.sigmoid(values)
    return sigma * (1.0 + values * (1.0 - sigma))


def rms_scale(values, offset=epsilon):
    return lax.rsqrt(jnp.mean(values * values, axis=-1, keepdims=True) + offset)


def norm_back(values, scale, grads):
    normed = values * scale
    return scale * (grads - normed * jnp.mean(grads * normed, axis=-1, keepdims=True))


def segment_of(places, ends):
    return jnp.sum((places[..., None] >= ends).astype(jnp.int32), axis=-1, dtype=jnp.int32)


def rotate(values, cos_table, sin_table):
    half = values.shape[-1] // 2
    front, back = values[..., :half], values[..., half:]
    return jnp.concatenate(
        [front * cos_table - back * sin_table, front * sin_table + back * cos_table], axis=-1
    )


def rotate_back(values, cos_table, sin_table):
    return rotate(values, cos_table, -sin_table)


def mm(left, right):
    return jnp.dot(left, right, preferred_element_type=jnp.float32)


def mm_trans(left, right):
    return lax.dot_general(
        left, right, (((1,), (1,)), ((), ())), preferred_element_type=jnp.float32
    )


def mm_inner(left, right):
    return lax.dot_general(
        left, right, (((0,), (0,)), ((), ())), preferred_element_type=jnp.float32
    )


def heads_dot(spec, left, right):
    return jnp.einsum(spec, left, right, preferred_element_type=jnp.float32)


def gather_full(shard, row_axis, column_axis):
    part = lax.all_gather(shard, "tp", axis=0 if row_axis == "tp" else 1, tiled=True)
    return lax.all_gather(part, "fsdp", axis=0 if row_axis == "fsdp" else 1, tiled=True)


def scatter_grad(grad, row_axis, column_axis):
    part = grad.astype(jnp.bfloat16)
    part = lax.psum_scatter(
        part, "fsdp", scatter_dimension=0 if row_axis == "fsdp" else 1, tiled=True
    )
    part = lax.psum_scatter(part, "tp", scatter_dimension=0 if row_axis == "tp" else 1, tiled=True)
    return part.astype(jnp.float32)


MESH = pl.DeviceIdType.MESH
VMEM_BYTES = 66_000_000


def place():
    f, t = lax.axis_index("fsdp"), lax.axis_index("tp")
    return f // 4, (f // 2) % 2, f % 2, f, t


def meet(peers):
    barrier = pltpu.get_barrier_semaphore()
    for peer in peers:
        pl.semaphore_signal(barrier, inc=1, device_id=peer, device_id_type=MESH)
    pl.semaphore_wait(barrier, len(peers))


def peers_of(f, t):
    core = (f // 2 * 2 + (1 - f % 2), t)
    along_x = (f // 4 * 4 + (f + 2) % 4, t)
    along_y = ((f + 4) % 8, t)
    along_z = [(f, (t + d) % 4) for d in (1, 2, 3)]
    return core, along_x, along_y, along_z


def gather_kernel(count, *refs):
    ins, outs = refs[:count], refs[count : 2 * count]
    own_sem, z_send, z_recv, n_send, n_recv, c_send, c_recv = refs[2 * count :]
    y, x, c, f, t = place()
    core, along_x, along_y, along_z = peers_of(f, t)
    meet([core, along_x, along_y, *along_z])
    pieces = [(w, h) for w in range(count) for h in range(2)]

    def rows_of(piece):
        w, h = piece
        half = ins[w].shape[0] // 2
        return pl.ds(h * half, half)

    def slot(piece, *index):
        return outs[piece[0]].at[(*index, rows_of(piece))]

    def remote(src, dst, send, recv, peer):
        return pltpu.make_async_remote_copy(
            src_ref=src, dst_ref=dst, send_sem=send, recv_sem=recv, device_id=peer, device_id_type=MESH
        )

    def own_copy(p):
        piece = pieces[p]
        return pltpu.make_async_copy(
            ins[piece[0]].at[rows_of(piece)], slot(piece, y, x, c, t), own_sem.at[p]
        )

    def z_copy(p, d, source):
        piece = pieces[p]
        return remote(
            ins[piece[0]].at[rows_of(piece)],
            slot(piece, y, x, c, source),
            z_send.at[p, d],
            z_recv.at[p, d],
            along_z[d],
        )

    def near_copy(p, stage, arriving):
        piece = pieces[p]
        over_x = (piece[1] == 0) == (stage == 0)
        if stage == 0:
            index = (y, x, c)
            if arriving:
                index = (y, 1 - x, c) if over_x else (1 - y, x, c)
        else:
            all_ = slice(None)
            if over_x:
                index = (all_, (1 - x) if arriving else x, c)
            else:
                index = ((1 - y) if arriving else y, all_, c)
        ref = slot(piece, *index, slice(None))
        return remote(
            ref, ref, n_send.at[p, stage], n_recv.at[p, stage], along_x if over_x else along_y
        )

    def core_copy(p, part, arriving):
        piece = pieces[p]
        side = (1 - c) if arriving else c
        first_x = piece[1] == 0
        all_ = slice(None)
        index = (
            (y, x, side),
            (y, 1 - x, side) if first_x else (1 - y, x, side),
            (1 - y, all_, side) if first_x else (all_, 1 - x, side),
        )[part]
        ref = slot(piece, *index, slice(None))
        return remote(ref, ref, c_send.at[p, part], c_recv.at[p, part], core)

    total = len(pieces)

    def start_z(p):
        own_copy(p).start()
        for d in range(3):
            z_copy(p, d, t).start()

    lead = 4
    for p in range(min(lead, total)):
        start_z(p)
    lag = 2
    for step in range(total + 2 * lag):
        if lead <= step + lead < total:
            start_z(step + lead)
        p = step
        if p < total:
            own_copy(p).wait()
            for d in range(3):
                z_copy(p, d, (t + 3 - d) % 4).wait_recv()
            near_copy(p, 0, False).start()
            core_copy(p, 0, False).start()
        p = step - lag
        if 0 <= p < total:
            near_copy(p, 0, True).wait_recv()
            near_copy(p, 1, False).start()
            core_copy(p, 1, False).start()
        p = step - 2 * lag
        if 0 <= p < total:
            near_copy(p, 1, True).wait_recv()
            core_copy(p, 2, False).start()
    for p in range(total):
        for part in range(3):
            core_copy(p, part, True).wait_recv()
    for p in range(total):
        for d in range(3):
            z_copy(p, d, t).wait_send()
        for stage in range(2):
            near_copy(p, stage, False).wait_send()
        for part in range(3):
            core_copy(p, part, False).wait_send()


def gather_weights(shards):
    count = len(shards)
    pieces = 2 * count
    dma = pltpu.SemaphoreType.DMA
    return pl.pallas_call(
        functools.partial(gather_kernel, count),
        name="gather_weights",
        out_shape=[jax.ShapeDtypeStruct((2, 2, 2, 4, *s.shape), s.dtype) for s in shards],
        in_specs=[pl.BlockSpec(memory_space=pltpu.VMEM)] * count,
        out_specs=[pl.BlockSpec(memory_space=pl.ANY)] * count,
        scratch_shapes=[
            dma((pieces,)),
            dma((pieces, 3)),
            dma((pieces, 3)),
            dma((pieces, 2)),
            dma((pieces, 2)),
            dma((pieces, 3)),
            dma((pieces, 3)),
        ],
        compiler_params=pltpu.CompilerParams(collective_id=0, has_side_effects=True),
    )(*shards)


def scatter_kernel(count, *refs):
    ins, outs = refs[:count], refs[count : 2 * count]
    rest = refs[2 * count :]
    mine, from_core, from_near, from_far, from_z = (
        rest[i * count : (i + 1) * count] for i in range(5)
    )
    own_sem, c_send, c_recv, n_send, n_recv, z_send, z_recv = rest[5 * count :]
    y, x, c, f, t = place()
    core, along_x, along_y, along_z = peers_of(f, t)
    meet([core, along_x, along_y, *along_z])
    pieces = [(w, h) for w in range(count) for h in range(2)]
    total = len(pieces)
    all_ = slice(None)

    def rows_of(p):
        w, h = pieces[p]
        half = outs[w].shape[0] // 2
        return pl.ds(h * half, half)

    def remote(src, dst, send, recv, peer):
        return pltpu.make_async_remote_copy(
            src_ref=src, dst_ref=dst, send_sem=send, recv_sem=recv, device_id=peer, device_id_type=MESH
        )

    def own_copy(p):
        w, rows = pieces[p][0], rows_of(p)
        return pltpu.make_async_copy(
            ins[w].at[:, :, c, :, rows], mine[w].at[:, :, :, rows], own_sem.at[p]
        )

    def core_copy(p):
        w, rows = pieces[p][0], rows_of(p)
        return remote(
            ins[w].at[:, :, 1 - c, :, rows],
            from_core[w].at[:, :, :, rows],
            c_send.at[p],
            c_recv.at[p],
            core,
        )

    def near_copy(p):
        (w, h), rows = pieces[p], rows_of(p)
        src = mine[w].at[1 - y, :, :, rows] if h == 0 else mine[w].at[:, 1 - x, :, rows]
        return remote(
            src,
            from_near[w].at[:, :, rows],
            n_send.at[p, 0],
            n_recv.at[p, 0],
            along_y if h == 0 else along_x,
        )

    def far_copy(p):
        (w, h), rows = pieces[p], rows_of(p)
        src = mine[w].at[y, 1 - x, :, rows] if h == 0 else mine[w].at[1 - y, x, :, rows]
        return remote(
            src,
            from_far[w].at[:, rows],
            n_send.at[p, 1],
            n_recv.at[p, 1],
            along_x if h == 0 else along_y,
        )

    def z_copy(p, d):
        w, rows = pieces[p][0], rows_of(p)
        return remote(
            mine[w].at[y, x, (t + d + 1) % 4, rows],
            from_z[w].at[d, rows],
            z_send.at[p, d],
            z_recv.at[p, d],
            along_z[d],
        )

    def add(steps, target, other):
        def step(i, carry):
            into, term = target(i), other(i)
            into[...] = (into[...].astype(jnp.float32) + term[...].astype(jnp.float32)).astype(
                jnp.bfloat16
            )
            return carry

        lax.fori_loop(0, steps, step, 0)

    def start(p):
        core_copy(p).start()
        own_copy(p).start()

    lead, lag = 4, 2
    for p in range(min(lead, total)):
        start(p)
    for step in range(total + 3 * lag):
        if lead <= step + lead < total:
            start(step + lead)
        p = step
        if p < total:
            (w, h), rows = pieces[p], rows_of(p)
            own_copy(p).wait()
            core_copy(p).wait_recv()
            add(
                16,
                lambda i: mine[w].at[i // 8, i // 4 % 2, i % 4, rows],
                lambda i: from_core[w].at[i // 8, i // 4 % 2, i % 4, rows],
            )
            near_copy(p).start()
        p = step - lag
        if 0 <= p < total:
            (w, h), rows = pieces[p], rows_of(p)
            near_copy(p).wait_recv()
            if h == 0:
                into = lambda i: mine[w].at[y, i // 4, i % 4, rows]
            else:
                into = lambda i: mine[w].at[i // 4, x, i % 4, rows]
            add(8, into, lambda i: from_near[w].at[i // 4, i % 4, rows])
            far_copy(p).start()
        p = step - 2 * lag
        if 0 <= p < total:
            (w, h), rows = pieces[p], rows_of(p)
            far_copy(p).wait_recv()
            add(4, lambda i: mine[w].at[y, x, i, rows], lambda i: from_far[w].at[i, rows])
            for d in range(3):
                z_copy(p, d).start()
        p = step - 3 * lag
        if 0 <= p < total:
            (w, h), rows = pieces[p], rows_of(p)
            for d in range(3):
                z_copy(p, d).wait_recv()
            result = mine[w][y, x, t, rows].astype(jnp.float32)
            for d in range(3):
                result = result + from_z[w][d, rows].astype(jnp.float32)
            outs[w][rows] = result
    for p in range(total):
        core_copy(p).wait_send()
        near_copy(p).wait_send()
        far_copy(p).wait_send()
        for d in range(3):
            z_copy(p, d).wait_send()


def scatter_grads(grads):
    count = len(grads)
    pieces = 2 * count
    dma = pltpu.SemaphoreType.DMA
    shards = [g.shape[4:] for g in grads]

    def buffers(*lead):
        return [pltpu.VMEM((*lead, *s), jnp.bfloat16) for s in shards]

    return pl.pallas_call(
        functools.partial(scatter_kernel, count),
        name="scatter_grads",
        out_shape=[jax.ShapeDtypeStruct(s, jnp.float32) for s in shards],
        in_specs=[pl.BlockSpec(memory_space=pl.ANY)] * count,
        out_specs=[pl.BlockSpec(memory_space=pltpu.VMEM)] * count,
        scratch_shapes=[
            *buffers(2, 2, 4),
            *buffers(2, 2, 4),
            *buffers(2, 4),
            *buffers(4),
            *buffers(3),
            dma((pieces,)),
            dma((pieces,)),
            dma((pieces,)),
            dma((pieces, 2)),
            dma((pieces, 2)),
            dma((pieces, 3)),
            dma((pieces, 3)),
        ],
        compiler_params=pltpu.CompilerParams(
            collective_id=1, has_side_effects=True, vmem_limit_bytes=VMEM_BYTES
        ),
    )(*grads)


def whole_in(blocks):
    depth, width = blocks.shape[4:]
    return blocks.reshape(8, 4, depth, width).transpose(0, 2, 1, 3).reshape(8 * depth, 4 * width)


def whole_out(blocks):
    depth, width = blocks.shape[4:]
    return blocks.reshape(8, 4, depth, width).transpose(1, 2, 0, 3).reshape(4 * depth, 8 * width)


def blocks_in(grad):
    depth, width = grad.shape[0] // 8, grad.shape[1] // 4
    part = grad.astype(jnp.bfloat16).reshape(8, depth, 4, width).transpose(0, 2, 1, 3)
    return part.reshape(2, 2, 2, 4, depth, width)


def blocks_out(grad):
    depth, width = grad.shape[0] // 4, grad.shape[1] // 8
    part = grad.astype(jnp.bfloat16).reshape(4, depth, 8, width).transpose(2, 0, 1, 3)
    return part.reshape(2, 2, 2, 4, depth, width)


def body(
    by_kernels,
    tokens,
    lengths,
    rates,
    w_query,
    w_key,
    w_value,
    w_update,
    w_output,
    w_gate,
    w_up,
    w_down,
    out_grad,
):
    tp_count = lax.axis_size("tp")
    tp_index = lax.axis_index("tp")
    rows, width = tokens.shape
    head_width = HEAD_DIM
    all_rates = lax.all_gather(rates, "tp", axis=0, tiled=True)
    heads = all_rates.shape[0]
    ends = jnp.cumsum(lengths[0], dtype=jnp.int32)
    first = tp_index * rows
    places = first + jnp.arange(rows, dtype=jnp.int32)
    segments = segment_of(places, ends)
    starts = ends - lengths[0]
    slots = jnp.arange(SLOTS, dtype=jnp.int32)
    positions = (
        places - jnp.sum(jnp.where(segments[:, None] == slots, starts, 0), axis=1)
    ).astype(jnp.float32)
    live = (segments < SLOTS - 1).astype(jnp.float32)
    frequency = 10000.0 ** (-2.0 * jnp.arange(head_width // 2, dtype=jnp.float32) / head_width)
    turned = positions[:, None] * frequency[None, :]
    cos_table, sin_table = jnp.cos(turned)[:, None, :], jnp.sin(turned)[:, None, :]

    gaps = places[:, None] - places[None, :]
    allowed = (segments[:, None] == segments[None, :]) & (gaps >= 0)
    spans = jnp.maximum(gaps, 0).astype(jnp.float32)
    decay = jnp.where(
        allowed[None], jnp.exp(-all_rates[:, None, None] * spans[None]), 0.0
    )
    blocks = jnp.arange(tp_count, dtype=jnp.int32)
    seg_before = segment_of(first - 1, ends)
    seg_after = segment_of(first + rows, ends)
    seg_last = segment_of(blocks * rows + rows - 1, ends)
    seg_first = segment_of(blocks * rows, ends)
    offsets = jnp.arange(rows, dtype=jnp.float32)

    def row_decay(distance, mask):
        return jnp.where(mask[:, None], jnp.exp(-distance[:, None] * all_rates[None]), 0.0)[
            :, :, None
        ]

    to_end = row_decay(rows - 1 - offsets, segments == segments[rows - 1])
    from_start = row_decay(offsets, segments == segments[0])
    into = row_decay(offsets + 1.0, segments == seg_before)
    out_of = row_decay(rows - offsets, segments == seg_after)

    def block_weights(mask, distance):
        distance = jnp.maximum(distance, 0).astype(jnp.float32)
        return jnp.where(mask[:, None], jnp.exp(-distance[:, None] * all_rates[None]), 0.0)

    before_weights = block_weights(
        (blocks < tp_index) & (seg_last == seg_before), (tp_index - blocks - 1) * rows
    )
    after_weights = block_weights(
        (blocks > tp_index) & (seg_first == seg_after), (blocks - tp_index - 1) * rows
    )

    tokens_f = tokens.astype(jnp.float32)
    scale1 = rms_scale(tokens_f)
    normed1 = (tokens_f * scale1).astype(jnp.bfloat16)
    shards = (w_query, w_key, w_value, w_update, w_output, w_gate, w_up, w_down)
    inner = (True, True, True, True, False, True, True, False)
    if by_kernels:
        full = [
            whole_in(w) if rows_first else whole_out(w)
            for w, rows_first in zip(gather_weights(shards), inner)
        ]
    else:
        full = [
            gather_full(w, "fsdp", "tp") if rows_first else gather_full(w, "tp", "fsdp")
            for w, rows_first in zip(shards, inner)
        ]
    (
        query_full,
        key_full,
        value_full,
        update_full,
        output_full,
        gate_full,
        up_full,
        down_full,
    ) = full
    shape_heads = (rows, heads, head_width)
    query_pre = mm(normed1, query_full)
    key_pre = mm(normed1, key_full)
    value_rows = mm(normed1, value_full).astype(jnp.bfloat16).reshape(shape_heads)
    update_pre = mm(normed1, update_full)
    query = rotate(swish(query_pre).reshape(shape_heads), cos_table, sin_table).astype(jnp.bfloat16)
    key_rows = rotate(swish(key_pre).reshape(shape_heads), cos_table, sin_table).astype(
        jnp.bfloat16
    )
    update = swish(update_pre)
    key_state = heads_dot(
        "shc,shd->hcd", (key_rows * to_end).astype(jnp.bfloat16), value_rows
    ).astype(jnp.bfloat16)
    key_states = lax.all_gather(key_state, "tp", axis=0, tiled=False)
    state_in = jnp.sum(
        key_states.astype(jnp.float32) * before_weights[:, :, None, None], axis=0
    ).astype(jnp.bfloat16)
    weights = (heads_dot("thc,shc->hts", query, key_rows) * decay).astype(jnp.bfloat16)
    attn = heads_dot("hts,shd->thd", weights, value_rows) + into * heads_dot(
        "thc,hcd->thd", query, state_in
    )
    scale_attn = rms_scale(attn, head_floor)
    normed_attn = (attn * scale_attn).reshape(rows, width)
    mixed = (normed_attn * update).astype(jnp.bfloat16)
    middle = tokens_f + mm(mixed, output_full)
    scale2 = rms_scale(middle)
    normed2 = (middle * scale2).astype(jnp.bfloat16)
    gate_rows = mm(normed2, gate_full)
    up_rows = mm(normed2, up_full)
    hidden = (gate_rows * up_rows).astype(jnp.bfloat16)
    result = (middle + mm(hidden, down_full)).astype(jnp.bfloat16)

    cotangent = out_grad.astype(jnp.float32) * live[:, None]
    cot_rows = cotangent.astype(jnp.bfloat16)
    grad_down = mm_inner(hidden, cot_rows)
    d_hidden = mm_trans(cot_rows, down_full)
    d_gate = (d_hidden * up_rows).astype(jnp.bfloat16)
    d_up = (d_hidden * gate_rows).astype(jnp.bfloat16)
    grad_gate = mm_inner(normed2, d_gate)
    grad_up = mm_inner(normed2, d_up)
    d_normed2 = mm_trans(d_gate, gate_full) + mm_trans(d_up, up_full)
    d_middle = cotangent + norm_back(middle, scale2, d_normed2)
    mid_rows = d_middle.astype(jnp.bfloat16)
    d_mixed = mm_trans(mid_rows, output_full)
    grad_output = mm_inner(mixed, mid_rows)
    d_update_pre = (d_mixed * normed_attn * swish_slope(update_pre)).astype(jnp.bfloat16)
    d_attn = norm_back(attn, scale_attn, (d_mixed * update).reshape(shape_heads)).astype(
        jnp.bfloat16
    )
    query_state = heads_dot(
        "thc,thd->hcd", (query * from_start).astype(jnp.bfloat16), d_attn
    ).astype(jnp.bfloat16)
    query_states = lax.all_gather(query_state, "tp", axis=0, tiled=False)
    state_back = jnp.sum(
        query_states.astype(jnp.float32) * after_weights[:, :, None, None], axis=0
    ).astype(jnp.bfloat16)
    d_raw = (heads_dot("thd,shd->hts", d_attn, value_rows) * decay).astype(jnp.bfloat16)
    d_value = heads_dot("hts,thd->shd", weights, d_attn) + out_of * heads_dot(
        "shc,hcd->shd", key_rows, state_back
    )
    d_query = heads_dot("hts,shc->thc", d_raw, key_rows) + into * heads_dot(
        "thd,hcd->thc", d_attn, state_in
    )
    d_key = heads_dot("hts,thc->shc", d_raw, query) + out_of * heads_dot(
        "shd,hcd->shc", value_rows, state_back
    )
    d_query_pre = (
        swish_slope(query_pre) * rotate_back(d_query, cos_table, sin_table).reshape(rows, width)
    ).astype(jnp.bfloat16)
    d_key_pre = (
        swish_slope(key_pre) * rotate_back(d_key, cos_table, sin_table).reshape(rows, width)
    ).astype(jnp.bfloat16)
    d_value_pre = d_value.reshape(rows, width).astype(jnp.bfloat16)
    grads = [mm_inner(normed1, d) for d in (d_query_pre, d_key_pre, d_value_pre, d_update_pre)]
    d_normed1 = (
        mm_trans(d_query_pre, query_full)
        + mm_trans(d_key_pre, key_full)
        + mm_trans(d_value_pre, value_full)
        + mm_trans(d_update_pre, update_full)
    )
    d_tokens = d_middle + norm_back(tokens_f, scale1, d_normed1)
    grads = (*grads, grad_output, grad_gate, grad_up, grad_down)
    if by_kernels:
        grads = scatter_grads(
            [blocks_in(g) if rows_first else blocks_out(g) for g, rows_first in zip(grads, inner)]
        )
    else:
        grads = [
            scatter_grad(g, "fsdp", "tp") if rows_first else scatter_grad(g, "tp", "fsdp")
            for g, rows_first in zip(grads, inner)
        ]
    return (result, d_tokens, *grads)


def solution(mesh):
    rows = P(AXES, None)
    inner, outer = P("fsdp", "tp"), P("tp", "fsdp")
    by_kernels = mesh.shape["fsdp"] == 8 and mesh.shape["tp"] == 4
    return jax.shard_map(
        functools.partial(body, by_kernels),
        mesh=mesh,
        in_specs=(
            rows,
            P("fsdp", None),
            P("tp"),
            inner,
            inner,
            inner,
            inner,
            outer,
            inner,
            inner,
            outer,
            rows,
        ),
        out_specs=(rows, rows, inner, inner, inner, inner, outer, inner, inner, outer),
        check_vma=False,
    )
```

```python
import functools

import jax
import jax.numpy as jnp
from jax import lax
from jax.experimental import pallas as pl
from jax.experimental.pallas import tpu as pltpu
from jax.sharding import PartitionSpec as P

HEAD_DIM = 128
SLOTS = 4

epsilon = 1e-06
head_floor = 1.0
AXES = ("fsdp", "tp")


def swish(values):
    return values * jax.nn.sigmoid(values)


def swish_slope(values):
    sigma = jax.nn.sigmoid(values)
    return sigma * (1.0 + values * (1.0 - sigma))


def rms_scale(values, offset=epsilon):
    return lax.rsqrt(jnp.mean(values * values, axis=-1, keepdims=True) + offset)


def norm_back(values, scale, grads):
    normed = values * scale
    return scale * (grads - normed * jnp.mean(grads * normed, axis=-1, keepdims=True))


def segment_of(places, ends):
    return jnp.sum((places[..., None] >= ends).astype(jnp.int32), axis=-1, dtype=jnp.int32)


def rotate(values, cos_table, sin_table):
    half = values.shape[-1] // 2
    front, back = values[..., :half], values[..., half:]
    return jnp.concatenate(
        [front * cos_table - back * sin_table, front * sin_table + back * cos_table], axis=-1
    )


def rotate_back(values, cos_table, sin_table):
    return rotate(values, cos_table, -sin_table)


def mm(left, right):
    return jnp.dot(left, right, preferred_element_type=jnp.float32)


def mm_trans(left, right):
    return lax.dot_general(
        left, right, (((1,), (1,)), ((), ())), preferred_element_type=jnp.float32
    )


def mm_inner(left, right):
    return lax.dot_general(
        left, right, (((0,), (0,)), ((), ())), preferred_element_type=jnp.float32
    )


def heads_dot(spec, left, right):
    return jnp.einsum(spec, left, right, preferred_element_type=jnp.float32)


def gather_full(shard, row_axis, column_axis):
    part = lax.all_gather(shard, "tp", axis=0 if row_axis == "tp" else 1, tiled=True)
    return lax.all_gather(part, "fsdp", axis=0 if row_axis == "fsdp" else 1, tiled=True)


def scatter_grad(grad, row_axis, column_axis):
    part = grad.astype(jnp.bfloat16)
    part = lax.psum_scatter(
        part, "fsdp", scatter_dimension=0 if row_axis == "fsdp" else 1, tiled=True
    )
    part = lax.psum_scatter(part, "tp", scatter_dimension=0 if row_axis == "tp" else 1, tiled=True)
    return part.astype(jnp.float32)


MESH = pl.DeviceIdType.MESH
VMEM_BYTES = 66_000_000


def place():
    f, t = lax.axis_index("fsdp"), lax.axis_index("tp")
    return f // 4, (f // 2) % 2, f % 2, f, t


def meet(peers):
    barrier = pltpu.get_barrier_semaphore()
    for peer in peers:
        pl.semaphore_signal(barrier, inc=1, device_id=peer, device_id_type=MESH)
    pl.semaphore_wait(barrier, len(peers))


def peers_of(f, t):
    core = (f // 2 * 2 + (1 - f % 2), t)
    along_x = (f // 4 * 4 + (f + 2) % 4, t)
    along_y = ((f + 4) % 8, t)
    along_z = [(f, (t + d) % 4) for d in (1, 2, 3)]
    return core, along_x, along_y, along_z


FAR = 1e7


def swish_of(values):
    return values * jax.nn.sigmoid(values)


def segment_at(where, ends):
    return sum((where >= end).astype(jnp.int32) for end in ends)


def row_tables(lengths_ref, t, rows):
    ends, total = [], jnp.int32(0)
    for j in range(SLOTS):
        total = total + lengths_ref[0, j]
        ends.append(total)
    first = t * rows
    offsets = lax.broadcasted_iota(jnp.int32, (rows, HEAD_DIM), 0)
    return ends, first, offsets, segment_at(first + offsets, ends)


def scalar_segment(where, ends):
    return sum(jnp.where(where >= end, 1, 0) for end in ends)


def fill_span(span_ref, ends, first):
    rows = span_ref.shape[0]
    row = first + lax.broadcasted_iota(jnp.int32, (rows, rows), 0)
    column = first + lax.broadcasted_iota(jnp.int32, (rows, rows), 1)
    allowed = (segment_at(row, ends) == segment_at(column, ends)) & (row >= column)
    span_ref[...] = jnp.where(allowed, (row - column).astype(jnp.float32), FAR)


def turn(values, cos, sin):
    return values * cos + pltpu.roll(values, HEAD_DIM // 2, 1) * sin


def dot(left, right):
    return jnp.dot(left, right, preferred_element_type=jnp.float32)


def dot_nt(left, right):
    return lax.dot_general(left, right, (((1,), (1,)), ((), ())), preferred_element_type=jnp.float32)


def dot_tn(left, right):
    return lax.dot_general(left, right, (((0,), (0,)), ((), ())), preferred_element_type=jnp.float32)


ORDER = (1, 2, 0, 3, 4, 5, 6, 7)
N_W = 8
FWD_IN = ("tokens", "cos", "sin", "lengths", "rates")
FWD_OUT = (
    "result", "qp", "kp", "up", "q", "k", "v", "o", "w", "y1", "n2", "a", "g", "e", "states", "rates8",
)


def forward_kernel(*refs):
    shards, refs = refs[:N_W], refs[N_W:]
    inp = dict(zip(FWD_IN, refs))
    refs = refs[len(FWD_IN) :]
    kept, refs = refs[:N_W], refs[N_W:]
    out = dict(zip(FWD_OUT, refs))
    refs = refs[len(FWD_OUT) :]
    full, refs = refs[:N_W], refs[N_W:]
    buf = dict(zip(FWD_OUT, refs))
    refs = refs[len(FWD_OUT) :]
    n1, span, states, rate_tiles, own_sem, z_send, z_recv, n_send, n_recv, c_send, c_recv = refs[:11]
    s_send, s_recv, r_send, r_recv, keep_sem, out_sem = refs[11:]
    rows = inp["tokens"].shape[0]
    y, x, c, f, t = place()
    core, along_x, along_y, along_z = peers_of(f, t)
    rate_tiles[t] = jnp.concatenate(
        [jnp.full((1, rows), inp["rates"][i % 2], jnp.float32) for i in range(8)], axis=0
    )
    meet([core, along_x, along_y, *along_z])
    pieces = [(w, h) for w in ORDER for h in range(2)]
    total = len(pieces)
    all_ = slice(None)

    def rows_of(piece):
        w, h = piece
        half = shards[w].shape[0] // 2
        return pl.ds(h * half, half)

    def slot(piece, *index):
        return full[piece[0]].at[(*index, rows_of(piece))]

    def remote(src, dst, send, recv, peer):
        return pltpu.make_async_remote_copy(
            src_ref=src, dst_ref=dst, send_sem=send, recv_sem=recv, device_id=peer, device_id_type=MESH
        )

    def own_copy(p):
        piece = pieces[p]
        return pltpu.make_async_copy(
            shards[piece[0]].at[rows_of(piece)], slot(piece, y, x, c, t), own_sem.at[p]
        )

    def z_copy(p, d, source):
        piece = pieces[p]
        return remote(
            shards[piece[0]].at[rows_of(piece)],
            slot(piece, y, x, c, source),
            z_send.at[p, d],
            z_recv.at[p, d],
            along_z[d],
        )

    def near_copy(p, stage, arriving):
        piece = pieces[p]
        over_x = (piece[1] == 0) == (stage == 0)
        if stage == 0:
            index = (y, x, c)
            if arriving:
                index = (y, 1 - x, c) if over_x else (1 - y, x, c)
        else:
            if over_x:
                index = (all_, (1 - x) if arriving else x, c)
            else:
                index = ((1 - y) if arriving else y, all_, c)
        ref = slot(piece, *index, all_)
        return remote(
            ref, ref, n_send.at[p, stage], n_recv.at[p, stage], along_x if over_x else along_y
        )

    def core_copy(p, part, arriving):
        piece = pieces[p]
        side = (1 - c) if arriving else c
        first_x = piece[1] == 0
        index = (
            (y, x, side),
            (y, 1 - x, side) if first_x else (1 - y, x, side),
            (1 - y, all_, side) if first_x else (all_, 1 - x, side),
        )[part]
        ref = slot(piece, *index, all_)
        return remote(ref, ref, c_send.at[p, part], c_recv.at[p, part], core)

    def start_z(p):
        own_copy(p).start()
        for d in range(3):
            z_copy(p, d, t).start()

    def arrived(w):
        for h in range(2):
            for part in range(3):
                core_copy(pieces.index((w, h)), part, True).wait_recv()
        keep(w).start()

    def keep(w):
        return pltpu.make_async_copy(full[w], kept[w], keep_sem.at[w])

    def save(name):
        return pltpu.make_async_copy(buf[name], out[name], out_sem.at[FWD_OUT.index(name)])

    def rate_copy(d, source):
        ref = rate_tiles.at[source]
        return remote(ref, ref, r_send.at[d], r_recv.at[d], along_z[d])

    def state_copy(d, source):
        ref = states.at[source]
        return remote(ref, ref, s_send.at[d], s_recv.at[d], along_z[d])

    ends, first, offsets, segments = row_tables(inp["lengths"], t, rows)
    steps_f = offsets.astype(jnp.float32)

    def rate_of(h):
        return buf["rates8"][pl.ds(h, 1), :]

    def begin():
        for d in range(3):
            rate_copy(d, t).start()
        values = inp["tokens"][...].astype(jnp.float32)
        n1[...] = (values * rms_scale(values)).astype(jnp.bfloat16)
        fill_span(span, ends, first)

    def rates_here():
        for d in range(3):
            rate_copy(d, (t + 3 - d) % 4).wait_recv()
        for j in range(4):
            buf["rates8"][2 * j : 2 * j + 2] = rate_tiles[j, 0:2]
        save("rates8").start()

    def project(w, finish):
        def run():
            arrived(w)

            def block(i, carry):
                columns = full[w][:, :, :, i].reshape(n1.shape[1], full[w].shape[5])
                values = dot(n1[...], columns)
                for j in range(2):
                    finish(2 * i + j, values[:, j * HEAD_DIM : (j + 1) * HEAD_DIM])
                return carry

            lax.fori_loop(0, 4, block, 0)

        return run

    def finish_key(h, values):
        buf["kp"][h] = values.astype(jnp.bfloat16)
        buf["k"][h] = turn(swish_of(values), inp["cos"][...], inp["sin"][...]).astype(jnp.bfloat16)

    def finish_query(h, values):
        buf["qp"][h] = values.astype(jnp.bfloat16)
        buf["q"][h] = turn(swish_of(values), inp["cos"][...], inp["sin"][...]).astype(jnp.bfloat16)

    def finish_value(h, values):
        buf["v"][h] = values.astype(jnp.bfloat16)

    def finish_update(h, values):
        buf["up"][h] = values.astype(jnp.bfloat16)
        columns = pl.ds(pl.multiple_of(h * HEAD_DIM, HEAD_DIM), HEAD_DIM)
        buf["y1"][:, columns] = swish_of(values)

    def make_states():
        last = scalar_segment(first + rows - 1, ends)

        def head(h, carry):
            rate = rate_of(h)[:, :HEAD_DIM]
            to_end = jnp.where(segments == last, jnp.exp(-(rows - 1.0 - steps_f) * rate), 0.0)
            scaled = (buf["k"][h].astype(jnp.float32) * to_end).astype(jnp.bfloat16)
            states[t, h] = dot_tn(scaled, buf["v"][h]).astype(jnp.bfloat16)
            return carry

        lax.fori_loop(0, 8, head, 0)
        for name in ("k", "v", "kp"):
            save(name).start()

    def send_states():
        for d in range(3):
            state_copy(d, t).start()

    def sum_states():
        for d in range(3):
            state_copy(d, (t + 3 - d) % 4).wait_recv()
        before = scalar_segment(first - 1, ends)

        def head(h, carry):
            rate = rate_of(h)[:, :HEAD_DIM]
            result = jnp.zeros((HEAD_DIM, HEAD_DIM), jnp.float32)
            for j in range(3):
                reach = jnp.where(
                    (j < t) & (scalar_segment(j * rows + rows - 1, ends) == before), 1.0, 0.0
                )
                distance = jnp.maximum(t - j - 1, 0).astype(jnp.float32) * rows
                weight = reach * jnp.exp(-rate * distance)
                result = result + weight * states[j, h].astype(jnp.float32)
            buf["states"][h] = result.astype(jnp.bfloat16)
            return carry

        lax.fori_loop(0, 8, head, 0)
        save("states").start()
        for name in ("q", "qp", "up"):
            save(name).start()

    def attend(lo, hi):
        before = scalar_segment(first - 1, ends)

        def head(h, carry):
            rate = rate_of(h)
            columns = pl.ds(pl.multiple_of(h * HEAD_DIM, HEAD_DIM), HEAD_DIM)
            half = rows // 2
            for b in range(2):
                mine = slice(b * half, (b + 1) * half)
                keys = (b + 1) * half
                query = buf["q"][h, mine]
                scores = dot_nt(query, buf["k"][h, :keys])
                decay = jnp.exp(-span[mine, :keys] * rate[:, :keys])
                weights = (scores * decay).astype(jnp.bfloat16)
                into = jnp.where(
                    segments[mine] == before, jnp.exp(-(steps_f[mine] + 1.0) * rate[:, :HEAD_DIM]), 0.0
                )
                attn = dot(weights, buf["v"][h, :keys]) + into * dot(query, buf["states"][h])
                buf["o"][h, mine] = attn
                normed = attn * rms_scale(attn, head_floor)
                buf["w"][mine, columns] = (normed * buf["y1"][mine, columns]).astype(jnp.bfloat16)
            return carry

        return lambda: (lax.fori_loop(lo, hi, head, 0), None)[1]

    def mix():
        save("o").start()
        save("w").start()
        arrived(4)

        def block(i, carry):
            sides = [full[4][i // 2, i % 2, s].reshape(n1.shape[1], HEAD_DIM) for s in range(2)]
            columns = pl.ds(pl.multiple_of(i * 2 * HEAD_DIM, 2 * HEAD_DIM), 2 * HEAD_DIM)
            buf["y1"][:, columns] = inp["tokens"][:, columns].astype(jnp.float32) + dot(
                buf["w"][...], jnp.concatenate(sides, axis=1)
            )
            return carry

        lax.fori_loop(0, 4, block, 0)
        values = buf["y1"][...]
        buf["n2"][...] = (values * rms_scale(values)).astype(jnp.bfloat16)
        save("y1").start()
        save("n2").start()

    def gate_up(i):
        def go():
            if i == 0:
                arrived(6)
            shape = (n1.shape[1], full[5].shape[5])
            for b in range(2):
                mine = slice(b * rows // 2, (b + 1) * rows // 2)
                gate = dot(buf["n2"][mine], full[5][:, :, :, i].reshape(shape))
                lift = dot(buf["n2"][mine], full[6][:, :, :, i].reshape(shape))
                buf["a"][i, mine] = (gate * lift).astype(jnp.bfloat16)
                buf["g"][i, mine] = gate.astype(jnp.bfloat16)
                buf["e"][i, mine] = lift.astype(jnp.bfloat16)
            if i == 3:
                for name in ("a", "g", "e"):
                    save(name).start()

        return go

    def close():
        arrived(7)

        def block(i, carry):
            columns = pl.ds(pl.multiple_of(i * 2 * HEAD_DIM, 2 * HEAD_DIM), 2 * HEAD_DIM)
            values = buf["y1"][:, columns]
            for j in range(4):
                sides = [full[7][i // 2, i % 2, s, j] for s in range(2)]
                values = values + dot(buf["a"][j], jnp.concatenate(sides, axis=1))
            buf["result"][:, columns] = values.astype(jnp.bfloat16)
            return carry

        lax.fori_loop(0, 4, block, 0)
        save("result").start()

    lead, lag = 4, 2

    def ready(w):
        return 2 * ORDER.index(w) + 1 + 2 * lag + 1

    work = [
        (0, begin),
        (4, rates_here),
        (ready(1), project(1, finish_key)),
        (ready(2), project(2, finish_value)),
        (ready(2), make_states),
        (ready(0), send_states),
        (ready(0), project(0, finish_query)),
        (ready(3), project(3, finish_update)),
        (ready(3), sum_states),
        *[(ready(3), attend(h, h + 2)) for h in range(0, 8, 2)],
        (ready(4), mix),
        (ready(5), lambda: arrived(5)),
        *[(ready(6), gate_up(i)) for i in range(4)],
        (ready(7), close),
    ]

    def some_work(step):
        if work and work[0][0] <= step:
            work.pop(0)[1]()

    for p in range(min(lead, total)):
        start_z(p)
    some_work(0)
    for step in range(total + 2 * lag):
        if lead <= step + lead < total:
            start_z(step + lead)
        p = step
        if p < total:
            own_copy(p).wait()
            for d in range(3):
                z_copy(p, d, (t + 3 - d) % 4).wait_recv()
            near_copy(p, 0, False).start()
            core_copy(p, 0, False).start()
            some_work(step)
        p = step - lag
        if 0 <= p < total:
            near_copy(p, 0, True).wait_recv()
            near_copy(p, 1, False).start()
            core_copy(p, 1, False).start()
            some_work(step)
        p = step - 2 * lag
        if 0 <= p < total:
            near_copy(p, 1, True).wait_recv()
            core_copy(p, 2, False).start()
            some_work(step)
    while work:
        work.pop(0)[1]()
    for d in range(3):
        rate_copy(d, t).wait_send()
        state_copy(d, t).wait_send()
    for p in range(total):
        for d in range(3):
            z_copy(p, d, t).wait_send()
        for stage in range(2):
            near_copy(p, stage, False).wait_send()
        for part in range(3):
            core_copy(p, part, False).wait_send()
    for w in range(N_W):
        keep(w).wait()
    for name in FWD_OUT:
        save(name).wait()


def forward(shards, tokens, cos, sin, lengths, rates):
    rows, width = tokens.shape
    units = shards[5].shape[1]
    heads = width // HEAD_DIM
    low, wide = jnp.bfloat16, jnp.float32
    by_head = (heads, rows, HEAD_DIM)
    by_unit = (4, rows, units)
    shapes = {
        "result": ((rows, width), low),
        "qp": (by_head, low),
        "kp": (by_head, low),
        "up": (by_head, low),
        "q": (by_head, low),
        "k": (by_head, low),
        "v": (by_head, low),
        "o": (by_head, wide),
        "w": ((rows, width), low),
        "y1": ((rows, width), wide),
        "n2": ((rows, width), low),
        "a": (by_unit, low),
        "g": (by_unit, low),
        "e": (by_unit, low),
        "states": ((heads, HEAD_DIM, HEAD_DIM), low),
        "rates8": ((8, rows), wide),
    }
    blocks = [(2, 2, 2, 4, *s.shape) for s in shards]
    pieces = 2 * N_W
    dma = pltpu.SemaphoreType.DMA
    in_vmem, in_smem = (pl.BlockSpec(memory_space=m) for m in (pltpu.VMEM, pltpu.SMEM))
    outs = pl.pallas_call(
        forward_kernel,
        name="gather_and_forward",
        out_shape=[jax.ShapeDtypeStruct(b, low) for b in blocks]
        + [jax.ShapeDtypeStruct(*shapes[name]) for name in FWD_OUT],
        in_specs=[in_vmem] * (N_W + 3) + [in_smem] * 2,
        out_specs=[pl.BlockSpec(memory_space=pl.ANY)] * (N_W + len(FWD_OUT)),
        scratch_shapes=[
            *[pltpu.VMEM(b, low) for b in blocks],
            *[pltpu.VMEM(*shapes[name]) for name in FWD_OUT],
            pltpu.VMEM((rows, width), low),
            pltpu.VMEM((rows, rows), wide),
            pltpu.VMEM((4, heads, HEAD_DIM, HEAD_DIM), low),
            pltpu.VMEM((4, 8, rows), wide),
            dma((pieces,)),
            dma((pieces, 3)),
            dma((pieces, 3)),
            dma((pieces, 2)),
            dma((pieces, 2)),
            dma((pieces, 3)),
            dma((pieces, 3)),
            dma((3,)),
            dma((3,)),
            dma((3,)),
            dma((3,)),
            dma((N_W,)),
            dma((len(FWD_OUT),)),
        ],
        compiler_params=pltpu.CompilerParams(
            collective_id=0, has_side_effects=True, vmem_limit_bytes=VMEM_BYTES
        ),
    )(*shards, tokens, cos, sin, lengths, rates)
    return outs[:N_W], dict(zip(FWD_OUT, outs[N_W:]))


def scatter_kernel(count, *refs):
    ins, outs = refs[:count], refs[count : 2 * count]
    rest = refs[2 * count :]
    mine, from_core, from_near, from_far, from_z = (
        rest[i * count : (i + 1) * count] for i in range(5)
    )
    own_sem, c_send, c_recv, n_send, n_recv, z_send, z_recv = rest[5 * count :]
    y, x, c, f, t = place()
    core, along_x, along_y, along_z = peers_of(f, t)
    meet([core, along_x, along_y, *along_z])
    pieces = [(w, h) for w in range(count) for h in range(2)]
    total = len(pieces)
    all_ = slice(None)

    def rows_of(p):
        w, h = pieces[p]
        half = outs[w].shape[0] // 2
        return pl.ds(h * half, half)

    def remote(src, dst, send, recv, peer):
        return pltpu.make_async_remote_copy(
            src_ref=src, dst_ref=dst, send_sem=send, recv_sem=recv, device_id=peer, device_id_type=MESH
        )

    def own_copy(p):
        w, rows = pieces[p][0], rows_of(p)
        return pltpu.make_async_copy(
            ins[w].at[:, :, c, :, rows], mine[w].at[:, :, :, rows], own_sem.at[p]
        )

    def core_copy(p):
        w, rows = pieces[p][0], rows_of(p)
        return remote(
            ins[w].at[:, :, 1 - c, :, rows],
            from_core[w].at[:, :, :, rows],
            c_send.at[p],
            c_recv.at[p],
            core,
        )

    def near_copy(p):
        (w, h), rows = pieces[p], rows_of(p)
        src = mine[w].at[1 - y, :, :, rows] if h == 0 else mine[w].at[:, 1 - x, :, rows]
        return remote(
            src,
            from_near[w].at[:, :, rows],
            n_send.at[p, 0],
            n_recv.at[p, 0],
            along_y if h == 0 else along_x,
        )

    def far_copy(p):
        (w, h), rows = pieces[p], rows_of(p)
        src = mine[w].at[y, 1 - x, :, rows] if h == 0 else mine[w].at[1 - y, x, :, rows]
        return remote(
            src,
            from_far[w].at[:, rows],
            n_send.at[p, 1],
            n_recv.at[p, 1],
            along_x if h == 0 else along_y,
        )

    def z_copy(p, d):
        w, rows = pieces[p][0], rows_of(p)
        return remote(
            mine[w].at[y, x, (t + d + 1) % 4, rows],
            from_z[w].at[d, rows],
            z_send.at[p, d],
            z_recv.at[p, d],
            along_z[d],
        )

    def add(steps, target, other):
        def step(i, carry):
            into, term = target(i), other(i)
            into[...] = (into[...].astype(jnp.float32) + term[...].astype(jnp.float32)).astype(
                jnp.bfloat16
            )
            return carry

        lax.fori_loop(0, steps, step, 0)

    def start(p):
        core_copy(p).start()
        own_copy(p).start()

    lead, lag = 4, 2
    for p in range(min(lead, total)):
        start(p)
    for step in range(total + 3 * lag):
        if lead <= step + lead < total:
            start(step + lead)
        p = step
        if p < total:
            (w, h), rows = pieces[p], rows_of(p)
            own_copy(p).wait()
            core_copy(p).wait_recv()
            add(
                16,
                lambda i: mine[w].at[i // 8, i // 4 % 2, i % 4, rows],
                lambda i: from_core[w].at[i // 8, i // 4 % 2, i % 4, rows],
            )
            near_copy(p).start()
        p = step - lag
        if 0 <= p < total:
            (w, h), rows = pieces[p], rows_of(p)
            near_copy(p).wait_recv()
            if h == 0:
                into = lambda i: mine[w].at[y, i // 4, i % 4, rows]
            else:
                into = lambda i: mine[w].at[i // 4, x, i % 4, rows]
            add(8, into, lambda i: from_near[w].at[i // 4, i % 4, rows])
            far_copy(p).start()
        p = step - 2 * lag
        if 0 <= p < total:
            (w, h), rows = pieces[p], rows_of(p)
            far_copy(p).wait_recv()
            add(4, lambda i: mine[w].at[y, x, i, rows], lambda i: from_far[w].at[i, rows])
            for d in range(3):
                z_copy(p, d).start()
        p = step - 3 * lag
        if 0 <= p < total:
            (w, h), rows = pieces[p], rows_of(p)
            for d in range(3):
                z_copy(p, d).wait_recv()
            result = mine[w][y, x, t, rows].astype(jnp.float32)
            for d in range(3):
                result = result + from_z[w][d, rows].astype(jnp.float32)
            outs[w][rows] = result
    for p in range(total):
        core_copy(p).wait_send()
        near_copy(p).wait_send()
        far_copy(p).wait_send()
        for d in range(3):
            z_copy(p, d).wait_send()


def scatter_grads(grads):
    count = len(grads)
    pieces = 2 * count
    dma = pltpu.SemaphoreType.DMA
    shards = [g.shape[4:] for g in grads]

    def buffers(*lead):
        return [pltpu.VMEM((*lead, *s), jnp.bfloat16) for s in shards]

    return pl.pallas_call(
        functools.partial(scatter_kernel, count),
        name="scatter_grads",
        out_shape=[jax.ShapeDtypeStruct(s, jnp.float32) for s in shards],
        in_specs=[pl.BlockSpec(memory_space=pl.ANY)] * count,
        out_specs=[pl.BlockSpec(memory_space=pltpu.VMEM)] * count,
        scratch_shapes=[
            *buffers(2, 2, 4),
            *buffers(2, 2, 4),
            *buffers(2, 4),
            *buffers(4),
            *buffers(3),
            dma((pieces,)),
            dma((pieces,)),
            dma((pieces,)),
            dma((pieces, 2)),
            dma((pieces, 2)),
            dma((pieces, 3)),
            dma((pieces, 3)),
        ],
        compiler_params=pltpu.CompilerParams(
            collective_id=1, has_side_effects=True, vmem_limit_bytes=VMEM_BYTES
        ),
    )(*grads)


def whole_in(blocks):
    depth, width = blocks.shape[4:]
    return blocks.reshape(8, 4, depth, width).transpose(0, 2, 1, 3).reshape(8 * depth, 4 * width)


def whole_out(blocks):
    depth, width = blocks.shape[4:]
    return blocks.reshape(8, 4, depth, width).transpose(1, 2, 0, 3).reshape(4 * depth, 8 * width)


def blocks_in(grad):
    depth, width = grad.shape[0] // 8, grad.shape[1] // 4
    part = grad.astype(jnp.bfloat16).reshape(8, depth, 4, width).transpose(0, 2, 1, 3)
    return part.reshape(2, 2, 2, 4, depth, width)


def blocks_out(grad):
    depth, width = grad.shape[0] // 4, grad.shape[1] // 8
    part = grad.astype(jnp.bfloat16).reshape(4, depth, 8, width).transpose(2, 0, 1, 3)
    return part.reshape(2, 2, 2, 4, depth, width)


def body(
    by_kernels,
    tokens,
    lengths,
    rates,
    w_query,
    w_key,
    w_value,
    w_update,
    w_output,
    w_gate,
    w_up,
    w_down,
    out_grad,
):
    tp_count = lax.axis_size("tp")
    tp_index = lax.axis_index("tp")
    rows, width = tokens.shape
    head_width = HEAD_DIM
    ends = jnp.cumsum(lengths[0], dtype=jnp.int32)
    first = tp_index * rows
    places = first + jnp.arange(rows, dtype=jnp.int32)
    segments = segment_of(places, ends)
    starts = ends - lengths[0]
    slots = jnp.arange(SLOTS, dtype=jnp.int32)
    positions = (
        places - jnp.sum(jnp.where(segments[:, None] == slots, starts, 0), axis=1)
    ).astype(jnp.float32)
    live = (segments < SLOTS - 1).astype(jnp.float32)
    frequency = 10000.0 ** (-2.0 * jnp.arange(head_width // 2, dtype=jnp.float32) / head_width)
    turned = positions[:, None] * frequency[None, :]
    cos_table, sin_table = jnp.cos(turned)[:, None, :], jnp.sin(turned)[:, None, :]

    tokens_f = tokens.astype(jnp.float32)
    scale1 = rms_scale(tokens_f)
    normed1 = (tokens_f * scale1).astype(jnp.bfloat16)
    shards = (w_query, w_key, w_value, w_update, w_output, w_gate, w_up, w_down)
    inner = (True, True, True, True, False, True, True, False)
    if by_kernels:
        cos2 = jnp.concatenate([cos_table, cos_table], axis=2).reshape(rows, head_width)
        sin2 = jnp.concatenate([-sin_table, sin_table], axis=2).reshape(rows, head_width)
        kept, saved = forward(shards, tokens, cos2, sin2, lengths, rates)
        full = [whole_in(w) if rows_first else whole_out(w) for w, rows_first in zip(kept, inner)]
        all_rates = saved["rates8"][:, 0]
    else:
        full = [
            gather_full(w, "fsdp", "tp") if rows_first else gather_full(w, "tp", "fsdp")
            for w, rows_first in zip(shards, inner)
        ]
        all_rates = lax.all_gather(rates, "tp", axis=0, tiled=True)
    heads = all_rates.shape[0]
    (
        query_full,
        key_full,
        value_full,
        update_full,
        output_full,
        gate_full,
        up_full,
        down_full,
    ) = full
    gaps = places[:, None] - places[None, :]
    allowed = (segments[:, None] == segments[None, :]) & (gaps >= 0)
    spans = jnp.maximum(gaps, 0).astype(jnp.float32)
    decay = jnp.where(
        allowed[None], jnp.exp(-all_rates[:, None, None] * spans[None]), 0.0
    )
    blocks = jnp.arange(tp_count, dtype=jnp.int32)
    seg_before = segment_of(first - 1, ends)
    seg_after = segment_of(first + rows, ends)
    seg_last = segment_of(blocks * rows + rows - 1, ends)
    seg_first = segment_of(blocks * rows, ends)
    offsets = jnp.arange(rows, dtype=jnp.float32)

    def row_decay(distance, mask):
        return jnp.where(mask[:, None], jnp.exp(-distance[:, None] * all_rates[None]), 0.0)[
            :, :, None
        ]

    to_end = row_decay(rows - 1 - offsets, segments == segments[rows - 1])
    from_start = row_decay(offsets, segments == segments[0])
    into = row_decay(offsets + 1.0, segments == seg_before)
    out_of = row_decay(rows - offsets, segments == seg_after)

    def block_weights(mask, distance):
        distance = jnp.maximum(distance, 0).astype(jnp.float32)
        return jnp.where(mask[:, None], jnp.exp(-distance[:, None] * all_rates[None]), 0.0)

    before_weights = block_weights(
        (blocks < tp_index) & (seg_last == seg_before), (tp_index - blocks - 1) * rows
    )
    after_weights = block_weights(
        (blocks > tp_index) & (seg_first == seg_after), (blocks - tp_index - 1) * rows
    )

    shape_heads = (rows, heads, head_width)
    if by_kernels:
        by_row = lambda name: saved[name].transpose(1, 0, 2)
        query_pre, key_pre, update_pre = (
            by_row(n).reshape(rows, width).astype(jnp.float32) for n in ("qp", "kp", "up")
        )
        query, key_rows, value_rows = (by_row(n) for n in ("q", "k", "v"))
        update = swish(update_pre)
        state_in = saved["states"]
        attn = by_row("o")
        weights = (heads_dot("thc,shc->hts", query, key_rows) * decay).astype(jnp.bfloat16)
        scale_attn = rms_scale(attn, head_floor)
        normed_attn = (attn * scale_attn).reshape(rows, width)
        mixed, middle, normed2, result = (saved[n] for n in ("w", "y1", "n2", "result"))
        scale2 = rms_scale(middle)
        hidden, gate_rows, up_rows = (by_row(n).reshape(rows, -1) for n in ("a", "g", "e"))
    else:
        query_pre = mm(normed1, query_full)
        key_pre = mm(normed1, key_full)
        value_rows = mm(normed1, value_full).astype(jnp.bfloat16).reshape(shape_heads)
        update_pre = mm(normed1, update_full)
        query = rotate(swish(query_pre).reshape(shape_heads), cos_table, sin_table).astype(jnp.bfloat16)
        key_rows = rotate(swish(key_pre).reshape(shape_heads), cos_table, sin_table).astype(
            jnp.bfloat16
        )
        update = swish(update_pre)
        key_state = heads_dot(
            "shc,shd->hcd", (key_rows * to_end).astype(jnp.bfloat16), value_rows
        ).astype(jnp.bfloat16)
        key_states = lax.all_gather(key_state, "tp", axis=0, tiled=False)
        state_in = jnp.sum(
            key_states.astype(jnp.float32) * before_weights[:, :, None, None], axis=0
        ).astype(jnp.bfloat16)
        weights = (heads_dot("thc,shc->hts", query, key_rows) * decay).astype(jnp.bfloat16)
        attn = heads_dot("hts,shd->thd", weights, value_rows) + into * heads_dot(
            "thc,hcd->thd", query, state_in
        )
        scale_attn = rms_scale(attn, head_floor)
        normed_attn = (attn * scale_attn).reshape(rows, width)
        mixed = (normed_attn * update).astype(jnp.bfloat16)
        middle = tokens_f + mm(mixed, output_full)
        scale2 = rms_scale(middle)
        normed2 = (middle * scale2).astype(jnp.bfloat16)
        gate_rows = mm(normed2, gate_full)
        up_rows = mm(normed2, up_full)
        hidden = (gate_rows * up_rows).astype(jnp.bfloat16)
        result = (middle + mm(hidden, down_full)).astype(jnp.bfloat16)

    cotangent = out_grad.astype(jnp.float32) * live[:, None]
    cot_rows = cotangent.astype(jnp.bfloat16)
    grad_down = mm_inner(hidden, cot_rows)
    d_hidden = mm_trans(cot_rows, down_full)
    d_gate = (d_hidden * up_rows).astype(jnp.bfloat16)
    d_up = (d_hidden * gate_rows).astype(jnp.bfloat16)
    grad_gate = mm_inner(normed2, d_gate)
    grad_up = mm_inner(normed2, d_up)
    d_normed2 = mm_trans(d_gate, gate_full) + mm_trans(d_up, up_full)
    d_middle = cotangent + norm_back(middle, scale2, d_normed2)
    mid_rows = d_middle.astype(jnp.bfloat16)
    d_mixed = mm_trans(mid_rows, output_full)
    grad_output = mm_inner(mixed, mid_rows)
    d_update_pre = (d_mixed * normed_attn * swish_slope(update_pre)).astype(jnp.bfloat16)
    d_attn = norm_back(attn, scale_attn, (d_mixed * update).reshape(shape_heads)).astype(
        jnp.bfloat16
    )
    query_state = heads_dot(
        "thc,thd->hcd", (query * from_start).astype(jnp.bfloat16), d_attn
    ).astype(jnp.bfloat16)
    query_states = lax.all_gather(query_state, "tp", axis=0, tiled=False)
    state_back = jnp.sum(
        query_states.astype(jnp.float32) * after_weights[:, :, None, None], axis=0
    ).astype(jnp.bfloat16)
    d_raw = (heads_dot("thd,shd->hts", d_attn, value_rows) * decay).astype(jnp.bfloat16)
    d_value = heads_dot("hts,thd->shd", weights, d_attn) + out_of * heads_dot(
        "shc,hcd->shd", key_rows, state_back
    )
    d_query = heads_dot("hts,shc->thc", d_raw, key_rows) + into * heads_dot(
        "thd,hcd->thc", d_attn, state_in
    )
    d_key = heads_dot("hts,thc->shc", d_raw, query) + out_of * heads_dot(
        "shd,hcd->shc", value_rows, state_back
    )
    d_query_pre = (
        swish_slope(query_pre) * rotate_back(d_query, cos_table, sin_table).reshape(rows, width)
    ).astype(jnp.bfloat16)
    d_key_pre = (
        swish_slope(key_pre) * rotate_back(d_key, cos_table, sin_table).reshape(rows, width)
    ).astype(jnp.bfloat16)
    d_value_pre = d_value.reshape(rows, width).astype(jnp.bfloat16)
    grads = [mm_inner(normed1, d) for d in (d_query_pre, d_key_pre, d_value_pre, d_update_pre)]
    d_normed1 = (
        mm_trans(d_query_pre, query_full)
        + mm_trans(d_key_pre, key_full)
        + mm_trans(d_value_pre, value_full)
        + mm_trans(d_update_pre, update_full)
    )
    d_tokens = d_middle + norm_back(tokens_f, scale1, d_normed1)
    grads = (*grads, grad_output, grad_gate, grad_up, grad_down)
    if by_kernels:
        grads = scatter_grads(
            [blocks_in(g) if rows_first else blocks_out(g) for g, rows_first in zip(grads, inner)]
        )
    else:
        grads = [
            scatter_grad(g, "fsdp", "tp") if rows_first else scatter_grad(g, "tp", "fsdp")
            for g, rows_first in zip(grads, inner)
        ]
    return (result, d_tokens, *grads)


def solution(mesh):
    rows = P(AXES, None)
    inner, outer = P("fsdp", "tp"), P("tp", "fsdp")
    by_kernels = mesh.shape["fsdp"] == 8 and mesh.shape["tp"] == 4
    return jax.shard_map(
        functools.partial(body, by_kernels),
        mesh=mesh,
        in_specs=(
            rows,
            P("fsdp", None),
            P("tp"),
            inner,
            inner,
            inner,
            inner,
            outer,
            inner,
            inner,
            outer,
            rows,
        ),
        out_specs=(rows, rows, inner, inner, inner, inner, outer, inner, inner, outer),
        check_vma=False,
    )
```

```python
import jax
import jax.numpy as jnp
from jax import lax
from jax.experimental import pallas as pl
from jax.experimental.pallas import tpu as pltpu
from jax.sharding import PartitionSpec as P

HEAD_DIM = 128
SLOTS = 4

epsilon = 1e-06
head_floor = 1.0
AXES = ("fsdp", "tp")


def swish(values):
    return values * jax.nn.sigmoid(values)


def swish_slope(values):
    sigma = jax.nn.sigmoid(values)
    return sigma * (1.0 + values * (1.0 - sigma))


def rms_scale(values, offset=epsilon):
    return lax.rsqrt(jnp.mean(values * values, axis=-1, keepdims=True) + offset)


def norm_back(values, scale, grads):
    normed = values * scale
    return scale * (grads - normed * jnp.mean(grads * normed, axis=-1, keepdims=True))


def segment_of(places, ends):
    return jnp.sum((places[..., None] >= ends).astype(jnp.int32), axis=-1, dtype=jnp.int32)


def rotate(values, cos_table, sin_table):
    half = values.shape[-1] // 2
    front, back = values[..., :half], values[..., half:]
    return jnp.concatenate(
        [front * cos_table - back * sin_table, front * sin_table + back * cos_table], axis=-1
    )


def rotate_back(values, cos_table, sin_table):
    return rotate(values, cos_table, -sin_table)


def mm(left, right):
    return jnp.dot(left, right, preferred_element_type=jnp.float32)


def mm_trans(left, right):
    return lax.dot_general(
        left, right, (((1,), (1,)), ((), ())), preferred_element_type=jnp.float32
    )


def mm_inner(left, right):
    return lax.dot_general(
        left, right, (((0,), (0,)), ((), ())), preferred_element_type=jnp.float32
    )


def heads_dot(spec, left, right):
    return jnp.einsum(spec, left, right, preferred_element_type=jnp.float32)


def gather_full(shard, row_axis, column_axis):
    part = lax.all_gather(shard, "tp", axis=0 if row_axis == "tp" else 1, tiled=True)
    return lax.all_gather(part, "fsdp", axis=0 if row_axis == "fsdp" else 1, tiled=True)


def scatter_grad(grad, row_axis, column_axis):
    part = grad.astype(jnp.bfloat16)
    part = lax.psum_scatter(
        part, "fsdp", scatter_dimension=0 if row_axis == "fsdp" else 1, tiled=True
    )
    part = lax.psum_scatter(part, "tp", scatter_dimension=0 if row_axis == "tp" else 1, tiled=True)
    return part.astype(jnp.float32)


MESH = pl.DeviceIdType.MESH
VMEM_BYTES = 66_000_000


def place():
    f, t = lax.axis_index("fsdp"), lax.axis_index("tp")
    return f // 4, (f // 2) % 2, f % 2, f, t


def meet(peers):
    barrier = pltpu.get_barrier_semaphore()
    for peer in peers:
        pl.semaphore_signal(barrier, inc=1, device_id=peer, device_id_type=MESH)
    pl.semaphore_wait(barrier, len(peers))


def peers_of(f, t):
    core = (f // 2 * 2 + (1 - f % 2), t)
    along_x = (f // 4 * 4 + (f + 2) % 4, t)
    along_y = ((f + 4) % 8, t)
    along_z = [(f, (t + d) % 4) for d in (1, 2, 3)]
    return core, along_x, along_y, along_z


FAR = 1e7


def swish_of(values):
    return values * jax.nn.sigmoid(values)


def segment_at(where, ends):
    return sum((where >= end).astype(jnp.int32) for end in ends)


def row_tables(lengths_ref, t, rows):
    ends, total = [], jnp.int32(0)
    for j in range(SLOTS):
        total = total + lengths_ref[0, j]
        ends.append(total)
    first = t * rows
    offsets = lax.broadcasted_iota(jnp.int32, (rows, HEAD_DIM), 0)
    return ends, first, offsets, segment_at(first + offsets, ends)


def scalar_segment(where, ends):
    return sum(jnp.where(where >= end, 1, 0) for end in ends)


def fill_span(span_ref, ends, first):
    rows = span_ref.shape[0]
    band = 32

    def step(i, carry):
        row = first + i * band + lax.broadcasted_iota(jnp.int32, (band, rows), 0)
        column = first + lax.broadcasted_iota(jnp.int32, (band, rows), 1)
        allowed = (segment_at(row, ends) == segment_at(column, ends)) & (row >= column)
        span_ref[pl.ds(pl.multiple_of(i * band, band), band), :] = jnp.where(
            allowed, (row - column).astype(jnp.float32), FAR
        )
        return carry

    lax.fori_loop(0, rows // band, step, 0)


def turn(values, cos, sin):
    return values * cos + pltpu.roll(values, HEAD_DIM // 2, 1) * sin


def dot(left, right):
    return jnp.dot(left, right, preferred_element_type=jnp.float32)


def dot_nt(left, right):
    return lax.dot_general(left, right, (((1,), (1,)), ((), ())), preferred_element_type=jnp.float32)


def dot_tn(left, right):
    return lax.dot_general(left, right, (((0,), (0,)), ((), ())), preferred_element_type=jnp.float32)


ORDER = (1, 2, 0, 3, 4, 5, 6, 7)
N_W = 8
FWD_IN = ("tokens", "cos", "sin", "lengths", "rates")
FWD_OUT = (
    "result",
    "qp",
    "kp",
    "up",
    "q",
    "k",
    "v",
    "o",
    "w_turned",
    "y1",
    "n1_turned",
    "n2_turned",
    "g",
    "e",
    "states",
    "rates8",
)


def forward_kernel(*refs):
    shards, refs = refs[:N_W], refs[N_W:]
    inp = dict(zip(FWD_IN, refs))
    refs = refs[len(FWD_IN) :]
    kept, refs = refs[:N_W], refs[N_W:]
    a_out, refs = refs[0], refs[1:]
    out = dict(zip(FWD_OUT, refs))
    refs = refs[len(FWD_OUT) :]
    full, refs = refs[:N_W], refs[N_W:]
    buf = dict(zip(FWD_OUT, refs))
    refs = refs[len(FWD_OUT) :]
    n1, n2, mixed, hidden, hidden_turned, span, states, rate_tiles = refs[:8]
    own_sem, z_send, z_recv, n_send, n_recv, c_send, c_recv = refs[8:15]
    s_send, s_recv, r_send, r_recv, keep_sem, out_sem, turn_sem = refs[15:]
    rows = inp["tokens"].shape[0]
    y, x, c, f, t = place()
    core, along_x, along_y, along_z = peers_of(f, t)
    rate_tiles[t] = jnp.concatenate(
        [jnp.full((1, rows), inp["rates"][i % 2], jnp.float32) for i in range(8)], axis=0
    )
    meet([core, along_x, along_y, *along_z])
    pieces = [(w, h) for w in ORDER for h in range(2)]
    total = len(pieces)
    all_ = slice(None)

    def rows_of(piece):
        w, h = piece
        half = shards[w].shape[0] // 2
        return pl.ds(h * half, half)

    def slot(piece, *index):
        return full[piece[0]].at[(*index, rows_of(piece))]

    def remote(src, dst, send, recv, peer):
        return pltpu.make_async_remote_copy(
            src_ref=src, dst_ref=dst, send_sem=send, recv_sem=recv, device_id=peer, device_id_type=MESH
        )

    def own_copy(p):
        piece = pieces[p]
        return pltpu.make_async_copy(
            shards[piece[0]].at[rows_of(piece)], slot(piece, y, x, c, t), own_sem.at[p]
        )

    def z_copy(p, d, source):
        piece = pieces[p]
        return remote(
            shards[piece[0]].at[rows_of(piece)],
            slot(piece, y, x, c, source),
            z_send.at[p, d],
            z_recv.at[p, d],
            along_z[d],
        )

    def near_copy(p, stage, arriving):
        piece = pieces[p]
        over_x = (piece[1] == 0) == (stage == 0)
        if stage == 0:
            index = (y, x, c)
            if arriving:
                index = (y, 1 - x, c) if over_x else (1 - y, x, c)
        else:
            if over_x:
                index = (all_, (1 - x) if arriving else x, c)
            else:
                index = ((1 - y) if arriving else y, all_, c)
        ref = slot(piece, *index, all_)
        return remote(
            ref, ref, n_send.at[p, stage], n_recv.at[p, stage], along_x if over_x else along_y
        )

    def core_copy(p, part, arriving):
        piece = pieces[p]
        side = (1 - c) if arriving else c
        first_x = piece[1] == 0
        index = (
            (y, x, side),
            (y, 1 - x, side) if first_x else (1 - y, x, side),
            (1 - y, all_, side) if first_x else (all_, 1 - x, side),
        )[part]
        ref = slot(piece, *index, all_)
        return remote(ref, ref, c_send.at[p, part], c_recv.at[p, part], core)

    def start_z(p):
        own_copy(p).start()
        for d in range(3):
            z_copy(p, d, t).start()

    def arrived(w):
        for h in range(2):
            for part in range(3):
                core_copy(pieces.index((w, h)), part, True).wait_recv()
        keep(w).start()

    def keep(w):
        return pltpu.make_async_copy(full[w], kept[w], keep_sem.at[w])

    def save(name):
        return pltpu.make_async_copy(buf[name], out[name], out_sem.at[FWD_OUT.index(name)])

    def rate_copy(d, source):
        ref = rate_tiles.at[source]
        return remote(ref, ref, r_send.at[d], r_recv.at[d], along_z[d])

    def state_copy(d, source):
        ref = states.at[source]
        return remote(ref, ref, s_send.at[d], s_recv.at[d], along_z[d])

    ends, first, offsets, segments = row_tables(inp["lengths"], t, rows)
    steps_f = offsets.astype(jnp.float32)

    def head_columns(i, j):
        return pl.ds(pl.multiple_of(i * 2 * HEAD_DIM + j * HEAD_DIM, HEAD_DIM), HEAD_DIM)

    def rate_of(h):
        return buf["rates8"][pl.ds(h, 1), :]

    def turn_rows(source, target):
        for j in range(8):
            part = source[:, j * HEAD_DIM : (j + 1) * HEAD_DIM]
            target[j % 2, j // 2 * HEAD_DIM : (j // 2 + 1) * HEAD_DIM] = part.T

    def begin():
        for d in range(3):
            rate_copy(d, t).start()
        values = inp["tokens"][...].astype(jnp.float32)
        n1[...] = (values * rms_scale(values)).astype(jnp.bfloat16)
        turn_rows(n1, buf["n1_turned"])
        save("n1_turned").start()
        fill_span(span, ends, first)

    def rates_here():
        for d in range(3):
            rate_copy(d, (t + 3 - d) % 4).wait_recv()
        for j in range(4):
            buf["rates8"][2 * j : 2 * j + 2] = rate_tiles[j, 0:2]
        save("rates8").start()

    def project(w, finish):
        def run():
            arrived(w)

            def block(i, carry):
                columns = full[w][:, :, :, i].reshape(n1.shape[1], full[w].shape[5])
                values = dot(n1[...], columns)
                for j in range(2):
                    finish(i, j, values[:, j * HEAD_DIM : (j + 1) * HEAD_DIM])
                return carry

            lax.fori_loop(0, 4, block, 0)

        return run

    def finish_key(i, j, values):
        lanes = slice(j * HEAD_DIM, (j + 1) * HEAD_DIM)
        buf["kp"][i, :, lanes] = values.astype(jnp.bfloat16)
        buf["k"][i, :, lanes] = turn(swish_of(values), inp["cos"][...], inp["sin"][...]).astype(jnp.bfloat16)

    def finish_query(i, j, values):
        lanes = slice(j * HEAD_DIM, (j + 1) * HEAD_DIM)
        buf["qp"][i, :, lanes] = values.astype(jnp.bfloat16)
        buf["q"][i, :, lanes] = turn(swish_of(values), inp["cos"][...], inp["sin"][...]).astype(jnp.bfloat16)

    def finish_value(i, j, values):
        lanes = slice(j * HEAD_DIM, (j + 1) * HEAD_DIM)
        buf["v"][i, :, lanes] = values.astype(jnp.bfloat16)

    def finish_update(i, j, values):
        lanes = slice(j * HEAD_DIM, (j + 1) * HEAD_DIM)
        buf["up"][i, :, lanes] = values.astype(jnp.bfloat16)
        buf["y1"][:, head_columns(i, j)] = swish_of(values)

    def make_states():
        last = scalar_segment(first + rows - 1, ends)

        def pair(i, carry):
            for j in range(2):
                h, lanes = 2 * i + j, slice(j * HEAD_DIM, (j + 1) * HEAD_DIM)
                rate = rate_of(h)[:, :HEAD_DIM]
                to_end = jnp.where(segments == last, jnp.exp(-(rows - 1.0 - steps_f) * rate), 0.0)
                scaled = (buf["k"][i, :, lanes].astype(jnp.float32) * to_end).astype(jnp.bfloat16)
                states[t, h] = dot_tn(scaled, buf["v"][i, :, lanes]).astype(jnp.bfloat16)
            return carry

        lax.fori_loop(0, 4, pair, 0)
        for name in ("k", "v", "kp"):
            save(name).start()

    def send_states():
        for d in range(3):
            state_copy(d, t).start()

    def sum_states():
        for d in range(3):
            state_copy(d, (t + 3 - d) % 4).wait_recv()
        before = scalar_segment(first - 1, ends)

        def head(h, carry):
            rate = rate_of(h)[:, :HEAD_DIM]
            result = jnp.zeros((HEAD_DIM, HEAD_DIM), jnp.float32)
            for j in range(3):
                reach = jnp.where(
                    (j < t) & (scalar_segment(j * rows + rows - 1, ends) == before), 1.0, 0.0
                )
                distance = jnp.maximum(t - j - 1, 0).astype(jnp.float32) * rows
                weight = reach * jnp.exp(-rate * distance)
                result = result + weight * states[j, h].astype(jnp.float32)
            buf["states"][h] = result.astype(jnp.bfloat16)
            return carry

        lax.fori_loop(0, 8, head, 0)
        save("states").start()
        for name in ("q", "qp", "up"):
            save(name).start()

    def attend(i):
        before = scalar_segment(first - 1, ends)
        half = rows // 2

        def go():
            for j in range(2):
                h, lanes = 2 * i + j, slice(j * HEAD_DIM, (j + 1) * HEAD_DIM)
                rate = rate_of(h)
                for b in range(2):
                    mine = slice(b * half, (b + 1) * half)
                    keys = (b + 1) * half
                    query = buf["q"][i, mine, lanes]
                    scores = dot_nt(query, buf["k"][i, :keys, lanes])
                    decay = jnp.exp(-span[mine, :keys] * rate[:, :keys])
                    weights = (scores * decay).astype(jnp.bfloat16)
                    into = jnp.where(
                        segments[mine] == before,
                        jnp.exp(-(steps_f[mine] + 1.0) * rate[:, :HEAD_DIM]),
                        0.0,
                    )
                    attn = dot(weights, buf["v"][i, :keys, lanes]) + into * dot(
                        query, buf["states"][h]
                    )
                    columns = head_columns(i, j)
                    buf["o"][mine, columns] = attn
                    normed = attn * rms_scale(attn, head_floor)
                    mixed[mine, columns] = (normed * buf["y1"][mine, columns]).astype(jnp.bfloat16)

        return go

    def attend_pairs(lo, hi):
        def step(i, carry):
            attend(i)()
            return carry

        return lambda: (lax.fori_loop(lo, hi, step, 0), None)[1]

    def mix():
        save("o").start()
        for i in range(4):
            columns = slice(i * 2 * HEAD_DIM, (i + 1) * 2 * HEAD_DIM)
            buf["w_turned"][i] = mixed[:, columns].T
        save("w_turned").start()
        arrived(4)

        def block(i, carry):
            sides = [full[4][i // 2, i % 2, s].reshape(n1.shape[1], HEAD_DIM) for s in range(2)]
            columns = pl.ds(pl.multiple_of(i * 2 * HEAD_DIM, 2 * HEAD_DIM), 2 * HEAD_DIM)
            buf["y1"][:, columns] = inp["tokens"][:, columns].astype(jnp.float32) + dot(
                mixed[...], jnp.concatenate(sides, axis=1)
            )
            return carry

        lax.fori_loop(0, 4, block, 0)
        values = buf["y1"][...]
        n2[...] = (values * rms_scale(values)).astype(jnp.bfloat16)
        turn_rows(n2, buf["n2_turned"])
        save("y1").start()
        save("n2_turned").start()

    def turned_out(i):
        return pltpu.make_async_copy(hidden_turned.at[i % 2], a_out.at[i], turn_sem.at[i])

    def gate_up(i):
        def go():
            if i == 0:
                arrived(6)
            shape = (n1.shape[1], full[5].shape[5])
            for b in range(2):
                mine = slice(b * rows // 2, (b + 1) * rows // 2)
                gate = dot(n2[mine], full[5][:, :, :, i].reshape(shape))
                lift = dot(n2[mine], full[6][:, :, :, i].reshape(shape))
                hidden[i, mine] = (gate * lift).astype(jnp.bfloat16)
                buf["g"][i, mine] = gate.astype(jnp.bfloat16)
                buf["e"][i, mine] = lift.astype(jnp.bfloat16)
            if i >= 2:
                turned_out(i - 2).wait()
            hidden_turned[i % 2] = hidden[i].T
            turned_out(i).start()
            if i == 3:
                for name in ("g", "e"):
                    save(name).start()

        return go

    def close():
        arrived(7)

        def block(i, carry):
            columns = pl.ds(pl.multiple_of(i * 2 * HEAD_DIM, 2 * HEAD_DIM), 2 * HEAD_DIM)
            values = buf["y1"][:, columns]
            for j in range(4):
                sides = [full[7][i // 2, i % 2, s, j] for s in range(2)]
                values = values + dot(hidden[j], jnp.concatenate(sides, axis=1))
            buf["result"][:, columns] = values.astype(jnp.bfloat16)
            return carry

        lax.fori_loop(0, 4, block, 0)
        save("result").start()

    lead, lag = 4, 2

    def ready(w):
        return 2 * ORDER.index(w) + 1 + 2 * lag + 1

    work = [
        (0, begin),
        (4, rates_here),
        (ready(1), project(1, finish_key)),
        (ready(2), project(2, finish_value)),
        (ready(2), make_states),
        (ready(0), send_states),
        (ready(0), project(0, finish_query)),
        (ready(3), project(3, finish_update)),
        (ready(3), sum_states),
        *[(ready(3), attend_pairs(i, i + 1)) for i in range(4)],
        (ready(4), mix),
        (ready(5), lambda: arrived(5)),
        *[(ready(6), gate_up(i)) for i in range(4)],
        (ready(7), close),
    ]

    def some_work(step):
        if work and work[0][0] <= step:
            work.pop(0)[1]()

    for p in range(min(lead, total)):
        start_z(p)
    some_work(0)
    for step in range(total + 2 * lag):
        if lead <= step + lead < total:
            start_z(step + lead)
        p = step
        if p < total:
            own_copy(p).wait()
            for d in range(3):
                z_copy(p, d, (t + 3 - d) % 4).wait_recv()
            near_copy(p, 0, False).start()
            core_copy(p, 0, False).start()
            some_work(step)
        p = step - lag
        if 0 <= p < total:
            near_copy(p, 0, True).wait_recv()
            near_copy(p, 1, False).start()
            core_copy(p, 1, False).start()
            some_work(step)
        p = step - 2 * lag
        if 0 <= p < total:
            near_copy(p, 1, True).wait_recv()
            core_copy(p, 2, False).start()
            some_work(step)
    while work:
        work.pop(0)[1]()
    for d in range(3):
        rate_copy(d, t).wait_send()
        state_copy(d, t).wait_send()
    for p in range(total):
        for d in range(3):
            z_copy(p, d, t).wait_send()
        for stage in range(2):
            near_copy(p, stage, False).wait_send()
        for part in range(3):
            core_copy(p, part, False).wait_send()
    for w in range(N_W):
        keep(w).wait()
    for name in FWD_OUT:
        save(name).wait()
    for i in range(2, 4):
        turned_out(i).wait()


def forward(shards, tokens, cos, sin, lengths, rates):
    rows, width = tokens.shape
    units = shards[5].shape[1]
    heads = width // HEAD_DIM
    low, wide = jnp.bfloat16, jnp.float32
    by_pair = (4, rows, heads // 4 * HEAD_DIM)
    turned = (2, width // 2, rows)
    by_unit = (4, rows, units)
    shapes = {
        "result": ((rows, width), low),
        "qp": (by_pair, low),
        "kp": (by_pair, low),
        "up": (by_pair, low),
        "q": (by_pair, low),
        "k": (by_pair, low),
        "v": (by_pair, low),
        "o": ((rows, width), wide),
        "w_turned": ((4, width // 4, rows), low),
        "y1": ((rows, width), wide),
        "n1_turned": (turned, low),
        "n2_turned": (turned, low),
        "g": (by_unit, low),
        "e": (by_unit, low),
        "states": ((heads, HEAD_DIM, HEAD_DIM), low),
        "rates8": ((8, rows), wide),
    }
    blocks = [(2, 2, 2, 4, *s.shape) for s in shards]
    pieces = 2 * N_W
    dma = pltpu.SemaphoreType.DMA
    in_vmem, in_smem = (pl.BlockSpec(memory_space=m) for m in (pltpu.VMEM, pltpu.SMEM))
    outs = pl.pallas_call(
        forward_kernel,
        name="gather_and_forward",
        out_shape=[jax.ShapeDtypeStruct(b, low) for b in blocks]
        + [jax.ShapeDtypeStruct((4, units, rows), low)]
        + [jax.ShapeDtypeStruct(*shapes[name]) for name in FWD_OUT],
        in_specs=[in_vmem] * (N_W + 3) + [in_smem] * 2,
        out_specs=[pl.BlockSpec(memory_space=pl.ANY)] * (N_W + 1 + len(FWD_OUT)),
        scratch_shapes=[
            *[pltpu.VMEM(b, low) for b in blocks],
            *[pltpu.VMEM(*shapes[name]) for name in FWD_OUT],
            pltpu.VMEM((rows, width), low),
            pltpu.VMEM((rows, width), low),
            pltpu.VMEM((rows, width), low),
            pltpu.VMEM(by_unit, low),
            pltpu.VMEM((2, units, rows), low),
            pltpu.VMEM((rows, rows), wide),
            pltpu.VMEM((4, heads, HEAD_DIM, HEAD_DIM), low),
            pltpu.VMEM((4, 8, rows), wide),
            dma((pieces,)),
            dma((pieces, 3)),
            dma((pieces, 3)),
            dma((pieces, 2)),
            dma((pieces, 2)),
            dma((pieces, 3)),
            dma((pieces, 3)),
            dma((3,)),
            dma((3,)),
            dma((3,)),
            dma((3,)),
            dma((N_W,)),
            dma((len(FWD_OUT),)),
            dma((4,)),
        ],
        compiler_params=pltpu.CompilerParams(
            collective_id=0, has_side_effects=True, vmem_limit_bytes=VMEM_BYTES
        ),
    )(*shards, tokens, cos, sin, lengths, rates)
    return outs[:N_W], outs[N_W], dict(zip(FWD_OUT, outs[N_W + 1 :]))


BWD_ANY = ("q", "k", "v", "up", "qp", "kp", "o", "w_turned", "y1", "n1_turned", "n2_turned", "g", "e")
BWD_VMEM = ("states", "rates8", "cos", "sin")
BAND = 32
LINK = 42_000.0


def slope_of(values):
    sigma = jax.nn.sigmoid(values)
    return sigma * (1.0 + values * (1.0 - sigma))


def turn_back(values, cos, sin):
    return values * cos - pltpu.roll(values, HEAD_DIM // 2, 1) * sin


def backward_kernel(*refs):
    kept, refs = refs[:N_W], refs[N_W:]
    a_in, refs = refs[0], refs[1:]
    inp = dict(zip(BWD_ANY + BWD_VMEM, refs))
    refs = refs[len(BWD_ANY + BWD_VMEM) :]
    tokens, out_grad, lengths = refs[:3]
    grads, d_tokens = refs[3 : 3 + N_W], refs[3 + N_W]
    refs = refs[4 + N_W :]
    mine, from_near, from_far, from_z = (refs[i * N_W : (i + 1) * N_W] for i in range(4))
    refs = refs[4 * N_W :]
    tall, wide, turned_a, gq, ev, d_side, n_turned, rows_a, rows_b, tall_w, wide_w = refs[:11]
    q_pre, w_turned, span, states, back = refs[11:16]
    load_sem, tall_sem, wide_sem, c_send, c_recv, n_send, n_recv, z_send, z_recv = refs[16:25]
    s_send, s_recv = refs[25:]
    rows, width = rows_a.shape
    half = rows // 2
    y, x, c, f, t = place()
    core, along_x, along_y, along_z = peers_of(f, t)
    all_ = slice(None)
    side = {"theirs": 1 - c, "mine": c}

    keys = {}

    def load(key, source, target):
        index = keys.setdefault(key, len(keys))
        return pltpu.make_async_copy(source, target, load_sem.at[index])

    def pair_columns(i):
        return slice(i * 2 * HEAD_DIM, (i + 1) * 2 * HEAD_DIM)

    def by_pairs(key, source, place_):
        return [load((key, i), source.at[:, pair_columns(i)], q_pre.at[place_, i]) for i in range(4)]

    lane_pair = [slice(0, 2 * HEAD_DIM), slice(2 * HEAD_DIM, 4 * HEAD_DIM)]
    loads = {
        "cot": by_pairs("cot", out_grad, 0),
        "tokens": by_pairs("tokens", tokens, 0),
        "a": [load("a", a_in, turned_a)],
        "g": [load("g", inp["g"], gq)],
        "e": [load("e", inp["e"], ev)],
        "n2": [load("n2", inp["n2_turned"], n_turned)],
        "n1": [load("n1", inp["n1_turned"], n_turned)],
        "y1": [load("y1", inp["y1"], rows_a)],
        "o": [load("o", inp["o"], rows_a)],
        "w": [load("w", inp["w_turned"], w_turned)],
        "qp": [load("qp", inp["qp"], q_pre.at[0])],
        "kp": [load("kp", inp["kp"], q_pre.at[1])],
        "q": [load("q", inp["q"], gq.at[:, :, lane_pair[0]])],
        "k": [load("k", inp["k"], gq.at[:, :, lane_pair[1]])],
        "v": [load("v", inp["v"], ev.at[:, :, lane_pair[0]])],
        "up": [load("up", inp["up"], turned_a.at[:, :rows, lane_pair[1]])],
        "out": [load("out", rows_b, d_tokens)],
    }

    def start(*names):
        for name in names:
            for copy in loads[name]:
                copy.start()

    def wait(*names):
        for name in names:
            for copy in loads[name]:
                copy.wait()

    def tile(w, i, slot):
        if w in (4, 7):
            depth = kept[w].shape[4]
            return pltpu.make_async_copy(
                kept[w].at[:, :, :, i], tall_w.at[slot, :, :, :, :depth], tall_sem.at[slot]
            )
        lanes = kept[w].shape[5]
        return pltpu.make_async_copy(
            kept[w].at[:, :, :, i], wide_w.at[slot, :, :, :, :, :lanes], wide_sem.at[slot]
        )

    def over_tiles(w, use):
        tile(w, 0, 0).start()

        def step(i, carry):
            slot = lax.rem(i, 2)

            @pl.when(i < 3)
            def _():
                tile(w, i + 1, 1 - slot).start()

            tile(w, i, slot).wait()
            use(i, slot)
            return carry

        lax.fori_loop(0, 4, step, 0)

    pieces = [(w, h) for w in range(N_W) for h in range(2)]

    def remote(src, dst, send, recv, peer):
        return pltpu.make_async_remote_copy(
            src_ref=src, dst_ref=dst, send_sem=send, recv_sem=recv, device_id=peer, device_id_type=MESH
        )

    def rows_of(p):
        w, h = pieces[p]
        part = grads[w].shape[0] // 2
        return pl.ds(h * part, part)

    def ring_of(w):
        return (tall, 0) if w in (4, 7) else (wide, 1)

    def core_copy(w, i):
        ring, kind = ring_of(w)
        depth, lanes = grads[w].shape
        return remote(
            ring.at[lax.rem(i, 2), :, :, :depth, :lanes],
            mine[w].at[:, :, i],
            c_send.at[kind, lax.rem(i, 2)],
            c_recv.at[w, i],
            core,
        )

    def near_copy(p):
        (w, h), part = pieces[p], rows_of(p)
        src = mine[w].at[1 - y, :, :, part] if h == 0 else mine[w].at[:, 1 - x, :, part]
        return remote(
            src,
            from_near[w].at[:, :, part],
            n_send.at[p, 0],
            n_recv.at[p, 0],
            along_y if h == 0 else along_x,
        )

    def far_copy(p):
        (w, h), part = pieces[p], rows_of(p)
        src = mine[w].at[y, 1 - x, :, part] if h == 0 else mine[w].at[1 - y, x, :, part]
        return remote(
            src,
            from_far[w].at[:, part],
            n_send.at[p, 1],
            n_recv.at[p, 1],
            along_x if h == 0 else along_y,
        )

    def z_copy(p, d):
        w, part = pieces[p][0], rows_of(p)
        return remote(
            mine[w].at[y, x, (t + d + 1) % 4, part],
            from_z[w].at[d, part],
            z_send.at[p, d],
            z_recv.at[p, d],
            along_z[d],
        )

    def add(steps, target, other):
        def step(i, carry):
            into, term = target(i), other(i)
            into[...] = (into[...].astype(jnp.float32) + term[...].astype(jnp.float32)).astype(
                jnp.bfloat16
            )
            return carry

        lax.fori_loop(0, steps, step, 0)

    def after_near(p):
        (w, h), part = pieces[p], rows_of(p)
        near_copy(p).wait_recv()
        if h == 0:
            into = lambda i: mine[w].at[y, i // 4, i % 4, part]
        else:
            into = lambda i: mine[w].at[i // 4, x, i % 4, part]
        add(8, into, lambda i: from_near[w].at[i // 4, i % 4, part])
        far_copy(p).start()

    def after_far(p):
        w, part = pieces[p][0], rows_of(p)
        far_copy(p).wait_recv()
        add(4, lambda i: mine[w].at[y, x, i, part], lambda i: from_far[w].at[i, part])
        for d in range(3):
            z_copy(p, d).start()

    def after_z(p):
        w, part = pieces[p][0], rows_of(p)
        for d in range(3):
            z_copy(p, d).wait_recv()
        result = mine[w][y, x, t, part].astype(jnp.float32)
        for d in range(3):
            result = result + from_z[w][d, part].astype(jnp.float32)
        grads[w][part] = result

    used = {0: None, 1: None}

    def gradient(w, whose, value):
        ring, kind = ring_of(w)
        depth, lanes = grads[w].shape

        def blocks(result):
            if kind == 1:
                return [(j // 2, j % 2, result[j * depth : (j + 1) * depth]) for j in range(4)]
            return [(j // 2, j % 2, result[:, j * lanes : (j + 1) * lanes]) for j in range(4)]

        def run():
            if whose == "theirs":
                before = used[kind]
                used[kind] = w

                def step(i, carry):
                    if before is not None:

                        @pl.when(i < 2)
                        def _():
                            core_copy(before, i + 2).wait_send()

                    @pl.when(i >= 2)
                    def _():
                        core_copy(w, i - 2).wait_send()

                    slot = lax.rem(i, 2)
                    result = value(i, side[whose]).astype(jnp.bfloat16)
                    for a, b, part in blocks(result):
                        ring[slot, a, b, :depth, :lanes] = part
                    core_copy(w, i).start()
                    return carry

                lax.fori_loop(0, 4, step, 0)
            else:

                def step(i, carry):
                    core_copy(w, i).wait_recv()
                    result = value(i, side[whose])
                    for a, b, part in blocks(result):
                        mine[w][a, b, i] = (mine[w][a, b, i].astype(jnp.float32) + part).astype(
                            jnp.bfloat16
                        )
                    return carry

                lax.fori_loop(0, 4, step, 0)
                for h in range(2):
                    near_copy(2 * w + h).start()

        return run

    ends, first, offsets, segments = row_tables(lengths, t, rows)
    steps_f = offsets.astype(jnp.float32)
    seg_before = scalar_segment(first - 1, ends)
    seg_after = scalar_segment(first + rows, ends)
    seg_first = scalar_segment(first, ends)

    def lanes_of(j, base=0):
        return slice(base + j * HEAD_DIM, base + (j + 1) * HEAD_DIM)

    def rate_of(h):
        return inp["rates8"][pl.ds(h, 1), :]

    def over_rows(use):
        def step(i, carry):
            use(pl.ds(pl.multiple_of(i * BAND, BAND), BAND))
            return carry

        lax.fori_loop(0, rows // BAND, step, 0)

    def begin():
        start("cot", "a", "e", "g", "n2", "y1", "w")
        fill_span(span, ends, first)
        live = jnp.where(segments < SLOTS - 1, 1.0, 0.0)
        wait("cot")
        for i in range(4):
            for s in range(2):
                part = q_pre[0, i, :, lanes_of(s)].astype(jnp.float32) * live
                d_side[s, :, lanes_of(i)] = part.astype(jnp.bfloat16)
        start("qp", "kp")
        wait("a")

    def expand():
        wait("e", "g")

        def use(i, slot):
            for b in range(2):
                part = slice(b * half, (b + 1) * half)
                d_hidden = sum(
                    dot_nt(
                        d_side[s, part],
                        jnp.concatenate([tall_w[slot, j // 2, j % 2, s] for j in range(4)], axis=1),
                    )
                    for s in range(2)
                )
                lift, gate = ev[i, part].astype(jnp.float32), gq[i, part].astype(jnp.float32)
                ev[i, part] = (d_hidden * lift).astype(jnp.bfloat16)
                gq[i, part] = (d_hidden * gate).astype(jnp.bfloat16)

        over_tiles(7, use)
        wait("n2")

    def through(w, source, target, clear):
        def run():
            if clear:
                target[...] = jnp.zeros_like(target)
            lanes = kept[w].shape[5]

            def use(i, slot):
                for j in range(4):
                    part = wide_w[slot, j // 2, j % 2, :, :, :lanes].reshape(2 * HEAD_DIM, lanes)
                    target[:, pair_columns(j)] += dot_nt(source(i), part)

            over_tiles(w, use)

        return run

    def middle_back():
        start("v", "q", "k")
        wait("y1")

        def use(part):
            values = rows_a[part, :]
            cot = jnp.concatenate(
                [d_side[j % 2, part, lanes_of(j // 2)].astype(jnp.float32) for j in range(8)], axis=1
            )
            result = cot + norm_back(values, rms_scale(values), rows_b[part, :])
            rows_b[part, :] = result
            for j in range(8):
                d_side[j % 2, part, lanes_of(j // 2)] = result[:, lanes_of(j)].astype(jnp.bfloat16)

        over_rows(use)
        start("o")
        wait("w")

    def mixed_back():
        wait("o", "up")

        def use(i, slot):
            d_mixed = sum(
                dot_nt(
                    d_side[s],
                    jnp.concatenate(
                        [tall_w[slot, j // 2, j % 2, s, : 2 * HEAD_DIM] for j in range(4)], axis=1
                    ),
                )
                for s in range(2)
            )
            for j in range(2):
                columns = pl.ds(pl.multiple_of((2 * i + j) * HEAD_DIM, HEAD_DIM), HEAD_DIM)
                attn = rows_a[:, columns]
                scale = rms_scale(attn, head_floor)
                normed = attn * scale
                pre = turned_a[i, :rows, lanes_of(j, 2 * HEAD_DIM)].astype(jnp.float32)
                part = d_mixed[:, lanes_of(j)]
                turned_a[i, :rows, lanes_of(j)] = (part * normed * slope_of(pre)).astype(jnp.bfloat16)
                d_attn = norm_back(attn, scale, part * swish_of(pre))
                ev[i, :, lanes_of(j, 2 * HEAD_DIM)] = d_attn.astype(jnp.bfloat16)

        over_tiles(4, use)
        wait("n1", "q")

    def make_states():
        def pair(i, carry):
            for j in range(2):
                rate = rate_of(2 * i + j)[:, :HEAD_DIM]
                from_start = jnp.where(segments == seg_first, jnp.exp(-steps_f * rate), 0.0)
                scaled = (gq[i, :, lanes_of(j)].astype(jnp.float32) * from_start).astype(jnp.bfloat16)
                states[t, 2 * i + j] = dot_tn(scaled, ev[i, :, lanes_of(j, 2 * HEAD_DIM)]).astype(
                    jnp.bfloat16
                )
            return carry

        lax.fori_loop(0, 4, pair, 0)

    def state_copy(d, source):
        ref = states.at[source]
        return remote(ref, ref, s_send.at[d], s_recv.at[d], along_z[d])

    def send_states():
        for d in range(3):
            state_copy(d, t).start()

    def sum_states():
        wait("v", "k", "qp", "kp")
        for d in range(3):
            state_copy(d, (t + 3 - d) % 4).wait_recv()

        def head(h, carry):
            rate = rate_of(h)[:, :HEAD_DIM]
            result = jnp.zeros((HEAD_DIM, HEAD_DIM), jnp.float32)
            for j in range(1, 4):
                reach = jnp.where((j > t) & (scalar_segment(j * rows, ends) == seg_after), 1.0, 0.0)
                distance = jnp.maximum(j - t - 1, 0).astype(jnp.float32) * rows
                weight = reach * jnp.exp(-rate * distance)
                result = result + weight * states[j, h].astype(jnp.float32)
            back[h] = result.astype(jnp.bfloat16)
            return carry

        lax.fori_loop(0, 8, head, 0)

    def attend_back(h, carry):
        cos, sin = inp["cos"][...], inp["sin"][...]
        i, j = h // 2, lax.rem(h, 2)
        low_lanes = pl.ds(pl.multiple_of(j * HEAD_DIM, HEAD_DIM), HEAD_DIM)
        high_lanes = pl.ds(pl.multiple_of((2 + j) * HEAD_DIM, HEAD_DIM), HEAD_DIM)
        rate = rate_of(h)
        short = rate[:, :HEAD_DIM]
        key, value = gq[i, :, high_lanes], ev[i, :, low_lanes]
        state_in, state_back = inp["states"][h], back[h]
        out_of = jnp.where(segments == seg_after, jnp.exp(-(rows - steps_f) * short), 0.0)
        d_value = out_of * dot(key, state_back)
        d_key = out_of * dot_nt(value, state_back)
        d_query = []
        for b in range(2):
            part = slice(b * half, (b + 1) * half)
            keys = (b + 1) * half
            query = gq[i, part, low_lanes]
            grad = ev[i, part, high_lanes]
            decay = jnp.exp(-span[part, :keys] * rate[:, :keys])
            weights = (dot_nt(query, key[:keys]) * decay).astype(jnp.bfloat16)
            d_raw = (dot_nt(grad, value[:keys]) * decay).astype(jnp.bfloat16)
            into = jnp.where(
                segments[part] == seg_before, jnp.exp(-(steps_f[part] + 1.0) * short), 0.0
            )
            d_query.append(dot(d_raw, key[:keys]) + into * dot_nt(grad, state_in))
            add_value, add_key = dot_tn(weights, grad), dot_tn(d_raw, query)
            if b == 0:
                d_value = jnp.concatenate([d_value[:half] + add_value, d_value[half:]], axis=0)
                d_key = jnp.concatenate([d_key[:half] + add_key, d_key[half:]], axis=0)
            else:
                d_value, d_key = d_value + add_value, d_key + add_key
        d_query = jnp.concatenate(d_query, axis=0)
        pre_query = q_pre[0, i, :, low_lanes].astype(jnp.float32)
        pre_key = q_pre[1, i, :, low_lanes].astype(jnp.float32)
        gq[i, :, low_lanes] = (slope_of(pre_query) * turn_back(d_query, cos, sin)).astype(
            jnp.bfloat16
        )
        gq[i, :, high_lanes] = (
            slope_of(pre_key) * turn_back(d_key, cos, sin)
        ).astype(jnp.bfloat16)
        ev[i, :, low_lanes] = d_value.astype(jnp.bfloat16)
        return carry

    def close():
        wait("tokens")

        def use(part):
            values = jnp.concatenate([q_pre[0, i, part, :] for i in range(4)], axis=1)
            values = values.astype(jnp.float32)
            rows_b[part, :] += norm_back(values, rms_scale(values), rows_a[part, :])

        over_rows(use)
        start("out")

    low_pair, high_pair = slice(0, 2 * HEAD_DIM), slice(2 * HEAD_DIM, 4 * HEAD_DIM)
    sources = {
        0: lambda i: gq[i, :, low_pair],
        1: lambda i: gq[i, :, high_pair],
        2: lambda i: ev[i, :, low_pair],
        3: lambda i: turned_a[i, :rows, low_pair],
        5: lambda i: ev[i],
        6: lambda i: gq[i],
    }

    def grad(w, whose):
        if w == 7:
            value = lambda i, s: dot(turned_a[i], d_side[s])
        elif w == 4:
            value = lambda i, s: dot(w_turned[i], d_side[s])
        else:
            value = lambda i, s: dot(n_turned[s], sources[w](i))
        return gradient(w, whose, value)

    def attend_pairs(lo, hi):
        return lambda: (lax.fori_loop(2 * lo, 2 * hi, attend_back, 0), None)[1]

    work = [
        (3.0, begin, None),
        (2.5, grad(7, "theirs"), None),
        (6.0, expand, None),
        (2.5, grad(5, "theirs"), None),
        (3.0, grad(7, "mine"), 7),
        (0.1, lambda: start("up"), None),
        (2.5, grad(6, "theirs"), None),
        (3.0, grad(5, "mine"), 5),
        (3.0, grad(6, "mine"), 6),
        (0.1, lambda: start("n1"), None),
        (5.0, through(5, sources[5], rows_b, True), None),
        (5.0, through(6, sources[6], rows_b, False), None),
        (3.0, middle_back, None),
        (1.0, grad(4, "theirs"), None),
        (6.0, mixed_back, None),
        (1.0, grad(3, "theirs"), None),
        (1.2, grad(4, "mine"), 4),
        (2.0, make_states, None),
        (1.2, grad(3, "mine"), 3),
        (0.1, send_states, None),
        (2.0, through(3, sources[3], rows_a, True), None),
        (1.0, sum_states, None),
        (4.0, attend_pairs(0, 1), None),
        (4.0, attend_pairs(1, 2), None),
        (4.0, attend_pairs(2, 3), None),
        (4.0, attend_pairs(3, 4), None),
        (1.0, grad(2, "theirs"), None),
        (1.0, grad(0, "theirs"), None),
        (1.0, grad(1, "theirs"), None),
        (1.2, grad(2, "mine"), 2),
        (1.2, grad(0, "mine"), 0),
        (1.2, grad(1, "mine"), 1),
        (0.1, lambda: start("tokens"), None),
        (2.0, through(2, sources[2], rows_a, False), None),
        (2.0, through(0, sources[0], rows_a, False), None),
        (2.0, through(1, sources[1], rows_a, False), None),
        (2.0, close, None),
    ]
    meet([core, along_x, along_y, *along_z])
    clock, free, events = 0.0, {"x": 0.0, "y": 0.0, "z": 0.0}, []

    def expect(link, blocks, p, step):
        size = blocks * grads[pieces[p][0]].size // 2 * 2
        free[link] = max(free[link], clock) + size / LINK
        events.append((free[link] + 2.0, step, p))

    while work or events:
        events.sort(key=lambda event: event[0])
        if events and (not work or events[0][0] <= clock):
            due, step, p = events.pop(0)
            clock = max(clock, due) + 0.3
            h = pieces[p][1]
            if step == "near":
                after_near(p)
                expect("x" if h == 0 else "y", 4, p, "far")
            elif step == "far":
                after_far(p)
                expect("z", 4, p, "z")
            else:
                after_z(p)
        else:
            time_, run, done = work.pop(0)
            run()
            clock += time_
            if done is not None:
                for h in range(2):
                    expect("y" if h == 0 else "x", 8, 2 * done + h, "near")
    for kind in range(2):
        for i in range(2, 4):
            core_copy(used[kind], i).wait_send()
    for p in range(len(pieces)):
        near_copy(p).wait_send()
        far_copy(p).wait_send()
        for d in range(3):
            z_copy(p, d).wait_send()
    for d in range(3):
        state_copy(d, t).wait_send()
    wait("out")


def backward(kept, a_turned, saved, cos, sin, tokens, out_grad, lengths):
    rows, width = tokens.shape
    low, wide = jnp.bfloat16, jnp.float32
    units = a_turned.shape[1]
    pair = width // 4
    shards = [w.shape[4:] for w in kept]
    dma = pltpu.SemaphoreType.DMA
    anywhere, in_vmem, in_smem = (
        pl.BlockSpec(memory_space=m) for m in (pl.ANY, pltpu.VMEM, pltpu.SMEM)
    )
    pieces = 2 * N_W

    def buffers(*lead):
        return [pltpu.VMEM((*lead, *s), low) for s in shards]

    outs = pl.pallas_call(
        backward_kernel,
        name="backward_and_scatter",
        out_shape=[jax.ShapeDtypeStruct(s, wide) for s in shards]
        + [jax.ShapeDtypeStruct((rows, width), wide)],
        in_specs=[anywhere] * (N_W + 1 + len(BWD_ANY))
        + [in_vmem] * len(BWD_VMEM)
        + [anywhere, anywhere, in_smem],
        out_specs=[in_vmem] * N_W + [anywhere],
        scratch_shapes=[
            *buffers(2, 2, 4),
            *buffers(2, 4),
            *buffers(4),
            *buffers(3),
            pltpu.VMEM((2, 2, 2, units, HEAD_DIM), low),
            pltpu.VMEM((2, 2, 2, HEAD_DIM, units), low),
            pltpu.VMEM((4, units, rows), low),
            pltpu.VMEM((4, rows, units), low),
            pltpu.VMEM((4, rows, units), low),
            pltpu.VMEM((2, rows, width // 2), low),
            pltpu.VMEM((2, width // 2, rows), low),
            pltpu.VMEM((rows, width), wide),
            pltpu.VMEM((rows, width), wide),
            pltpu.VMEM((2, 2, 2, 2, units, HEAD_DIM), low),
            pltpu.VMEM((2, 2, 2, 2, HEAD_DIM, units), low),
            pltpu.VMEM((2, 4, rows, pair), low),
            pltpu.VMEM((4, pair, rows), low),
            pltpu.VMEM((rows, rows), wide),
            pltpu.VMEM((4, width // HEAD_DIM, HEAD_DIM, HEAD_DIM), low),
            pltpu.VMEM((width // HEAD_DIM, HEAD_DIM, HEAD_DIM), low),
            dma((24,)),
            dma((2,)),
            dma((2,)),
            dma((2, 2)),
            dma((N_W, 4)),
            dma((pieces, 2)),
            dma((pieces, 2)),
            dma((pieces, 3)),
            dma((pieces, 3)),
            dma((3,)),
            dma((3,)),
        ],
        compiler_params=pltpu.CompilerParams(
            collective_id=1, has_side_effects=True, vmem_limit_bytes=VMEM_BYTES
        ),
    )(
        *kept,
        a_turned,
        *[saved[name] for name in BWD_ANY],
        saved["states"],
        saved["rates8"],
        cos,
        sin,
        tokens,
        out_grad,
        lengths,
    )
    return outs[:N_W], outs[N_W]


def body_by_kernels(
    tokens,
    lengths,
    rates,
    w_query,
    w_key,
    w_value,
    w_update,
    w_output,
    w_gate,
    w_up,
    w_down,
    out_grad,
):
    rows = tokens.shape[0]
    ends = jnp.cumsum(lengths[0], dtype=jnp.int32)
    places = lax.axis_index("tp") * rows + jnp.arange(rows, dtype=jnp.int32)
    segments = segment_of(places, ends)
    slots = jnp.arange(SLOTS, dtype=jnp.int32)
    starts = jnp.sum(jnp.where(segments[:, None] == slots, ends - lengths[0], 0), axis=1)
    positions = (places - starts).astype(jnp.float32)
    frequency = 10000.0 ** (-2.0 * jnp.arange(HEAD_DIM // 2, dtype=jnp.float32) / HEAD_DIM)
    turned = positions[:, None] * frequency[None, :]
    cos_half, sin_half = jnp.cos(turned), jnp.sin(turned)
    cos = jnp.concatenate([cos_half, cos_half], axis=1)
    sin = jnp.concatenate([-sin_half, sin_half], axis=1)
    shards = (w_query, w_key, w_value, w_update, w_output, w_gate, w_up, w_down)
    kept, a_turned, saved = forward(shards, tokens, cos, sin, lengths, rates)
    grads, d_tokens = backward(kept, a_turned, saved, cos, sin, tokens, out_grad, lengths)
    return (saved["result"], d_tokens, *grads)


def body(
    tokens,
    lengths,
    rates,
    w_query,
    w_key,
    w_value,
    w_update,
    w_output,
    w_gate,
    w_up,
    w_down,
    out_grad,
):
    tp_count = lax.axis_size("tp")
    tp_index = lax.axis_index("tp")
    rows, width = tokens.shape
    head_width = HEAD_DIM
    all_rates = lax.all_gather(rates, "tp", axis=0, tiled=True)
    heads = all_rates.shape[0]
    ends = jnp.cumsum(lengths[0], dtype=jnp.int32)
    first = tp_index * rows
    places = first + jnp.arange(rows, dtype=jnp.int32)
    segments = segment_of(places, ends)
    starts = ends - lengths[0]
    slots = jnp.arange(SLOTS, dtype=jnp.int32)
    positions = (
        places - jnp.sum(jnp.where(segments[:, None] == slots, starts, 0), axis=1)
    ).astype(jnp.float32)
    live = (segments < SLOTS - 1).astype(jnp.float32)
    frequency = 10000.0 ** (-2.0 * jnp.arange(head_width // 2, dtype=jnp.float32) / head_width)
    turned = positions[:, None] * frequency[None, :]
    cos_table, sin_table = jnp.cos(turned)[:, None, :], jnp.sin(turned)[:, None, :]

    gaps = places[:, None] - places[None, :]
    allowed = (segments[:, None] == segments[None, :]) & (gaps >= 0)
    spans = jnp.maximum(gaps, 0).astype(jnp.float32)
    decay = jnp.where(
        allowed[None], jnp.exp(-all_rates[:, None, None] * spans[None]), 0.0
    )
    blocks = jnp.arange(tp_count, dtype=jnp.int32)
    seg_before = segment_of(first - 1, ends)
    seg_after = segment_of(first + rows, ends)
    seg_last = segment_of(blocks * rows + rows - 1, ends)
    seg_first = segment_of(blocks * rows, ends)
    offsets = jnp.arange(rows, dtype=jnp.float32)

    def row_decay(distance, mask):
        return jnp.where(mask[:, None], jnp.exp(-distance[:, None] * all_rates[None]), 0.0)[
            :, :, None
        ]

    to_end = row_decay(rows - 1 - offsets, segments == segments[rows - 1])
    from_start = row_decay(offsets, segments == segments[0])
    into = row_decay(offsets + 1.0, segments == seg_before)
    out_of = row_decay(rows - offsets, segments == seg_after)

    def block_weights(mask, distance):
        distance = jnp.maximum(distance, 0).astype(jnp.float32)
        return jnp.where(mask[:, None], jnp.exp(-distance[:, None] * all_rates[None]), 0.0)

    before_weights = block_weights(
        (blocks < tp_index) & (seg_last == seg_before), (tp_index - blocks - 1) * rows
    )
    after_weights = block_weights(
        (blocks > tp_index) & (seg_first == seg_after), (blocks - tp_index - 1) * rows
    )

    tokens_f = tokens.astype(jnp.float32)
    scale1 = rms_scale(tokens_f)
    normed1 = (tokens_f * scale1).astype(jnp.bfloat16)
    shards = (w_query, w_key, w_value, w_update, w_output, w_gate, w_up, w_down)
    inner = (True, True, True, True, False, True, True, False)
    full = [
        gather_full(w, "fsdp", "tp") if rows_first else gather_full(w, "tp", "fsdp")
        for w, rows_first in zip(shards, inner)
    ]
    (
        query_full,
        key_full,
        value_full,
        update_full,
        output_full,
        gate_full,
        up_full,
        down_full,
    ) = full
    shape_heads = (rows, heads, head_width)
    query_pre = mm(normed1, query_full)
    key_pre = mm(normed1, key_full)
    value_rows = mm(normed1, value_full).astype(jnp.bfloat16).reshape(shape_heads)
    update_pre = mm(normed1, update_full)
    query = rotate(swish(query_pre).reshape(shape_heads), cos_table, sin_table).astype(jnp.bfloat16)
    key_rows = rotate(swish(key_pre).reshape(shape_heads), cos_table, sin_table).astype(
        jnp.bfloat16
    )
    update = swish(update_pre)
    key_state = heads_dot(
        "shc,shd->hcd", (key_rows * to_end).astype(jnp.bfloat16), value_rows
    ).astype(jnp.bfloat16)
    key_states = lax.all_gather(key_state, "tp", axis=0, tiled=False)
    state_in = jnp.sum(
        key_states.astype(jnp.float32) * before_weights[:, :, None, None], axis=0
    ).astype(jnp.bfloat16)
    weights = (heads_dot("thc,shc->hts", query, key_rows) * decay).astype(jnp.bfloat16)
    attn = heads_dot("hts,shd->thd", weights, value_rows) + into * heads_dot(
        "thc,hcd->thd", query, state_in
    )
    scale_attn = rms_scale(attn, head_floor)
    normed_attn = (attn * scale_attn).reshape(rows, width)
    mixed = (normed_attn * update).astype(jnp.bfloat16)
    middle = tokens_f + mm(mixed, output_full)
    scale2 = rms_scale(middle)
    normed2 = (middle * scale2).astype(jnp.bfloat16)
    gate_rows = mm(normed2, gate_full)
    up_rows = mm(normed2, up_full)
    hidden = (gate_rows * up_rows).astype(jnp.bfloat16)
    result = (middle + mm(hidden, down_full)).astype(jnp.bfloat16)

    cotangent = out_grad.astype(jnp.float32) * live[:, None]
    cot_rows = cotangent.astype(jnp.bfloat16)
    grad_down = mm_inner(hidden, cot_rows)
    d_hidden = mm_trans(cot_rows, down_full)
    d_gate = (d_hidden * up_rows).astype(jnp.bfloat16)
    d_up = (d_hidden * gate_rows).astype(jnp.bfloat16)
    grad_gate = mm_inner(normed2, d_gate)
    grad_up = mm_inner(normed2, d_up)
    d_normed2 = mm_trans(d_gate, gate_full) + mm_trans(d_up, up_full)
    d_middle = cotangent + norm_back(middle, scale2, d_normed2)
    mid_rows = d_middle.astype(jnp.bfloat16)
    d_mixed = mm_trans(mid_rows, output_full)
    grad_output = mm_inner(mixed, mid_rows)
    d_update_pre = (d_mixed * normed_attn * swish_slope(update_pre)).astype(jnp.bfloat16)
    d_attn = norm_back(attn, scale_attn, (d_mixed * update).reshape(shape_heads)).astype(
        jnp.bfloat16
    )
    query_state = heads_dot(
        "thc,thd->hcd", (query * from_start).astype(jnp.bfloat16), d_attn
    ).astype(jnp.bfloat16)
    query_states = lax.all_gather(query_state, "tp", axis=0, tiled=False)
    state_back = jnp.sum(
        query_states.astype(jnp.float32) * after_weights[:, :, None, None], axis=0
    ).astype(jnp.bfloat16)
    d_raw = (heads_dot("thd,shd->hts", d_attn, value_rows) * decay).astype(jnp.bfloat16)
    d_value = heads_dot("hts,thd->shd", weights, d_attn) + out_of * heads_dot(
        "shc,hcd->shd", key_rows, state_back
    )
    d_query = heads_dot("hts,shc->thc", d_raw, key_rows) + into * heads_dot(
        "thd,hcd->thc", d_attn, state_in
    )
    d_key = heads_dot("hts,thc->shc", d_raw, query) + out_of * heads_dot(
        "shd,hcd->shc", value_rows, state_back
    )
    d_query_pre = (
        swish_slope(query_pre) * rotate_back(d_query, cos_table, sin_table).reshape(rows, width)
    ).astype(jnp.bfloat16)
    d_key_pre = (
        swish_slope(key_pre) * rotate_back(d_key, cos_table, sin_table).reshape(rows, width)
    ).astype(jnp.bfloat16)
    d_value_pre = d_value.reshape(rows, width).astype(jnp.bfloat16)
    grads = [mm_inner(normed1, d) for d in (d_query_pre, d_key_pre, d_value_pre, d_update_pre)]
    d_normed1 = (
        mm_trans(d_query_pre, query_full)
        + mm_trans(d_key_pre, key_full)
        + mm_trans(d_value_pre, value_full)
        + mm_trans(d_update_pre, update_full)
    )
    d_tokens = d_middle + norm_back(tokens_f, scale1, d_normed1)
    grads = (*grads, grad_output, grad_gate, grad_up, grad_down)
    grads = [
        scatter_grad(g, "fsdp", "tp") if rows_first else scatter_grad(g, "tp", "fsdp")
        for g, rows_first in zip(grads, inner)
    ]
    return (result, d_tokens, *grads)


def solution(mesh):
    rows = P(AXES, None)
    inner, outer = P("fsdp", "tp"), P("tp", "fsdp")
    by_kernels = mesh.shape["fsdp"] == 8 and mesh.shape["tp"] == 4
    return jax.shard_map(
        body_by_kernels if by_kernels else body,
        mesh=mesh,
        in_specs=(
            rows,
            P("fsdp", None),
            P("tp"),
            inner,
            inner,
            inner,
            inner,
            outer,
            inner,
            inner,
            outer,
            rows,
        ),
        out_specs=(rows, rows, inner, inner, inner, inner, outer, inner, inner, outer),
        check_vma=False,
    )
```

```python
import functools

import jax
import jax.numpy as jnp
from jax import lax
from jax.experimental import pallas as pl
from jax.experimental.pallas import tpu as pltpu
from jax.sharding import PartitionSpec as P

HEAD_DIM = 128
SLOTS = 4

epsilon = 1e-06
head_floor = 1.0
AXES = ("fsdp", "tp")


def swish(values):
    return values * jax.nn.sigmoid(values)


def swish_slope(values):
    sigma = jax.nn.sigmoid(values)
    return sigma * (1.0 + values * (1.0 - sigma))


def rms_scale(values, offset=epsilon):
    return lax.rsqrt(jnp.mean(values * values, axis=-1, keepdims=True) + offset)


def norm_back(values, scale, grads):
    normed = values * scale
    return scale * (grads - normed * jnp.mean(grads * normed, axis=-1, keepdims=True))


def segment_of(places, ends):
    return jnp.sum((places[..., None] >= ends).astype(jnp.int32), axis=-1, dtype=jnp.int32)


def rotate(values, cos_table, sin_table):
    half = values.shape[-1] // 2
    front, back = values[..., :half], values[..., half:]
    return jnp.concatenate(
        [front * cos_table - back * sin_table, front * sin_table + back * cos_table], axis=-1
    )


def rotate_back(values, cos_table, sin_table):
    return rotate(values, cos_table, -sin_table)


def mm(left, right):
    return jnp.dot(left, right, preferred_element_type=jnp.float32)


def mm_trans(left, right):
    return lax.dot_general(
        left, right, (((1,), (1,)), ((), ())), preferred_element_type=jnp.float32
    )


def mm_inner(left, right):
    return lax.dot_general(
        left, right, (((0,), (0,)), ((), ())), preferred_element_type=jnp.float32
    )


def heads_dot(spec, left, right):
    return jnp.einsum(spec, left, right, preferred_element_type=jnp.float32)


def gather_full(shard, row_axis, column_axis):
    part = lax.all_gather(shard, "tp", axis=0 if row_axis == "tp" else 1, tiled=True)
    return lax.all_gather(part, "fsdp", axis=0 if row_axis == "fsdp" else 1, tiled=True)


def scatter_grad(grad, row_axis, column_axis):
    part = grad.astype(jnp.bfloat16)
    part = lax.psum_scatter(
        part, "fsdp", scatter_dimension=0 if row_axis == "fsdp" else 1, tiled=True
    )
    part = lax.psum_scatter(part, "tp", scatter_dimension=0 if row_axis == "tp" else 1, tiled=True)
    return part.astype(jnp.float32)


MESH = pl.DeviceIdType.MESH
VMEM_BYTES = 66_000_000


def place():
    f, t = lax.axis_index("fsdp"), lax.axis_index("tp")
    return f // 4, (f // 2) % 2, f % 2, f, t


def meet(peers):
    barrier = pltpu.get_barrier_semaphore()
    for peer in peers:
        pl.semaphore_signal(barrier, inc=1, device_id=peer, device_id_type=MESH)
    pl.semaphore_wait(barrier, len(peers))


def peers_of(f, t):
    core = (f // 2 * 2 + (1 - f % 2), t)
    along_x = (f // 4 * 4 + (f + 2) % 4, t)
    along_y = ((f + 4) % 8, t)
    along_z = [(f, (t + d) % 4) for d in (1, 2, 3)]
    return core, along_x, along_y, along_z


FAR = 1e7


def swish_of(values):
    return values * jax.nn.sigmoid(values)


def segment_at(where, ends):
    return sum((where >= end).astype(jnp.int32) for end in ends)


def row_tables(lengths_ref, t, rows):
    ends, total = [], jnp.int32(0)
    for j in range(SLOTS):
        total = total + lengths_ref[0, j]
        ends.append(total)
    first = t * rows
    offsets = lax.broadcasted_iota(jnp.int32, (rows, HEAD_DIM), 0)
    return ends, first, offsets, segment_at(first + offsets, ends)


def scalar_segment(where, ends):
    return sum(jnp.where(where >= end, 1, 0) for end in ends)


def fill_span(span_ref, ends, first):
    rows = span_ref.shape[0]
    band = 32

    def step(i, carry):
        row = first + i * band + lax.broadcasted_iota(jnp.int32, (band, rows), 0)
        column = first + lax.broadcasted_iota(jnp.int32, (band, rows), 1)
        allowed = (segment_at(row, ends) == segment_at(column, ends)) & (row >= column)
        span_ref[pl.ds(pl.multiple_of(i * band, band), band), :] = jnp.where(
            allowed, (row - column).astype(jnp.float32), FAR
        )
        return carry

    lax.fori_loop(0, rows // band, step, 0)


def turn(values, cos, sin):
    return values * cos + pltpu.roll(values, HEAD_DIM // 2, 1) * sin


def dot(left, right):
    return jnp.dot(left, right, preferred_element_type=jnp.float32)


def dot_nt(left, right):
    return lax.dot_general(left, right, (((1,), (1,)), ((), ())), preferred_element_type=jnp.float32)


def dot_tn(left, right):
    return lax.dot_general(left, right, (((0,), (0,)), ((), ())), preferred_element_type=jnp.float32)


ORDER = (1, 2, 0, 3, 4, 5, 6, 7)
ROUTES = ("ab", "ab", "ab", "ab", "ab", "cdab", "abab", "abab")
SLACK = 10.0
RATE = 42_000.0


def arrange(work, first, after):
    clock, free, waiting, events, count = 0.0, {}, {}, [], 0
    known, work = set(), list(work)

    def offer(name):
        known.add(name)
        for item in after(name):
            waiting.setdefault(item[0], []).append(item)

    def pump():
        nonlocal count
        for link, items in waiting.items():
            while items and free.get(link, 0.0) <= clock + SLACK:
                _, size, send, receive, name = items.pop(0)
                send()
                free[link] = max(free.get(link, 0.0), clock) + size / RATE + 0.2
                events.append((free[link] + 2.0, count, receive, name))
                count += 1
        events.sort(key=lambda event: event[:2])

    for name in first:
        offer(name)
    pump()
    while work or events:
        if events and events[0][0] <= clock:
            _, _, receive, name = events.pop(0)
            receive()
            offer(name)
        elif work and work[0][2] <= known:
            took, step, _, done = work.pop(0)
            step()
            clock += took
            if done is not None:
                offer(done)
        else:
            times = [free[link] - SLACK for link, items in waiting.items() if items]
            clock = max(clock, min(times + [event[0] for event in events]))
        pump()


N_W = 8
FWD_IN = ("tokens", "cos", "sin", "lengths", "rates")
FWD_OUT = (
    "res",
    "qp",
    "kp",
    "up",
    "q",
    "k",
    "v",
    "o",
    "wt",
    "y1",
    "n1t",
    "n2t",
    "g",
    "e",
    "st",
    "r8",
)


def forward_kernel(*refs):
    shards, refs = refs[:N_W], refs[N_W:]
    inp = dict(zip(FWD_IN, refs))
    refs = refs[len(FWD_IN) :]
    kept, refs = refs[:N_W], refs[N_W:]
    a_out, refs = refs[0], refs[1:]
    out = dict(zip(FWD_OUT, refs))
    refs = refs[len(FWD_OUT) :]
    full, refs = refs[:N_W], refs[N_W:]
    buf = dict(zip(FWD_OUT, refs))
    refs = refs[len(FWD_OUT) :]
    n1, hidden, hidden_turned, span, states, rate_tiles, gate_shard, up_shard = refs[:8]
    own_sem, z_send, z_recv, n_send, n_recv, c_send, c_recv = refs[8:15]
    s_send, s_recv, r_send, r_recv, keep_sem, out_sem, turn_sem = refs[15:]
    gate_shard[...], up_shard[...] = shards[5][...].T, shards[6][...].T
    shards = (*shards[:5], gate_shard, up_shard, shards[7])
    n2, mixed = n1, buf["res"]
    rows = inp["tokens"].shape[0]
    y, x, c, f, t = place()
    core, along_x, along_y, along_z = peers_of(f, t)
    rate_tiles[t] = jnp.concatenate(
        [jnp.full((1, rows), inp["rates"][i % 2], jnp.float32) for i in range(8)], axis=0
    )
    meet([core, along_x, along_y, *along_z])
    pieces = [(w, h) for w in ORDER for h in range(len(ROUTES[w]))]
    total = len(pieces)
    all_ = slice(None)

    def rows_of(p):
        w, h = pieces[p]
        part = shards[w].shape[0] // len(ROUTES[w])
        return pl.ds(h * part, part)

    def route_of(p):
        w, h = pieces[p]
        return ROUTES[w][h]

    def slot(p, *index):
        return full[pieces[p][0]].at[(*index, rows_of(p))]

    def remote(src, dst, send, recv, peer):
        return pltpu.make_async_remote_copy(
            src_ref=src, dst_ref=dst, send_sem=send, recv_sem=recv, device_id=peer, device_id_type=MESH
        )

    def own_copy(p):
        return pltpu.make_async_copy(
            shards[pieces[p][0]].at[rows_of(p)], slot(p, y, x, c, t), own_sem.at[p]
        )

    def z_copy(p, d, source):
        if route_of(p) in "ab":
            src, dst = shards[pieces[p][0]].at[rows_of(p)], slot(p, y, x, c, source)
        else:
            src, dst = slot(p, all_, all_, c, t), slot(p, all_, all_, c, source)
        return remote(src, dst, z_send.at[p, d], z_recv.at[p, d], along_z[d])

    def near_copy(p, stage, arriving):
        over_x = (route_of(p) in "ac") == (stage == 0)
        if stage == 0:
            index = (y, x, c)
            if arriving:
                index = (y, 1 - x, c) if over_x else (1 - y, x, c)
        else:
            if over_x:
                index = (all_, (1 - x) if arriving else x, c)
            else:
                index = ((1 - y) if arriving else y, all_, c)
        ref = slot(p, *index, all_ if route_of(p) in "ab" else t)
        src = ref
        if stage == 0 and route_of(p) in "cd":
            src = shards[pieces[p][0]].at[rows_of(p)]
        return remote(
            src, ref, n_send.at[p, stage], n_recv.at[p, stage], along_x if over_x else along_y
        )

    def core_parts(p):
        return range(3 if route_of(p) in "ab" else 4)

    def core_copy(p, part, arriving):
        side = (1 - c) if arriving else c
        if route_of(p) in "ab":
            first_x = route_of(p) == "a"
            index = (
                (y, x, side, all_),
                (y, 1 - x, side, all_) if first_x else (1 - y, x, side, all_),
                (1 - y, all_, side, all_) if first_x else (all_, 1 - x, side, all_),
            )[part]
        else:
            index = (all_, all_, side, (t + part) % 4)
        ref = slot(p, *index)
        return remote(ref, ref, c_send.at[p, part], c_recv.at[p, part], core)

    def arrived(w):
        for p in range(total):
            if pieces[p][0] == w:
                for part in core_parts(p):
                    core_copy(p, part, True).wait_recv()
        keep(w).start()

    def keep(w):
        return pltpu.make_async_copy(full[w], kept[w], keep_sem.at[w])

    def save(name):
        return pltpu.make_async_copy(buf[name], out[name], out_sem.at[FWD_OUT.index(name)])

    def rate_copy(d, source):
        ref = rate_tiles.at[source]
        return remote(ref, ref, r_send.at[d], r_recv.at[d], along_z[d])

    def state_copy(d, source):
        ref = states.at[source]
        return remote(ref, ref, s_send.at[d], s_recv.at[d], along_z[d])

    ends, first, offsets, segments = row_tables(inp["lengths"], t, rows)
    steps_f = offsets.astype(jnp.float32)

    def head_columns(i, j):
        return pl.ds(pl.multiple_of(i * 2 * HEAD_DIM + j * HEAD_DIM, HEAD_DIM), HEAD_DIM)

    def rate_of(h):
        return buf["r8"][pl.ds(h, 1), :]

    def turn_rows(source, target):
        for j in range(8):
            part = source[:, j * HEAD_DIM : (j + 1) * HEAD_DIM]
            target[j % 2, j // 2 * HEAD_DIM : (j // 2 + 1) * HEAD_DIM] = part.T

    def begin():
        for d in range(3):
            rate_copy(d, t).start()
        values = inp["tokens"][...].astype(jnp.float32)
        n1[...] = (values * rms_scale(values)).astype(jnp.bfloat16)
        turn_rows(n1, buf["n1t"])
        save("n1t").start()
        fill_span(span, ends, first)

    def rates_here():
        for d in range(3):
            rate_copy(d, (t + 3 - d) % 4).wait_recv()
        for j in range(4):
            buf["r8"][2 * j : 2 * j + 2] = rate_tiles[j, 0:2]
        save("r8").start()

    def project(w, finish):
        def run():
            arrived(w)

            def block(i, carry):
                columns = full[w][:, :, :, i].reshape(n1.shape[1], full[w].shape[5])
                values = dot(n1[...], columns)
                for j in range(2):
                    finish(i, j, values[:, j * HEAD_DIM : (j + 1) * HEAD_DIM])
                return carry

            lax.fori_loop(0, 4, block, 0)

        return run

    def finish_key(i, j, values):
        lanes = slice(j * HEAD_DIM, (j + 1) * HEAD_DIM)
        buf["kp"][i, :, lanes] = values.astype(jnp.bfloat16)
        buf["k"][i, :, lanes] = turn(swish_of(values), inp["cos"][...], inp["sin"][...]).astype(jnp.bfloat16)

    def finish_query(i, j, values):
        lanes = slice(j * HEAD_DIM, (j + 1) * HEAD_DIM)
        buf["qp"][i, :, lanes] = values.astype(jnp.bfloat16)
        buf["q"][i, :, lanes] = turn(swish_of(values), inp["cos"][...], inp["sin"][...]).astype(jnp.bfloat16)

    def finish_value(i, j, values):
        lanes = slice(j * HEAD_DIM, (j + 1) * HEAD_DIM)
        buf["v"][i, :, lanes] = values.astype(jnp.bfloat16)

    def finish_update(i, j, values):
        lanes = slice(j * HEAD_DIM, (j + 1) * HEAD_DIM)
        buf["up"][i, :, lanes] = values.astype(jnp.bfloat16)
        buf["y1"][:, head_columns(i, j)] = swish_of(values)

    def make_states():
        last = scalar_segment(first + rows - 1, ends)

        def pair(i, carry):
            for j in range(2):
                h, lanes = 2 * i + j, slice(j * HEAD_DIM, (j + 1) * HEAD_DIM)
                rate = rate_of(h)[:, :HEAD_DIM]
                to_end = jnp.where(segments == last, jnp.exp(-(rows - 1.0 - steps_f) * rate), 0.0)
                scaled = (buf["k"][i, :, lanes].astype(jnp.float32) * to_end).astype(jnp.bfloat16)
                states[t, h] = dot_tn(scaled, buf["v"][i, :, lanes]).astype(jnp.bfloat16)
            return carry

        lax.fori_loop(0, 4, pair, 0)
        for name in ("k", "v", "kp"):
            save(name).start()

    def send_states():
        for d in range(3):
            state_copy(d, t).start()

    def sum_states():
        for d in range(3):
            state_copy(d, (t + 3 - d) % 4).wait_recv()
        before = scalar_segment(first - 1, ends)

        def head(h, carry):
            rate = rate_of(h)[:, :HEAD_DIM]
            result = jnp.zeros((HEAD_DIM, HEAD_DIM), jnp.float32)
            for j in range(3):
                reach = jnp.where(
                    (j < t) & (scalar_segment(j * rows + rows - 1, ends) == before), 1.0, 0.0
                )
                distance = jnp.maximum(t - j - 1, 0).astype(jnp.float32) * rows
                weight = reach * jnp.exp(-rate * distance)
                result = result + weight * states[j, h].astype(jnp.float32)
            buf["st"][h] = result.astype(jnp.bfloat16)
            return carry

        lax.fori_loop(0, 8, head, 0)
        save("st").start()
        for name in ("q", "qp", "up"):
            save(name).start()

    def attend(h, carry):
        before = scalar_segment(first - 1, ends)
        half = rows // 2
        i = h // 2
        lanes = pl.ds(pl.multiple_of(lax.rem(h, 2) * HEAD_DIM, HEAD_DIM), HEAD_DIM)
        columns = pl.ds(pl.multiple_of(h * HEAD_DIM, HEAD_DIM), HEAD_DIM)
        rate = rate_of(h)
        for b in range(2):
            mine = slice(b * half, (b + 1) * half)
            keys = (b + 1) * half
            query = buf["q"][i, mine, lanes]
            scores = dot_nt(query, buf["k"][i, :keys, lanes])
            decay = jnp.exp(-span[mine, :keys] * rate[:, :keys])
            weights = (scores * decay).astype(jnp.bfloat16)
            into = jnp.where(
                segments[mine] == before,
                jnp.exp(-(steps_f[mine] + 1.0) * rate[:, :HEAD_DIM]),
                0.0,
            )
            attn = dot(weights, buf["v"][i, :keys, lanes]) + into * dot(query, buf["st"][h])
            buf["o"][mine, columns] = attn
            normed = attn * rms_scale(attn, head_floor)
            mixed[mine, columns] = (normed * buf["y1"][mine, columns]).astype(jnp.bfloat16)
        return carry

    def attend_pairs(lo, hi):
        return lambda: (lax.fori_loop(2 * lo, 2 * hi, attend, 0), None)[1]

    def mix():
        save("o").start()
        for i in range(4):
            columns = slice(i * 2 * HEAD_DIM, (i + 1) * 2 * HEAD_DIM)
            buf["wt"][i] = mixed[:, columns].T
        save("wt").start()
        arrived(4)

        def block(i, carry):
            sides = [full[4][i // 2, i % 2, s].reshape(n1.shape[1], HEAD_DIM) for s in range(2)]
            columns = pl.ds(pl.multiple_of(i * 2 * HEAD_DIM, 2 * HEAD_DIM), 2 * HEAD_DIM)
            buf["y1"][:, columns] = inp["tokens"][:, columns].astype(jnp.float32) + dot(
                mixed[...], jnp.concatenate(sides, axis=1)
            )
            return carry

        lax.fori_loop(0, 4, block, 0)
        values = buf["y1"][...]
        n2[...] = (values * rms_scale(values)).astype(jnp.bfloat16)
        turn_rows(n2, buf["n2t"])
        save("y1").start()
        save("n2t").start()

    def turned_out(i):
        return pltpu.make_async_copy(hidden_turned.at[i % 2], a_out.at[i], turn_sem.at[i])

    def gate_up(i):
        def go():
            if i == 0:
                arrived(6)
            shape = (n1.shape[1], full[5].shape[5])

            def band(b, carry):
                mine = pl.ds(pl.multiple_of(b * rows // 2, rows // 2), rows // 2)
                gate = dot(n2[mine], full[5][:, :, :, i].reshape(shape))
                lift = dot(n2[mine], full[6][:, :, :, i].reshape(shape))
                hidden[i, mine] = (gate * lift).astype(jnp.bfloat16)
                buf["g"][i, mine] = gate.astype(jnp.bfloat16)
                buf["e"][i, mine] = lift.astype(jnp.bfloat16)
                return carry

            lax.fori_loop(0, 2, band, 0)
            if i >= 2:
                turned_out(i - 2).wait()
            hidden_turned[i % 2] = hidden[i].T
            turned_out(i).start()
            if i == 3:
                for name in ("g", "e"):
                    save(name).start()

        return go

    def close():
        arrived(7)

        def block(i, carry):
            columns = pl.ds(pl.multiple_of(i * 2 * HEAD_DIM, 2 * HEAD_DIM), 2 * HEAD_DIM)
            values = buf["y1"][:, columns]
            for j in range(4):
                sides = [full[7][i // 2, i % 2, s, j] for s in range(2)]
                values = values + dot(hidden[j], jnp.concatenate(sides, axis=1))
            buf["res"][:, columns] = values.astype(jnp.bfloat16)
            return carry

        lax.fori_loop(0, 4, block, 0)
        save("res").start()

    def after(name):
        stage, p, part = name
        size = shards[pieces[p][0]].size * 2 // len(ROUTES[pieces[p][0]])
        early = route_of(p) in "ab"

        def over_z():
            def send():
                for d in range(3):
                    z_copy(p, d, t).start()

            def receive():
                for d in range(3):
                    z_copy(p, d, (t + 3 - d) % 4).wait_recv()
                if early:
                    own_copy(p).wait()

            return ("z", (4 if early else 16) * size, send, receive, ("z", p, 0))

        def over_near(k):
            blocks = (4, 8)[k] if early else (1, 2)[k]
            link = "x" if (route_of(p) in "ac") == (k == 0) else "y"

            def receive():
                near_copy(p, k, True).wait_recv()
                if k == 0 and not early:
                    own_copy(p).wait()

            return (link, blocks * size, near_copy(p, k, False).start, receive, ("n", p, k))

        def over_core(k, blocks):
            def send():
                core_copy(p, k, False).start()

            return ("c", blocks * size // 4, send, lambda: None, ("c", p, k))

        if stage == "go":
            own_copy(p).start()
            return [over_z() if early else over_near(0)]
        if stage == "z":
            if early:
                return [over_near(0), over_core(0, 4)]
            return [over_core(k, 4) for k in (1, 2, 3)]
        if stage == "n":
            if part == 0:
                return [over_near(1)] + ([over_core(1, 4)] if early else [])
            return [over_core(2, 8)] if early else [over_z(), over_core(0, 4)]
        return []

    needs = set()
    steps = []

    def then(took, step, *weights):
        for p in range(total):
            if pieces[p][0] in weights:
                needs.update(("c", p, k) for k in core_parts(p))
        steps.append((took, step, set(needs), None))

    then(2.0, begin)
    then(0.2, rates_here)
    then(2.2, project(1, finish_key), 1)
    then(2.2, project(2, finish_value), 2)
    then(1.5, make_states)
    then(2.2, project(0, finish_query), 0)
    then(0.2, send_states)
    then(2.2, project(3, finish_update), 3)
    then(0.5, sum_states)
    for i in range(4):
        then(1.8, attend_pairs(i, i + 1))
    then(3.0, mix, 4)
    then(0.1, lambda: arrived(5), 5)
    for i in range(4):
        then(3.0, gate_up(i), 6)
    then(4.0, close, 7)
    arrange(steps, [("go", p, 0) for p in range(total)], after)
    for d in range(3):
        rate_copy(d, t).wait_send()
        state_copy(d, t).wait_send()
    for p in range(total):
        for d in range(3):
            z_copy(p, d, t).wait_send()
        for stage in range(2):
            near_copy(p, stage, False).wait_send()
        for part in core_parts(p):
            core_copy(p, part, False).wait_send()
    for w in range(N_W):
        keep(w).wait()
    for name in FWD_OUT:
        save(name).wait()
    for i in range(2, 4):
        turned_out(i).wait()


def forward(shards, tokens, cos, sin, lengths, rates):
    rows, width = tokens.shape
    units, depth = shards[5].shape
    heads = width // HEAD_DIM
    low, wide = jnp.bfloat16, jnp.float32
    by_pair = (4, rows, heads // 4 * HEAD_DIM)
    turned = (2, width // 2, rows)
    by_unit = (4, rows, units)
    shapes = {
        "res": ((rows, width), low),
        "qp": (by_pair, low),
        "kp": (by_pair, low),
        "up": (by_pair, low),
        "q": (by_pair, low),
        "k": (by_pair, low),
        "v": (by_pair, low),
        "o": ((rows, width), wide),
        "wt": ((4, width // 4, rows), low),
        "y1": ((rows, width), wide),
        "n1t": (turned, low),
        "n2t": (turned, low),
        "g": (by_unit, low),
        "e": (by_unit, low),
        "st": ((heads, HEAD_DIM, HEAD_DIM), low),
        "r8": ((8, rows), wide),
    }
    blocks = [(2, 2, 2, 4, *(s.shape[::-1] if i in (5, 6) else s.shape)) for i, s in enumerate(shards)]
    pieces = sum(len(route) for route in ROUTES)
    dma = pltpu.SemaphoreType.DMA
    in_vmem, in_smem = (pl.BlockSpec(memory_space=m) for m in (pltpu.VMEM, pltpu.SMEM))
    outs = pl.pallas_call(
        forward_kernel,
        name="gather_and_forward",
        out_shape=[jax.ShapeDtypeStruct(b, low) for b in blocks]
        + [jax.ShapeDtypeStruct((4, units, rows), low)]
        + [jax.ShapeDtypeStruct(*shapes[name]) for name in FWD_OUT],
        in_specs=[in_vmem] * (N_W + 3) + [in_smem] * 2,
        out_specs=[pl.BlockSpec(memory_space=pl.ANY)] * (N_W + 1 + len(FWD_OUT)),
        scratch_shapes=[
            *[pltpu.VMEM(b, low) for b in blocks],
            *[pltpu.VMEM(*shapes[name]) for name in FWD_OUT],
            pltpu.VMEM((rows, width), low),
            pltpu.VMEM(by_unit, low),
            pltpu.VMEM((2, units, rows), low),
            pltpu.VMEM((rows, rows), wide),
            pltpu.VMEM((4, heads, HEAD_DIM, HEAD_DIM), low),
            pltpu.VMEM((4, 8, rows), wide),
            pltpu.VMEM((depth, units), low),
            pltpu.VMEM((depth, units), low),
            dma((pieces,)),
            dma((pieces, 3)),
            dma((pieces, 3)),
            dma((pieces, 2)),
            dma((pieces, 2)),
            dma((pieces, 4)),
            dma((pieces, 4)),
            dma((3,)),
            dma((3,)),
            dma((3,)),
            dma((3,)),
            dma((N_W,)),
            dma((len(FWD_OUT),)),
            dma((4,)),
        ],
        compiler_params=pltpu.CompilerParams(
            collective_id=0, has_side_effects=True, vmem_limit_bytes=VMEM_BYTES
        ),
    )(*shards, tokens, cos, sin, lengths, rates)
    return outs[:N_W], outs[N_W], dict(zip(FWD_OUT, outs[N_W + 1 :]))


BWD_ANY = ("q", "k", "v", "up", "qp", "kp", "o", "wt", "y1", "n1t", "n2t", "g", "e")
BWD_VMEM = ("st", "r8", "cos", "sin")
BAND = 32
SUMS = ("ab", "ab", "ab", "ab", "ab", "cb", "ab", "ab")


def slope_of(values):
    sigma = jax.nn.sigmoid(values)
    return sigma * (1.0 + values * (1.0 - sigma))


def turn_back(values, cos, sin):
    return values * cos - pltpu.roll(values, HEAD_DIM // 2, 1) * sin


def backward_kernel(*refs):
    kept, refs = refs[:N_W], refs[N_W:]
    a_in, refs = refs[0], refs[1:]
    inp = dict(zip(BWD_ANY + BWD_VMEM, refs))
    refs = refs[len(BWD_ANY + BWD_VMEM) :]
    tokens, out_grad, lengths = refs[:3]
    grads, d_tokens = refs[3 : 3 + N_W], refs[3 + N_W]
    refs = refs[4 + N_W :]
    mine, from_near, from_far, from_z = (refs[i * N_W : (i + 1) * N_W] for i in range(4))
    refs = refs[4 * N_W :]
    tall, wide, turned_a, gq, ev, d_side, n_turned, rows_a, rows_b, tall_w, wide_w = refs[:11]
    q_pre, w_turned, span, states, back = refs[11:16]
    load_sem, tall_sem, wide_sem, c_send, c_recv, n_send, n_recv, z_send, z_recv = refs[16:25]
    s_send, s_recv, o_send, o_recv = refs[25:]
    rows, width = rows_a.shape
    half = rows // 2
    y, x, c, f, t = place()
    core, along_x, along_y, along_z = peers_of(f, t)
    all_ = slice(None)

    keys = {}

    def load(key, source, target):
        index = keys.setdefault(key, len(keys))
        return pltpu.make_async_copy(source, target, load_sem.at[index])

    def pair_columns(i):
        return slice(i * 2 * HEAD_DIM, (i + 1) * 2 * HEAD_DIM)

    def by_pairs(key, source, place_):
        return [load((key, i), source.at[:, pair_columns(i)], q_pre.at[place_, i]) for i in range(4)]

    lane_pair = [slice(0, 2 * HEAD_DIM), slice(2 * HEAD_DIM, 4 * HEAD_DIM)]
    loads = {
        "cot": by_pairs("cot", out_grad, 0),
        "tokens": by_pairs("tokens", tokens, 0),
        "a": [load("a", a_in, turned_a)],
        "g": [load("g", inp["g"], gq)],
        "e": [load("e", inp["e"], ev)],
        "n2": [load("n2", inp["n2t"], n_turned)],
        "n1": [load("n1", inp["n1t"], n_turned)],
        "y1": [load("y1", inp["y1"], rows_a)],
        "o": [load("o", inp["o"], rows_a)],
        "w": [load("w", inp["wt"], w_turned)],
        "qp": [load("qp", inp["qp"], q_pre.at[0])],
        "kp": [load("kp", inp["kp"], q_pre.at[1])],
        "q": [load("q", inp["q"], gq.at[:, :, lane_pair[0]])],
        "k": [load("k", inp["k"], gq.at[:, :, lane_pair[1]])],
        "v": [load("v", inp["v"], ev.at[:, :, lane_pair[0]])],
        "up": [load("up", inp["up"], turned_a.at[:, :rows, lane_pair[1]])],
        "out": [load("out", rows_b, d_tokens)],
    }

    def start(*names):
        for name in names:
            for copy in loads[name]:
                copy.start()

    def wait(*names):
        for name in names:
            for copy in loads[name]:
                copy.wait()

    def tile(w, i, slot):
        if w in (4, 7):
            depth = kept[w].shape[4]
            return pltpu.make_async_copy(
                kept[w].at[:, :, :, i], tall_w.at[slot, :, :, :, :depth], tall_sem.at[slot]
            )
        lanes = kept[w].shape[5]
        return pltpu.make_async_copy(
            kept[w].at[:, :, :, i], wide_w.at[slot, :, :, :, :, :lanes], wide_sem.at[slot]
        )

    def over_tiles(w, use, lo=0, hi=4):
        tile(w, lo, lo % 2).start()

        def step(i, carry):
            slot = lax.rem(i, 2)

            @pl.when(i < hi - 1)
            def _():
                tile(w, i + 1, 1 - slot).start()

            tile(w, i, slot).wait()
            use(i, slot)
            return carry

        lax.fori_loop(lo, hi, step, 0)

    pieces = [(w, h) for w in range(N_W) for h in range(2)]

    def remote(src, dst, send, recv, peer):
        return pltpu.make_async_remote_copy(
            src_ref=src, dst_ref=dst, send_sem=send, recv_sem=recv, device_id=peer, device_id_type=MESH
        )

    def rows_of(p):
        w, h = pieces[p]
        part = grads[w].shape[0] // 2
        return pl.ds(h * part, part)

    def ring_of(w):
        return (tall, 0) if w in (4, 7) else (wide, 1)

    def core_copy(w, i):
        ring, kind = ring_of(w)
        depth, lanes = grads[w].shape
        return remote(
            ring.at[lax.rem(i, 2), :, :, :depth, :lanes],
            mine[w].at[:, :, i],
            c_send.at[kind, lax.rem(i, 2)],
            c_recv.at[w, i],
            core,
        )

    def near_copy(p):
        (w, h), part = pieces[p], rows_of(p)
        src = mine[w].at[1 - y, :, :, part] if h == 0 else mine[w].at[:, 1 - x, :, part]
        return remote(
            src,
            from_near[w].at[:, :, part],
            n_send.at[p, 0],
            n_recv.at[p, 0],
            along_y if h == 0 else along_x,
        )

    def far_copy(p):
        (w, h), part = pieces[p], rows_of(p)
        src = mine[w].at[y, 1 - x, :, part] if h == 0 else mine[w].at[1 - y, x, :, part]
        return remote(
            src,
            from_far[w].at[:, part],
            n_send.at[p, 1],
            n_recv.at[p, 1],
            along_x if h == 0 else along_y,
        )

    def z_copy(p, d):
        w, part = pieces[p][0], rows_of(p)
        return remote(
            mine[w].at[y, x, (t + d + 1) % 4, part],
            from_z[w].at[d, part],
            z_send.at[p, d],
            z_recv.at[p, d],
            along_z[d],
        )

    def far_first(p, d, a, source):
        w, part = pieces[p][0], rows_of(p)
        dst = from_near[w].at[d, 2 * a : 2 * a + 2] if d < 2 else from_far[w].at[2 * a : 2 * a + 2]
        return remote(
            mine[w].at[a, :, source, part],
            dst.at[:, part],
            o_send.at[2 * d + a],
            o_recv.at[2 * d + a],
            along_z[d],
        )

    def then_near(p, k):
        w, part = pieces[p][0], rows_of(p)
        if k == 0:
            src, dst = mine[w].at[1 - y, :, t, part], from_z[w].at[0:2, part]
        else:
            src, dst = mine[w].at[y, 1 - x, t, part], from_z[w].at[2, part]
        return remote(src, dst, o_send.at[6 + k], o_recv.at[6 + k], (along_y, along_x)[k])

    def plus(into, *terms):
        total = into[...].astype(jnp.float32)
        for term in terms:
            total = total + term[...].astype(jnp.float32)
        return total

    def add(steps, target, other):
        def step(i, carry):
            into, term = target(i), other(i)
            into[...] = (into[...].astype(jnp.float32) + term[...].astype(jnp.float32)).astype(
                jnp.bfloat16
            )
            return carry

        lax.fori_loop(0, steps, step, 0)

    def after_near(p):
        (w, h), part = pieces[p], rows_of(p)
        near_copy(p).wait_recv()
        if h == 0:
            into = lambda i: mine[w].at[y, i // 4, i % 4, part]
        else:
            into = lambda i: mine[w].at[i // 4, x, i % 4, part]
        add(8, into, lambda i: from_near[w].at[i // 4, i % 4, part])

    def after_far(p):
        w, part = pieces[p][0], rows_of(p)
        far_copy(p).wait_recv()
        add(4, lambda i: mine[w].at[y, x, i, part], lambda i: from_far[w].at[i, part])

    def after_z(p):
        w, part = pieces[p][0], rows_of(p)
        for d in range(3):
            z_copy(p, d).wait_recv()
        result = mine[w][y, x, t, part].astype(jnp.float32)
        for d in range(3):
            result = result + from_z[w][d, part].astype(jnp.float32)
        grads[w][part] = result

    used = {0: None, 1: None}

    def gradient(w, own, value):
        ring, kind = ring_of(w)
        depth, lanes = grads[w].shape

        def blocks(i):
            for q in range(2):
                result = value(i, (c if own else 1 - c), slice(2 * q * HEAD_DIM, (2 * q + 2) * HEAD_DIM))
                for b in range(2):
                    if kind == 1:
                        yield q, b, result[b * depth : (b + 1) * depth]
                    else:
                        yield q, b, result[:, b * lanes : (b + 1) * lanes]

        def run():
            if not own:
                before = used[kind]
                used[kind] = w

                def step(i, carry):
                    if before is not None:

                        @pl.when(i < 2)
                        def _():
                            core_copy(before, i + 2).wait_send()

                    @pl.when(i >= 2)
                    def _():
                        core_copy(w, i - 2).wait_send()

                    slot = lax.rem(i, 2)
                    for a, b, part in blocks(i):
                        ring[slot, a, b, :depth, :lanes] = part.astype(jnp.bfloat16)
                    core_copy(w, i).start()
                    return carry

                lax.fori_loop(0, 4, step, 0)
            else:

                def step(i, carry):
                    core_copy(w, i).wait_recv()
                    for a, b, part in blocks(i):
                        mine[w][a, b, i] = (mine[w][a, b, i].astype(jnp.float32) + part).astype(
                            jnp.bfloat16
                        )
                    return carry

                lax.fori_loop(0, 4, step, 0)

        return run

    ends, first, offsets, segments = row_tables(lengths, t, rows)
    steps_f = offsets.astype(jnp.float32)
    seg_before = scalar_segment(first - 1, ends)
    seg_after = scalar_segment(first + rows, ends)
    seg_first = scalar_segment(first, ends)

    def lanes_of(j, base=0):
        return slice(base + j * HEAD_DIM, base + (j + 1) * HEAD_DIM)

    def rate_of(h):
        return inp["r8"][pl.ds(h, 1), :]

    def over_rows(use):
        def step(i, carry):
            use(pl.ds(pl.multiple_of(i * BAND, BAND), BAND))
            return carry

        lax.fori_loop(0, rows // BAND, step, 0)

    def begin():
        start("cot", "a", "e", "g", "n2", "y1", "w")
        fill_span(span, ends, first)
        live = jnp.where(segments < SLOTS - 1, 1.0, 0.0)
        wait("cot")
        for i in range(4):
            for s in range(2):
                part = q_pre[0, i, :, lanes_of(s)].astype(jnp.float32) * live
                d_side[s, :, lanes_of(i)] = part.astype(jnp.bfloat16)
        start("qp", "kp")
        wait("a")

    def expand(lo, hi):
        def use(i, slot):
            def band(b, carry):
                part = pl.ds(pl.multiple_of(b * half, half), half)
                d_hidden = sum(
                    dot_nt(
                        d_side[s, part],
                        jnp.concatenate([tall_w[slot, j // 2, j % 2, s] for j in range(4)], axis=1),
                    )
                    for s in range(2)
                )
                lift, gate = ev[i, part].astype(jnp.float32), gq[i, part].astype(jnp.float32)
                ev[i, part] = (d_hidden * lift).astype(jnp.bfloat16)
                gq[i, part] = (d_hidden * gate).astype(jnp.bfloat16)
                return carry

            lax.fori_loop(0, 2, band, 0)

        def run():
            if lo == 0:
                wait("e", "g")
            over_tiles(7, use, lo, hi)
            if hi == 4:
                wait("n2")

        return run

    def through(w, source, target, clear):
        def run():
            if clear:
                target[...] = jnp.zeros_like(target)
            lanes = kept[w].shape[5]

            def use(i, slot):
                for j in range(4):
                    part = wide_w[slot, j // 2, j % 2, :, :, :lanes].reshape(2 * HEAD_DIM, lanes)
                    target[:, pair_columns(j)] += dot_nt(source(i), part)

            over_tiles(w, use)

        return run

    def middle_back():
        start("v", "q", "k")
        wait("y1")

        def use(part):
            values = rows_a[part, :]
            cot = jnp.concatenate(
                [d_side[j % 2, part, lanes_of(j // 2)].astype(jnp.float32) for j in range(8)], axis=1
            )
            result = cot + norm_back(values, rms_scale(values), rows_b[part, :])
            rows_b[part, :] = result
            for j in range(8):
                d_side[j % 2, part, lanes_of(j // 2)] = result[:, lanes_of(j)].astype(jnp.bfloat16)

        over_rows(use)
        start("o")
        wait("w")

    def mixed_back():
        wait("o", "up")

        def use(i, slot):
            def band(b, carry):
                part = pl.ds(pl.multiple_of(b * half, half), half)
                d_mixed = sum(
                    dot_nt(
                        d_side[s, part],
                        jnp.concatenate(
                            [tall_w[slot, j // 2, j % 2, s, : 2 * HEAD_DIM] for j in range(4)], axis=1
                        ),
                    )
                    for s in range(2)
                )
                for j in range(2):
                    columns = pl.ds(pl.multiple_of((2 * i + j) * HEAD_DIM, HEAD_DIM), HEAD_DIM)
                    attn = rows_a[part, columns]
                    scale = rms_scale(attn, head_floor)
                    normed = attn * scale
                    pre = turned_a[i, part, lanes_of(j, 2 * HEAD_DIM)].astype(jnp.float32)
                    grad_ = d_mixed[:, lanes_of(j)]
                    turned_a[i, part, lanes_of(j)] = (grad_ * normed * slope_of(pre)).astype(
                        jnp.bfloat16
                    )
                    d_attn = norm_back(attn, scale, grad_ * swish_of(pre))
                    ev[i, part, lanes_of(j, 2 * HEAD_DIM)] = d_attn.astype(jnp.bfloat16)
                return carry

            lax.fori_loop(0, 2, band, 0)

        over_tiles(4, use)
        wait("n1", "q")

    def make_states():
        def pair(i, carry):
            for j in range(2):
                rate = rate_of(2 * i + j)[:, :HEAD_DIM]
                from_start = jnp.where(segments == seg_first, jnp.exp(-steps_f * rate), 0.0)
                scaled = (gq[i, :, lanes_of(j)].astype(jnp.float32) * from_start).astype(jnp.bfloat16)
                states[t, 2 * i + j] = dot_tn(scaled, ev[i, :, lanes_of(j, 2 * HEAD_DIM)]).astype(
                    jnp.bfloat16
                )
            return carry

        lax.fori_loop(0, 4, pair, 0)

    def state_copy(d, source):
        ref = states.at[source]
        return remote(ref, ref, s_send.at[d], s_recv.at[d], along_z[d])

    def send_states():
        for d in range(3):
            state_copy(d, t).start()

    def sum_states():
        wait("v", "k", "qp", "kp")
        for d in range(3):
            state_copy(d, (t + 3 - d) % 4).wait_recv()

        def head(h, carry):
            rate = rate_of(h)[:, :HEAD_DIM]
            result = jnp.zeros((HEAD_DIM, HEAD_DIM), jnp.float32)
            for j in range(1, 4):
                reach = jnp.where((j > t) & (scalar_segment(j * rows, ends) == seg_after), 1.0, 0.0)
                distance = jnp.maximum(j - t - 1, 0).astype(jnp.float32) * rows
                weight = reach * jnp.exp(-rate * distance)
                result = result + weight * states[j, h].astype(jnp.float32)
            back[h] = result.astype(jnp.bfloat16)
            return carry

        lax.fori_loop(0, 8, head, 0)

    def attend_back(h, carry):
        cos, sin = inp["cos"][...], inp["sin"][...]
        i, j = h // 2, lax.rem(h, 2)
        low_lanes = pl.ds(pl.multiple_of(j * HEAD_DIM, HEAD_DIM), HEAD_DIM)
        high_lanes = pl.ds(pl.multiple_of((2 + j) * HEAD_DIM, HEAD_DIM), HEAD_DIM)
        rate = rate_of(h)
        short = rate[:, :HEAD_DIM]
        key, value = gq[i, :, high_lanes], ev[i, :, low_lanes]
        state_in, state_back = inp["st"][h], back[h]
        out_of = jnp.where(segments == seg_after, jnp.exp(-(rows - steps_f) * short), 0.0)
        d_value = out_of * dot(key, state_back)
        d_key = out_of * dot_nt(value, state_back)
        d_query = []
        for b in range(2):
            part = slice(b * half, (b + 1) * half)
            keys = (b + 1) * half
            query = gq[i, part, low_lanes]
            grad = ev[i, part, high_lanes]
            decay = jnp.exp(-span[part, :keys] * rate[:, :keys])
            weights = (dot_nt(query, key[:keys]) * decay).astype(jnp.bfloat16)
            d_raw = (dot_nt(grad, value[:keys]) * decay).astype(jnp.bfloat16)
            into = jnp.where(
                segments[part] == seg_before, jnp.exp(-(steps_f[part] + 1.0) * short), 0.0
            )
            d_query.append(dot(d_raw, key[:keys]) + into * dot_nt(grad, state_in))
            add_value, add_key = dot_tn(weights, grad), dot_tn(d_raw, query)
            if b == 0:
                d_value = jnp.concatenate([d_value[:half] + add_value, d_value[half:]], axis=0)
                d_key = jnp.concatenate([d_key[:half] + add_key, d_key[half:]], axis=0)
            else:
                d_value, d_key = d_value + add_value, d_key + add_key
        d_query = jnp.concatenate(d_query, axis=0)
        pre_query = q_pre[0, i, :, low_lanes].astype(jnp.float32)
        pre_key = q_pre[1, i, :, low_lanes].astype(jnp.float32)
        gq[i, :, low_lanes] = (slope_of(pre_query) * turn_back(d_query, cos, sin)).astype(
            jnp.bfloat16
        )
        gq[i, :, high_lanes] = (
            slope_of(pre_key) * turn_back(d_key, cos, sin)
        ).astype(jnp.bfloat16)
        ev[i, :, low_lanes] = d_value.astype(jnp.bfloat16)
        return carry

    def close():
        wait("tokens")

        def use(part):
            values = jnp.concatenate([q_pre[0, i, part, :] for i in range(4)], axis=1)
            values = values.astype(jnp.float32)
            rows_b[part, :] += norm_back(values, rms_scale(values), rows_a[part, :])

        over_rows(use)
        start("out")

    low_pair, high_pair = slice(0, 2 * HEAD_DIM), slice(2 * HEAD_DIM, 4 * HEAD_DIM)
    sources = {
        0: lambda i: gq[i, :, low_pair],
        1: lambda i: gq[i, :, high_pair],
        2: lambda i: ev[i, :, low_pair],
        3: lambda i: turned_a[i, :rows, low_pair],
        5: lambda i: ev[i],
        6: lambda i: gq[i],
    }

    def grad(w, own):
        if w == 7:
            value = lambda i, s, half_: dot(turned_a[i], d_side[s, :, half_])
        elif w == 4:
            value = lambda i, s, half_: dot(w_turned[i], d_side[s, :, half_])
        else:
            value = lambda i, s, half_: dot(n_turned[s, half_], sources[w](i))
        return gradient(w, own, value)

    def attend_pairs(lo, hi):
        return lambda: (lax.fori_loop(2 * lo, 2 * hi, attend_back, 0), None)[1]

    work = [
        (3.0, begin, None),
        (2.5, grad(7, False), None),
        (3.0, expand(0, 2), None),
        (3.0, grad(7, True), 7),
        (3.0, expand(2, 4), None),
        (2.5, grad(5, False), None),
        (0.1, lambda: start("up"), None),
        (2.5, grad(6, False), None),
        (3.0, grad(5, True), 5),
        (3.0, grad(6, True), 6),
        (0.1, lambda: start("n1"), None),
        (5.0, through(5, sources[5], rows_b, True), None),
        (5.0, through(6, sources[6], rows_b, False), None),
        (3.0, middle_back, None),
        (1.0, grad(4, False), None),
        (6.0, mixed_back, None),
        (1.0, grad(3, False), None),
        (1.2, grad(4, True), 4),
        (2.0, make_states, None),
        (1.2, grad(3, True), 3),
        (0.1, send_states, None),
        (2.0, through(3, sources[3], rows_a, True), None),
        (1.0, sum_states, None),
        (4.0, attend_pairs(0, 1), None),
        (4.0, attend_pairs(1, 2), None),
        (4.0, attend_pairs(2, 3), None),
        (4.0, attend_pairs(3, 4), None),
        (1.0, grad(2, False), None),
        (1.0, grad(0, False), None),
        (1.0, grad(1, False), None),
        (1.2, grad(2, True), 2),
        (1.2, grad(0, True), 0),
        (1.2, grad(1, True), 1),
        (0.1, lambda: start("tokens"), None),
        (2.0, through(2, sources[2], rows_a, False), None),
        (2.0, through(0, sources[0], rows_a, False), None),
        (2.0, through(1, sources[1], rows_a, False), None),
        (2.0, close, None),
    ]
    meet([core, along_x, along_y, *along_z])

    def after(name):
        stage, p = name
        if stage == "grad":
            return [first_send(2 * p + h) for h in range(2)]
        (w, h), part = pieces[p], rows_of(p)
        size = grads[w].size
        route = SUMS[w][h]
        if stage == "near":
            link = "x" if route == "a" else "y"
            return [(link, 4 * size, far_copy(p).start, lambda: after_far(p), ("far", p))]
        if stage == "far":

            def send():
                for d in range(3):
                    z_copy(p, d).start()

            return [("z", 4 * size, send, lambda: after_z(p), ("z", p))]
        if stage == "c0":

            def receive_y():
                then_near(p, 0).wait_recv()
                for b in range(2):
                    into = mine[w].at[y, b, t, part]
                    into[...] = plus(into, from_z[w].at[b, part]).astype(jnp.bfloat16)

            return [("y", 2 * size, then_near(p, 0).start, receive_y, ("c1", p))]
        if stage == "c1":

            def receive_x():
                then_near(p, 1).wait_recv()
                grads[w][part] = plus(mine[w].at[y, x, t, part], from_z[w].at[2, part])

            return [("x", size, then_near(p, 1).start, receive_x, ("c2", p))]
        return []

    def first_send(p):
        (w, h), part = pieces[p], rows_of(p)
        size = grads[w].size
        if SUMS[w][h] == "c":

            def send():
                for d in range(3):
                    for a in range(2):
                        far_first(p, d, a, (t + d + 1) % 4).start()

            def receive():
                for d in range(3):
                    for a in range(2):
                        far_first(p, d, a, (t + d + 1) % 4).wait_recv()
                for i in range(4):
                    into = mine[w].at[i // 2, i % 2, t, part]
                    into[...] = plus(
                        into,
                        from_near[w].at[0, i, part],
                        from_near[w].at[1, i, part],
                        from_far[w].at[i, part],
                    ).astype(jnp.bfloat16)

            return ("z", 16 * size, send, receive, ("c0", p))
        link = "y" if SUMS[w][h] == "a" else "x"
        return (link, 8 * size, near_copy(p).start, lambda: after_near(p), ("near", p))

    arrange(
        [(took, run, set(), None if done is None else ("grad", done)) for took, run, done in work],
        [],
        after,
    )
    for kind in range(2):
        for i in range(2, 4):
            core_copy(used[kind], i).wait_send()
    for p in range(len(pieces)):
        if SUMS[pieces[p][0]][pieces[p][1]] == "c":
            for d in range(3):
                for a in range(2):
                    far_first(p, d, a, (t + d + 1) % 4).wait_send()
            then_near(p, 0).wait_send()
            then_near(p, 1).wait_send()
        else:
            near_copy(p).wait_send()
            far_copy(p).wait_send()
            for d in range(3):
                z_copy(p, d).wait_send()
    for d in range(3):
        state_copy(d, t).wait_send()
    wait("out")


def backward(kept, a_turned, saved, cos, sin, tokens, out_grad, lengths):
    rows, width = tokens.shape
    low, wide = jnp.bfloat16, jnp.float32
    units = a_turned.shape[1]
    pair = width // 4
    shards = [w.shape[4:] for w in kept]
    dma = pltpu.SemaphoreType.DMA
    anywhere, in_vmem, in_smem = (
        pl.BlockSpec(memory_space=m) for m in (pl.ANY, pltpu.VMEM, pltpu.SMEM)
    )
    pieces = 2 * N_W

    def buffers(*lead):
        return [pltpu.VMEM((*lead, *s), low) for s in shards]

    outs = pl.pallas_call(
        backward_kernel,
        name="backward_and_scatter",
        out_shape=[jax.ShapeDtypeStruct(s, wide) for s in shards]
        + [jax.ShapeDtypeStruct((rows, width), wide)],
        in_specs=[anywhere] * (N_W + 1 + len(BWD_ANY))
        + [in_vmem] * len(BWD_VMEM)
        + [anywhere, anywhere, in_smem],
        out_specs=[in_vmem] * N_W + [anywhere],
        scratch_shapes=[
            *buffers(2, 2, 4),
            *buffers(2, 4),
            *buffers(4),
            *buffers(3),
            pltpu.VMEM((2, 2, 2, units, HEAD_DIM), low),
            pltpu.VMEM((2, 2, 2, HEAD_DIM, units), low),
            pltpu.VMEM((4, units, rows), low),
            pltpu.VMEM((4, rows, units), low),
            pltpu.VMEM((4, rows, units), low),
            pltpu.VMEM((2, rows, width // 2), low),
            pltpu.VMEM((2, width // 2, rows), low),
            pltpu.VMEM((rows, width), wide),
            pltpu.VMEM((rows, width), wide),
            pltpu.VMEM((2, 2, 2, 2, units, HEAD_DIM), low),
            pltpu.VMEM((2, 2, 2, 2, HEAD_DIM, units), low),
            pltpu.VMEM((2, 4, rows, pair), low),
            pltpu.VMEM((4, pair, rows), low),
            pltpu.VMEM((rows, rows), wide),
            pltpu.VMEM((4, width // HEAD_DIM, HEAD_DIM, HEAD_DIM), low),
            pltpu.VMEM((width // HEAD_DIM, HEAD_DIM, HEAD_DIM), low),
            dma((24,)),
            dma((2,)),
            dma((2,)),
            dma((2, 2)),
            dma((N_W, 4)),
            dma((pieces, 2)),
            dma((pieces, 2)),
            dma((pieces, 3)),
            dma((pieces, 3)),
            dma((3,)),
            dma((3,)),
            dma((8,)),
            dma((8,)),
        ],
        compiler_params=pltpu.CompilerParams(
            collective_id=1, has_side_effects=True, vmem_limit_bytes=VMEM_BYTES
        ),
    )(
        *kept,
        a_turned,
        *[saved[name] for name in BWD_ANY],
        saved["st"],
        saved["r8"],
        cos,
        sin,
        tokens,
        out_grad,
        lengths,
    )
    return outs[:N_W], outs[N_W]


def hand_out_kernel(turned, *refs):
    count = (len(refs) - 2 - len(turned)) // 3
    ins, outs, bufs = (refs[i * count : (i + 1) * count] for i in range(3))
    flipped, (load_sem, store_sem) = refs[3 * count : -2], refs[-2:]
    loads = [pltpu.make_async_copy(ins[i], bufs[i], load_sem.at[i]) for i in range(count)]
    order = [*turned, *(i for i in range(count) if i not in turned)]
    stores = []
    for i in order:
        loads[i].start()
    for i in order:
        loads[i].wait()
        source = bufs[i]
        if i in turned:
            source = flipped[turned.index(i)]
            source[...] = bufs[i][...].T
        stores.append(pltpu.make_async_copy(source, outs[i], store_sem.at[i]))
        stores[-1].start()
    for store in stores:
        store.wait()


def hand_out(arrays, turned):
    anywhere = pl.BlockSpec(memory_space=pl.ANY)
    shapes = [a.shape[::-1] if i in turned else a.shape for i, a in enumerate(arrays)]
    outs = pl.pallas_call(
        functools.partial(hand_out_kernel, turned),
        name="hand_out",
        out_shape=[jax.ShapeDtypeStruct(s, a.dtype) for s, a in zip(shapes, arrays)],
        in_specs=[anywhere] * len(arrays),
        out_specs=[anywhere] * len(arrays),
        scratch_shapes=[
            *[pltpu.VMEM(a.shape, a.dtype) for a in arrays],
            *[pltpu.VMEM(shapes[i], arrays[i].dtype) for i in turned],
            pltpu.SemaphoreType.DMA((len(arrays),)),
            pltpu.SemaphoreType.DMA((len(arrays),)),
        ],
    )(*arrays)
    return [out.T if i in turned else out for i, out in enumerate(outs)]


def body_by_kernels(
    tokens,
    lengths,
    rates,
    w_query,
    w_key,
    w_value,
    w_update,
    w_output,
    w_gate,
    w_up,
    w_down,
    out_grad,
):
    rows = tokens.shape[0]
    ends = jnp.cumsum(lengths[0], dtype=jnp.int32)
    places = lax.axis_index("tp") * rows + jnp.arange(rows, dtype=jnp.int32)
    segments = segment_of(places, ends)
    slots = jnp.arange(SLOTS, dtype=jnp.int32)
    starts = jnp.sum(jnp.where(segments[:, None] == slots, ends - lengths[0], 0), axis=1)
    positions = (places - starts).astype(jnp.float32)
    frequency = 10000.0 ** (-2.0 * jnp.arange(HEAD_DIM // 2, dtype=jnp.float32) / HEAD_DIM)
    turned = positions[:, None] * frequency[None, :]
    cos_half, sin_half = jnp.cos(turned), jnp.sin(turned)
    cos = jnp.concatenate([cos_half, cos_half], axis=1)
    sin = jnp.concatenate([-sin_half, sin_half], axis=1)
    shards = (w_query, w_key, w_value, w_update, w_output, w_gate.T, w_up.T, w_down)
    kept, a_turned, saved = forward(shards, tokens, cos, sin, lengths, rates)
    grads, d_tokens = backward(kept, a_turned, saved, cos, sin, tokens, out_grad, lengths)
    return tuple(hand_out([saved["res"], d_tokens, *grads], (7, 8)))


def body(
    tokens,
    lengths,
    rates,
    w_query,
    w_key,
    w_value,
    w_update,
    w_output,
    w_gate,
    w_up,
    w_down,
    out_grad,
):
    tp_count = lax.axis_size("tp")
    tp_index = lax.axis_index("tp")
    rows, width = tokens.shape
    head_width = HEAD_DIM
    all_rates = lax.all_gather(rates, "tp", axis=0, tiled=True)
    heads = all_rates.shape[0]
    ends = jnp.cumsum(lengths[0], dtype=jnp.int32)
    first = tp_index * rows
    places = first + jnp.arange(rows, dtype=jnp.int32)
    segments = segment_of(places, ends)
    starts = ends - lengths[0]
    slots = jnp.arange(SLOTS, dtype=jnp.int32)
    positions = (
        places - jnp.sum(jnp.where(segments[:, None] == slots, starts, 0), axis=1)
    ).astype(jnp.float32)
    live = (segments < SLOTS - 1).astype(jnp.float32)
    frequency = 10000.0 ** (-2.0 * jnp.arange(head_width // 2, dtype=jnp.float32) / head_width)
    turned = positions[:, None] * frequency[None, :]
    cos_table, sin_table = jnp.cos(turned)[:, None, :], jnp.sin(turned)[:, None, :]

    gaps = places[:, None] - places[None, :]
    allowed = (segments[:, None] == segments[None, :]) & (gaps >= 0)
    spans = jnp.maximum(gaps, 0).astype(jnp.float32)
    decay = jnp.where(
        allowed[None], jnp.exp(-all_rates[:, None, None] * spans[None]), 0.0
    )
    blocks = jnp.arange(tp_count, dtype=jnp.int32)
    seg_before = segment_of(first - 1, ends)
    seg_after = segment_of(first + rows, ends)
    seg_last = segment_of(blocks * rows + rows - 1, ends)
    seg_first = segment_of(blocks * rows, ends)
    offsets = jnp.arange(rows, dtype=jnp.float32)

    def row_decay(distance, mask):
        return jnp.where(mask[:, None], jnp.exp(-distance[:, None] * all_rates[None]), 0.0)[
            :, :, None
        ]

    to_end = row_decay(rows - 1 - offsets, segments == segments[rows - 1])
    from_start = row_decay(offsets, segments == segments[0])
    into = row_decay(offsets + 1.0, segments == seg_before)
    out_of = row_decay(rows - offsets, segments == seg_after)

    def block_weights(mask, distance):
        distance = jnp.maximum(distance, 0).astype(jnp.float32)
        return jnp.where(mask[:, None], jnp.exp(-distance[:, None] * all_rates[None]), 0.0)

    before_weights = block_weights(
        (blocks < tp_index) & (seg_last == seg_before), (tp_index - blocks - 1) * rows
    )
    after_weights = block_weights(
        (blocks > tp_index) & (seg_first == seg_after), (blocks - tp_index - 1) * rows
    )

    tokens_f = tokens.astype(jnp.float32)
    scale1 = rms_scale(tokens_f)
    normed1 = (tokens_f * scale1).astype(jnp.bfloat16)
    shards = (w_query, w_key, w_value, w_update, w_output, w_gate, w_up, w_down)
    inner = (True, True, True, True, False, True, True, False)
    full = [
        gather_full(w, "fsdp", "tp") if rows_first else gather_full(w, "tp", "fsdp")
        for w, rows_first in zip(shards, inner)
    ]
    (
        query_full,
        key_full,
        value_full,
        update_full,
        output_full,
        gate_full,
        up_full,
        down_full,
    ) = full
    shape_heads = (rows, heads, head_width)
    query_pre = mm(normed1, query_full)
    key_pre = mm(normed1, key_full)
    value_rows = mm(normed1, value_full).astype(jnp.bfloat16).reshape(shape_heads)
    update_pre = mm(normed1, update_full)
    query = rotate(swish(query_pre).reshape(shape_heads), cos_table, sin_table).astype(jnp.bfloat16)
    key_rows = rotate(swish(key_pre).reshape(shape_heads), cos_table, sin_table).astype(
        jnp.bfloat16
    )
    update = swish(update_pre)
    key_state = heads_dot(
        "shc,shd->hcd", (key_rows * to_end).astype(jnp.bfloat16), value_rows
    ).astype(jnp.bfloat16)
    key_states = lax.all_gather(key_state, "tp", axis=0, tiled=False)
    state_in = jnp.sum(
        key_states.astype(jnp.float32) * before_weights[:, :, None, None], axis=0
    ).astype(jnp.bfloat16)
    weights = (heads_dot("thc,shc->hts", query, key_rows) * decay).astype(jnp.bfloat16)
    attn = heads_dot("hts,shd->thd", weights, value_rows) + into * heads_dot(
        "thc,hcd->thd", query, state_in
    )
    scale_attn = rms_scale(attn, head_floor)
    normed_attn = (attn * scale_attn).reshape(rows, width)
    mixed = (normed_attn * update).astype(jnp.bfloat16)
    middle = tokens_f + mm(mixed, output_full)
    scale2 = rms_scale(middle)
    normed2 = (middle * scale2).astype(jnp.bfloat16)
    gate_rows = mm(normed2, gate_full)
    up_rows = mm(normed2, up_full)
    hidden = (gate_rows * up_rows).astype(jnp.bfloat16)
    result = (middle + mm(hidden, down_full)).astype(jnp.bfloat16)

    cotangent = out_grad.astype(jnp.float32) * live[:, None]
    cot_rows = cotangent.astype(jnp.bfloat16)
    grad_down = mm_inner(hidden, cot_rows)
    d_hidden = mm_trans(cot_rows, down_full)
    d_gate = (d_hidden * up_rows).astype(jnp.bfloat16)
    d_up = (d_hidden * gate_rows).astype(jnp.bfloat16)
    grad_gate = mm_inner(normed2, d_gate)
    grad_up = mm_inner(normed2, d_up)
    d_normed2 = mm_trans(d_gate, gate_full) + mm_trans(d_up, up_full)
    d_middle = cotangent + norm_back(middle, scale2, d_normed2)
    mid_rows = d_middle.astype(jnp.bfloat16)
    d_mixed = mm_trans(mid_rows, output_full)
    grad_output = mm_inner(mixed, mid_rows)
    d_update_pre = (d_mixed * normed_attn * swish_slope(update_pre)).astype(jnp.bfloat16)
    d_attn = norm_back(attn, scale_attn, (d_mixed * update).reshape(shape_heads)).astype(
        jnp.bfloat16
    )
    query_state = heads_dot(
        "thc,thd->hcd", (query * from_start).astype(jnp.bfloat16), d_attn
    ).astype(jnp.bfloat16)
    query_states = lax.all_gather(query_state, "tp", axis=0, tiled=False)
    state_back = jnp.sum(
        query_states.astype(jnp.float32) * after_weights[:, :, None, None], axis=0
    ).astype(jnp.bfloat16)
    d_raw = (heads_dot("thd,shd->hts", d_attn, value_rows) * decay).astype(jnp.bfloat16)
    d_value = heads_dot("hts,thd->shd", weights, d_attn) + out_of * heads_dot(
        "shc,hcd->shd", key_rows, state_back
    )
    d_query = heads_dot("hts,shc->thc", d_raw, key_rows) + into * heads_dot(
        "thd,hcd->thc", d_attn, state_in
    )
    d_key = heads_dot("hts,thc->shc", d_raw, query) + out_of * heads_dot(
        "shd,hcd->shc", value_rows, state_back
    )
    d_query_pre = (
        swish_slope(query_pre) * rotate_back(d_query, cos_table, sin_table).reshape(rows, width)
    ).astype(jnp.bfloat16)
    d_key_pre = (
        swish_slope(key_pre) * rotate_back(d_key, cos_table, sin_table).reshape(rows, width)
    ).astype(jnp.bfloat16)
    d_value_pre = d_value.reshape(rows, width).astype(jnp.bfloat16)
    grads = [mm_inner(normed1, d) for d in (d_query_pre, d_key_pre, d_value_pre, d_update_pre)]
    d_normed1 = (
        mm_trans(d_query_pre, query_full)
        + mm_trans(d_key_pre, key_full)
        + mm_trans(d_value_pre, value_full)
        + mm_trans(d_update_pre, update_full)
    )
    d_tokens = d_middle + norm_back(tokens_f, scale1, d_normed1)
    grads = (*grads, grad_output, grad_gate, grad_up, grad_down)
    grads = [
        scatter_grad(g, "fsdp", "tp") if rows_first else scatter_grad(g, "tp", "fsdp")
        for g, rows_first in zip(grads, inner)
    ]
    return (result, d_tokens, *grads)


def solution(mesh):
    rows = P(AXES, None)
    inner, outer = P("fsdp", "tp"), P("tp", "fsdp")
    by_kernels = mesh.shape["fsdp"] == 8 and mesh.shape["tp"] == 4
    return jax.shard_map(
        body_by_kernels if by_kernels else body,
        mesh=mesh,
        in_specs=(
            rows,
            P("fsdp", None),
            P("tp"),
            inner,
            inner,
            inner,
            inner,
            outer,
            inner,
            inner,
            outer,
            rows,
        ),
        out_specs=(rows, rows, inner, inner, inner, inner, outer, inner, inner, outer),
        check_vma=False,
    )
```

```python
import functools

import jax
import jax.numpy as jnp
from jax import lax
from jax.experimental import pallas as pl
from jax.experimental.pallas import tpu as pltpu
from jax.sharding import PartitionSpec as P

HEAD_DIM = 128
SLOTS = 4

epsilon = 1e-06
head_floor = 1.0
AXES = ("fsdp", "tp")


def swish(values):
    return values * jax.nn.sigmoid(values)


def swish_slope(values):
    sigma = jax.nn.sigmoid(values)
    return sigma * (1.0 + values * (1.0 - sigma))


def rms_scale(values, offset=epsilon):
    return lax.rsqrt(jnp.mean(values * values, axis=-1, keepdims=True) + offset)


def norm_back(values, scale, grads):
    normed = values * scale
    return scale * (grads - normed * jnp.mean(grads * normed, axis=-1, keepdims=True))


def segment_of(places, ends):
    return jnp.sum((places[..., None] >= ends).astype(jnp.int32), axis=-1, dtype=jnp.int32)


def rotate(values, cos_table, sin_table):
    half = values.shape[-1] // 2
    front, back = values[..., :half], values[..., half:]
    return jnp.concatenate(
        [front * cos_table - back * sin_table, front * sin_table + back * cos_table], axis=-1
    )


def rotate_back(values, cos_table, sin_table):
    return rotate(values, cos_table, -sin_table)


def mm(left, right):
    return jnp.dot(left, right, preferred_element_type=jnp.float32)


def mm_trans(left, right):
    return lax.dot_general(
        left, right, (((1,), (1,)), ((), ())), preferred_element_type=jnp.float32
    )


def mm_inner(left, right):
    return lax.dot_general(
        left, right, (((0,), (0,)), ((), ())), preferred_element_type=jnp.float32
    )


def heads_dot(spec, left, right):
    return jnp.einsum(spec, left, right, preferred_element_type=jnp.float32)


def gather_full(shard, row_axis, column_axis):
    part = lax.all_gather(shard, "tp", axis=0 if row_axis == "tp" else 1, tiled=True)
    return lax.all_gather(part, "fsdp", axis=0 if row_axis == "fsdp" else 1, tiled=True)


def scatter_grad(grad, row_axis, column_axis):
    part = grad.astype(jnp.bfloat16)
    part = lax.psum_scatter(
        part, "fsdp", scatter_dimension=0 if row_axis == "fsdp" else 1, tiled=True
    )
    part = lax.psum_scatter(part, "tp", scatter_dimension=0 if row_axis == "tp" else 1, tiled=True)
    return part.astype(jnp.float32)


MESH = pl.DeviceIdType.MESH
VMEM_BYTES = 66_000_000


def place():
    f, t = lax.axis_index("fsdp"), lax.axis_index("tp")
    return f // 4, (f // 2) % 2, f % 2, f, t


def meet(peers):
    barrier = pltpu.get_barrier_semaphore()
    for peer in peers:
        pl.semaphore_signal(barrier, inc=1, device_id=peer, device_id_type=MESH)
    pl.semaphore_wait(barrier, len(peers))


def peers_of(f, t):
    core = (f // 2 * 2 + (1 - f % 2), t)
    along_x = (f // 4 * 4 + (f + 2) % 4, t)
    along_y = ((f + 4) % 8, t)
    along_z = [(f, (t + d) % 4) for d in (1, 2, 3)]
    return core, along_x, along_y, along_z


FAR = 1e7


def swish_of(values):
    return values * jax.nn.sigmoid(values)


def segment_at(where, ends):
    return sum((where >= end).astype(jnp.int32) for end in ends)


def row_tables(lengths_ref, t, rows):
    ends, total = [], jnp.int32(0)
    for j in range(SLOTS):
        total = total + lengths_ref[0, j]
        ends.append(total)
    first = t * rows
    offsets = lax.broadcasted_iota(jnp.int32, (rows, HEAD_DIM), 0)
    return ends, first, offsets, segment_at(first + offsets, ends)


def scalar_segment(where, ends):
    return sum(jnp.where(where >= end, 1, 0) for end in ends)


def fill_span(span_ref, ends, first):
    rows = span_ref.shape[0]
    band = 32

    def step(i, carry):
        row = first + i * band + lax.broadcasted_iota(jnp.int32, (band, rows), 0)
        column = first + lax.broadcasted_iota(jnp.int32, (band, rows), 1)
        allowed = (segment_at(row, ends) == segment_at(column, ends)) & (row >= column)
        span_ref[pl.ds(pl.multiple_of(i * band, band), band), :] = jnp.where(
            allowed, (row - column).astype(jnp.float32), FAR
        )
        return carry

    lax.fori_loop(0, rows // band, step, 0)


def turn(values, cos, sin):
    return values * cos + pltpu.roll(values, HEAD_DIM // 2, 1) * sin


def dot(left, right):
    return jnp.dot(left, right, preferred_element_type=jnp.float32)


def dot_nt(left, right):
    return lax.dot_general(left, right, (((1,), (1,)), ((), ())), preferred_element_type=jnp.float32)


def dot_tn(left, right):
    return lax.dot_general(left, right, (((0,), (0,)), ((), ())), preferred_element_type=jnp.float32)


ORDER = (1, 2, 0, 3, 4, 5, 6, 7)
ROUTES = ("ab", "ab", "ab", "ab", "ab", "cdab", "abab", "abab")
STATE_BYTES = 8 * HEAD_DIM * HEAD_DIM * 2
SLACK = 10.0
RATE = 42_000.0


def arrange(work, first, after):
    clock, free, waiting, events, count = 0.0, {}, {}, [], 0
    known, work = set(), list(work)

    def offer(name):
        known.add(name)
        for item in after(name):
            items = waiting.setdefault(item[0], [])
            items.insert(0 if name[0] == "st" else len(items), item)

    def pump():
        nonlocal count
        for link, items in waiting.items():
            while items and free.get(link, 0.0) <= clock + SLACK:
                _, size, send, receive, name = items.pop(0)
                send()
                free[link] = max(free.get(link, 0.0), clock) + size / RATE + 0.2
                events.append((free[link] + 2.0, count, receive, name))
                count += 1
        events.sort(key=lambda event: event[:2])

    for name in first:
        offer(name)
    pump()
    while work or events:
        if events and events[0][0] <= clock:
            _, _, receive, name = events.pop(0)
            receive()
            offer(name)
        elif work and work[0][2] <= known:
            took, step, _, done = work.pop(0)
            step()
            clock += took
            if done is not None:
                offer(done)
        else:
            times = [free[link] - SLACK for link, items in waiting.items() if items]
            clock = max(clock, min(times + [event[0] for event in events]))
        pump()


N_W = 8
FWD_IN = ("tokens", "cos", "sin", "lengths", "rates")
FWD_OUT = (
    "res",
    "qp",
    "kp",
    "up",
    "q",
    "k",
    "v",
    "o",
    "wt",
    "y1",
    "n1t",
    "n2t",
    "g",
    "e",
    "st",
    "r8",
)


def forward_kernel(*refs):
    shards, refs = refs[:N_W], refs[N_W:]
    inp = dict(zip(FWD_IN, refs))
    refs = refs[len(FWD_IN) :]
    kept, refs = refs[:N_W], refs[N_W:]
    a_out, refs = refs[0], refs[1:]
    out = dict(zip(FWD_OUT, refs))
    refs = refs[len(FWD_OUT) :]
    full, refs = refs[:N_W], refs[N_W:]
    buf = dict(zip(FWD_OUT, refs))
    refs = refs[len(FWD_OUT) :]
    n1, hidden, hidden_turned, span, states, rate_tiles, gate_shard, up_shard = refs[:8]
    own_sem, z_send, z_recv, n_send, n_recv, c_send, c_recv = refs[8:15]
    s_send, s_recv, r_send, r_recv, keep_sem, out_sem, turn_sem = refs[15:]
    gate_shard[...], up_shard[...] = shards[5][...].T, shards[6][...].T
    shards = (*shards[:5], gate_shard, up_shard, shards[7])
    n2, mixed = n1, buf["res"]
    rows = inp["tokens"].shape[0]
    y, x, c, f, t = place()
    core, along_x, along_y, along_z = peers_of(f, t)
    rate_tiles[t] = jnp.concatenate(
        [jnp.full((1, rows), inp["rates"][i % 2], jnp.float32) for i in range(8)], axis=0
    )
    meet([core, along_x, along_y, *along_z])
    pieces = [(w, h) for w in ORDER for h in range(len(ROUTES[w]))]
    total = len(pieces)
    all_ = slice(None)

    def rows_of(p):
        w, h = pieces[p]
        part = shards[w].shape[0] // len(ROUTES[w])
        return pl.ds(h * part, part)

    def route_of(p):
        w, h = pieces[p]
        return ROUTES[w][h]

    def slot(p, *index):
        return full[pieces[p][0]].at[(*index, rows_of(p))]

    def remote(src, dst, send, recv, peer):
        return pltpu.make_async_remote_copy(
            src_ref=src, dst_ref=dst, send_sem=send, recv_sem=recv, device_id=peer, device_id_type=MESH
        )

    def own_copy(p):
        return pltpu.make_async_copy(
            shards[pieces[p][0]].at[rows_of(p)], slot(p, y, x, c, t), own_sem.at[p]
        )

    def z_copy(p, d, source):
        if route_of(p) in "ab":
            src, dst = shards[pieces[p][0]].at[rows_of(p)], slot(p, y, x, c, source)
        else:
            src, dst = slot(p, all_, all_, c, t), slot(p, all_, all_, c, source)
        return remote(src, dst, z_send.at[p, d], z_recv.at[p, d], along_z[d])

    def near_copy(p, stage, arriving):
        over_x = (route_of(p) in "ac") == (stage == 0)
        if stage == 0:
            index = (y, x, c)
            if arriving:
                index = (y, 1 - x, c) if over_x else (1 - y, x, c)
        else:
            if over_x:
                index = (all_, (1 - x) if arriving else x, c)
            else:
                index = ((1 - y) if arriving else y, all_, c)
        ref = slot(p, *index, all_ if route_of(p) in "ab" else t)
        src = ref
        if stage == 0 and route_of(p) in "cd":
            src = shards[pieces[p][0]].at[rows_of(p)]
        return remote(
            src, ref, n_send.at[p, stage], n_recv.at[p, stage], along_x if over_x else along_y
        )

    def core_parts(p):
        return range(3 if route_of(p) in "ab" else 4)

    def core_copy(p, part, arriving):
        side = (1 - c) if arriving else c
        if route_of(p) in "ab":
            first_x = route_of(p) == "a"
            index = (
                (y, x, side, all_),
                (y, 1 - x, side, all_) if first_x else (1 - y, x, side, all_),
                (1 - y, all_, side, all_) if first_x else (all_, 1 - x, side, all_),
            )[part]
        else:
            index = (all_, all_, side, (t + part) % 4)
        ref = slot(p, *index)
        return remote(ref, ref, c_send.at[p, part], c_recv.at[p, part], core)

    def arrived(w):
        for p in range(total):
            if pieces[p][0] == w:
                for part in core_parts(p):
                    core_copy(p, part, True).wait_recv()
        keep(w).start()

    def keep(w):
        return pltpu.make_async_copy(full[w], kept[w], keep_sem.at[w])

    def save(name):
        return pltpu.make_async_copy(buf[name], out[name], out_sem.at[FWD_OUT.index(name)])

    def rate_copy(d, source):
        ref = rate_tiles.at[source]
        return remote(ref, ref, r_send.at[d], r_recv.at[d], along_z[d])

    def state_copy(d, source):
        ref = states.at[source]
        return remote(ref, ref, s_send.at[d], s_recv.at[d], along_z[d])

    ends, first, offsets, segments = row_tables(inp["lengths"], t, rows)
    steps_f = offsets.astype(jnp.float32)

    def head_columns(i, j):
        return pl.ds(pl.multiple_of(i * 2 * HEAD_DIM + j * HEAD_DIM, HEAD_DIM), HEAD_DIM)

    def rate_of(h):
        return buf["r8"][pl.ds(h, 1), :]

    def turn_rows(source, target):
        for j in range(8):
            part = source[:, j * HEAD_DIM : (j + 1) * HEAD_DIM]
            target[j % 2, j // 2 * HEAD_DIM : (j // 2 + 1) * HEAD_DIM] = part.T

    def begin():
        for d in range(3):
            rate_copy(d, t).start()
        values = inp["tokens"][...].astype(jnp.float32)
        n1[...] = (values * rms_scale(values)).astype(jnp.bfloat16)
        turn_rows(n1, buf["n1t"])
        save("n1t").start()
        fill_span(span, ends, first)

    def rates_here():
        for d in range(3):
            rate_copy(d, (t + 3 - d) % 4).wait_recv()
        for j in range(4):
            buf["r8"][2 * j : 2 * j + 2] = rate_tiles[j, 0:2]
        save("r8").start()

    def project(w, finish):
        def run():
            arrived(w)

            def block(i, carry):
                columns = full[w][:, :, :, i].reshape(n1.shape[1], full[w].shape[5])
                values = dot(n1[...], columns)
                for j in range(2):
                    finish(i, j, values[:, j * HEAD_DIM : (j + 1) * HEAD_DIM])
                return carry

            lax.fori_loop(0, 4, block, 0)

        return run

    def finish_key(i, j, values):
        lanes = slice(j * HEAD_DIM, (j + 1) * HEAD_DIM)
        buf["kp"][i, :, lanes] = values.astype(jnp.bfloat16)
        buf["k"][i, :, lanes] = turn(swish_of(values), inp["cos"][...], inp["sin"][...]).astype(jnp.bfloat16)

    def finish_query(i, j, values):
        lanes = slice(j * HEAD_DIM, (j + 1) * HEAD_DIM)
        buf["qp"][i, :, lanes] = values.astype(jnp.bfloat16)
        buf["q"][i, :, lanes] = turn(swish_of(values), inp["cos"][...], inp["sin"][...]).astype(jnp.bfloat16)

    def finish_value(i, j, values):
        lanes = slice(j * HEAD_DIM, (j + 1) * HEAD_DIM)
        buf["v"][i, :, lanes] = values.astype(jnp.bfloat16)

    def finish_update(i, j, values):
        lanes = slice(j * HEAD_DIM, (j + 1) * HEAD_DIM)
        buf["up"][i, :, lanes] = values.astype(jnp.bfloat16)
        buf["y1"][:, head_columns(i, j)] = swish_of(values)

    def make_states():
        last = scalar_segment(first + rows - 1, ends)

        def pair(i, carry):
            for j in range(2):
                h, lanes = 2 * i + j, slice(j * HEAD_DIM, (j + 1) * HEAD_DIM)
                rate = rate_of(h)[:, :HEAD_DIM]
                to_end = jnp.where(segments == last, jnp.exp(-(rows - 1.0 - steps_f) * rate), 0.0)
                scaled = (buf["k"][i, :, lanes].astype(jnp.float32) * to_end).astype(jnp.bfloat16)
                states[t, h] = dot_tn(scaled, buf["v"][i, :, lanes]).astype(jnp.bfloat16)
            return carry

        lax.fori_loop(0, 4, pair, 0)
        for name in ("k", "v", "kp"):
            save(name).start()

    def send_states():
        for d in range(3):
            state_copy(d, t).start()

    def receive_states():
        for d in range(3):
            state_copy(d, (t + 3 - d) % 4).wait_recv()

    def sum_states():
        before = scalar_segment(first - 1, ends)

        def head(h, carry):
            rate = rate_of(h)[:, :HEAD_DIM]
            result = jnp.zeros((HEAD_DIM, HEAD_DIM), jnp.float32)
            for j in range(3):
                reach = jnp.where(
                    (j < t) & (scalar_segment(j * rows + rows - 1, ends) == before), 1.0, 0.0
                )
                distance = jnp.maximum(t - j - 1, 0).astype(jnp.float32) * rows
                weight = reach * jnp.exp(-rate * distance)
                result = result + weight * states[j, h].astype(jnp.float32)
            buf["st"][h] = result.astype(jnp.bfloat16)
            return carry

        lax.fori_loop(0, 8, head, 0)
        save("st").start()
        for name in ("q", "qp", "up"):
            save(name).start()

    def attend(h, carry):
        before = scalar_segment(first - 1, ends)
        half = rows // 2
        i = h // 2
        lanes = pl.ds(pl.multiple_of(lax.rem(h, 2) * HEAD_DIM, HEAD_DIM), HEAD_DIM)
        columns = pl.ds(pl.multiple_of(h * HEAD_DIM, HEAD_DIM), HEAD_DIM)
        rate = rate_of(h)
        for b in range(2):
            mine = slice(b * half, (b + 1) * half)
            keys = (b + 1) * half
            query = buf["q"][i, mine, lanes]
            scores = dot_nt(query, buf["k"][i, :keys, lanes])
            decay = jnp.exp(-span[mine, :keys] * rate[:, :keys])
            weights = (scores * decay).astype(jnp.bfloat16)
            into = jnp.where(
                segments[mine] == before,
                jnp.exp(-(steps_f[mine] + 1.0) * rate[:, :HEAD_DIM]),
                0.0,
            )
            attn = dot(weights, buf["v"][i, :keys, lanes]) + into * dot(query, buf["st"][h])
            buf["o"][mine, columns] = attn
            normed = attn * rms_scale(attn, head_floor)
            mixed[mine, columns] = (normed * buf["y1"][mine, columns]).astype(jnp.bfloat16)
        return carry

    def attend_pairs(lo, hi):
        return lambda: (lax.fori_loop(2 * lo, 2 * hi, attend, 0), None)[1]

    def mix():
        save("o").start()
        for i in range(4):
            columns = slice(i * 2 * HEAD_DIM, (i + 1) * 2 * HEAD_DIM)
            buf["wt"][i] = mixed[:, columns].T
        save("wt").start()
        arrived(4)

        def block(i, carry):
            sides = [full[4][i // 2, i % 2, s].reshape(n1.shape[1], HEAD_DIM) for s in range(2)]
            columns = pl.ds(pl.multiple_of(i * 2 * HEAD_DIM, 2 * HEAD_DIM), 2 * HEAD_DIM)
            buf["y1"][:, columns] = inp["tokens"][:, columns].astype(jnp.float32) + dot(
                mixed[...], jnp.concatenate(sides, axis=1)
            )
            return carry

        lax.fori_loop(0, 4, block, 0)
        values = buf["y1"][...]
        n2[...] = (values * rms_scale(values)).astype(jnp.bfloat16)
        turn_rows(n2, buf["n2t"])
        save("y1").start()
        save("n2t").start()

    def turned_out(i):
        return pltpu.make_async_copy(hidden_turned.at[i % 2], a_out.at[i], turn_sem.at[i])

    def gate_up(i):
        def go():
            if i == 0:
                arrived(6)
            shape = (n1.shape[1], full[5].shape[5])

            def band(b, carry):
                mine = pl.ds(pl.multiple_of(b * rows // 2, rows // 2), rows // 2)
                gate = dot(n2[mine], full[5][:, :, :, i].reshape(shape))
                lift = dot(n2[mine], full[6][:, :, :, i].reshape(shape))
                hidden[i, mine] = (gate * lift).astype(jnp.bfloat16)
                buf["g"][i, mine] = gate.astype(jnp.bfloat16)
                buf["e"][i, mine] = lift.astype(jnp.bfloat16)
                return carry

            lax.fori_loop(0, 2, band, 0)
            if i >= 2:
                turned_out(i - 2).wait()
            hidden_turned[i % 2] = hidden[i].T
            turned_out(i).start()
            if i == 3:
                for name in ("g", "e"):
                    save(name).start()

        return go

    def close():
        arrived(7)

        def block(i, carry):
            columns = pl.ds(pl.multiple_of(i * 2 * HEAD_DIM, 2 * HEAD_DIM), 2 * HEAD_DIM)
            values = buf["y1"][:, columns]
            for j in range(4):
                sides = [full[7][i // 2, i % 2, s, j] for s in range(2)]
                values = values + dot(hidden[j], jnp.concatenate(sides, axis=1))
            buf["res"][:, columns] = values.astype(jnp.bfloat16)
            return carry

        lax.fori_loop(0, 4, block, 0)
        save("res").start()

    def after(name):
        stage, p, part = name
        size = shards[pieces[p][0]].size * 2 // len(ROUTES[pieces[p][0]])
        early = route_of(p) in "ab"

        def over_z():
            def send():
                for d in range(3):
                    z_copy(p, d, t).start()

            def receive():
                for d in range(3):
                    z_copy(p, d, (t + 3 - d) % 4).wait_recv()
                if early:
                    own_copy(p).wait()

            return ("z", (4 if early else 16) * size, send, receive, ("z", p, 0))

        def over_near(k):
            blocks = (4, 8)[k] if early else (1, 2)[k]
            link = "x" if (route_of(p) in "ac") == (k == 0) else "y"

            def receive():
                near_copy(p, k, True).wait_recv()
                if k == 0 and not early:
                    own_copy(p).wait()

            return (link, blocks * size, near_copy(p, k, False).start, receive, ("n", p, k))

        def over_core(k, blocks):
            def send():
                core_copy(p, k, False).start()

            return ("c", blocks * size // 4, send, lambda: None, ("c", p, k))

        if stage == "st":
            return [("z", 4 * STATE_BYTES, send_states, receive_states, ("sr", 0, 0))]
        if stage == "go":
            own_copy(p).start()
            return [over_z() if early else over_near(0)]
        if stage == "z":
            if early:
                return [over_near(0), over_core(0, 4)]
            return [over_core(k, 4) for k in (1, 2, 3)]
        if stage == "n":
            if part == 0:
                return [over_near(1)] + ([over_core(1, 4)] if early else [])
            return [over_core(2, 8)] if early else [over_z(), over_core(0, 4)]
        return []

    needs = set()
    steps = []

    def then(took, step, *weights, done=None):
        for p in range(total):
            if pieces[p][0] in weights:
                needs.update(("c", p, k) for k in core_parts(p))
        steps.append((took, step, set(needs), done))

    then(2.0, begin)
    then(0.2, rates_here)
    then(2.2, project(1, finish_key), 1)
    then(2.2, project(2, finish_value), 2)
    then(1.5, make_states, done=("st", 0, 0))
    then(2.2, project(0, finish_query), 0)
    then(2.2, project(3, finish_update), 3)
    needs.add(("sr", 0, 0))
    then(0.5, sum_states)
    for i in range(4):
        then(1.8, attend_pairs(i, i + 1))
    then(3.0, mix, 4)
    then(0.1, lambda: arrived(5), 5)
    for i in range(4):
        then(3.0, gate_up(i), 6)
    then(4.0, close, 7)
    arrange(steps, [("go", p, 0) for p in range(total)], after)
    for d in range(3):
        rate_copy(d, t).wait_send()
        state_copy(d, t).wait_send()
    for p in range(total):
        for d in range(3):
            z_copy(p, d, t).wait_send()
        for stage in range(2):
            near_copy(p, stage, False).wait_send()
        for part in core_parts(p):
            core_copy(p, part, False).wait_send()
    for w in range(N_W):
        keep(w).wait()
    for name in FWD_OUT:
        save(name).wait()
    for i in range(2, 4):
        turned_out(i).wait()


def forward(shards, tokens, cos, sin, lengths, rates):
    rows, width = tokens.shape
    units, depth = shards[5].shape
    heads = width // HEAD_DIM
    low, wide = jnp.bfloat16, jnp.float32
    by_pair = (4, rows, heads // 4 * HEAD_DIM)
    turned = (2, width // 2, rows)
    by_unit = (4, rows, units)
    shapes = {
        "res": ((rows, width), low),
        "qp": (by_pair, low),
        "kp": (by_pair, low),
        "up": (by_pair, low),
        "q": (by_pair, low),
        "k": (by_pair, low),
        "v": (by_pair, low),
        "o": ((rows, width), wide),
        "wt": ((4, width // 4, rows), low),
        "y1": ((rows, width), wide),
        "n1t": (turned, low),
        "n2t": (turned, low),
        "g": (by_unit, low),
        "e": (by_unit, low),
        "st": ((heads, HEAD_DIM, HEAD_DIM), low),
        "r8": ((8, rows), wide),
    }
    blocks = [(2, 2, 2, 4, *(s.shape[::-1] if i in (5, 6) else s.shape)) for i, s in enumerate(shards)]
    pieces = sum(len(route) for route in ROUTES)
    dma = pltpu.SemaphoreType.DMA
    in_vmem, in_smem = (pl.BlockSpec(memory_space=m) for m in (pltpu.VMEM, pltpu.SMEM))
    outs = pl.pallas_call(
        forward_kernel,
        name="gather_and_forward",
        out_shape=[jax.ShapeDtypeStruct(b, low) for b in blocks]
        + [jax.ShapeDtypeStruct((4, units, rows), low)]
        + [jax.ShapeDtypeStruct(*shapes[name]) for name in FWD_OUT],
        in_specs=[in_vmem] * (N_W + 3) + [in_smem] * 2,
        out_specs=[pl.BlockSpec(memory_space=pl.ANY)] * (N_W + 1 + len(FWD_OUT)),
        scratch_shapes=[
            *[pltpu.VMEM(b, low) for b in blocks],
            *[pltpu.VMEM(*shapes[name]) for name in FWD_OUT],
            pltpu.VMEM((rows, width), low),
            pltpu.VMEM(by_unit, low),
            pltpu.VMEM((2, units, rows), low),
            pltpu.VMEM((rows, rows), wide),
            pltpu.VMEM((4, heads, HEAD_DIM, HEAD_DIM), low),
            pltpu.VMEM((4, 8, rows), wide),
            pltpu.VMEM((depth, units), low),
            pltpu.VMEM((depth, units), low),
            dma((pieces,)),
            dma((pieces, 3)),
            dma((pieces, 3)),
            dma((pieces, 2)),
            dma((pieces, 2)),
            dma((pieces, 4)),
            dma((pieces, 4)),
            dma((3,)),
            dma((3,)),
            dma((3,)),
            dma((3,)),
            dma((N_W,)),
            dma((len(FWD_OUT),)),
            dma((4,)),
        ],
        compiler_params=pltpu.CompilerParams(
            collective_id=0, has_side_effects=True, vmem_limit_bytes=VMEM_BYTES
        ),
    )(*shards, tokens, cos, sin, lengths, rates)
    return outs[:N_W], outs[N_W], dict(zip(FWD_OUT, outs[N_W + 1 :]))


BWD_ANY = ("q", "k", "v", "up", "qp", "kp", "o", "wt", "y1", "n1t", "n2t", "g", "e")
BWD_VMEM = ("st", "r8", "cos", "sin")
BAND = 32
SUMS = ("ab", "ab", "ab", "ab", "ab", "cb", "ab", "ab")


def slope_of(values):
    sigma = jax.nn.sigmoid(values)
    return sigma * (1.0 + values * (1.0 - sigma))


def turn_back(values, cos, sin):
    return values * cos - pltpu.roll(values, HEAD_DIM // 2, 1) * sin


def backward_kernel(*refs):
    kept, refs = refs[:N_W], refs[N_W:]
    a_in, refs = refs[0], refs[1:]
    inp = dict(zip(BWD_ANY + BWD_VMEM, refs))
    refs = refs[len(BWD_ANY + BWD_VMEM) :]
    tokens, out_grad, lengths = refs[:3]
    grads, d_tokens = refs[3 : 3 + N_W], refs[3 + N_W]
    refs = refs[4 + N_W :]
    mine, from_near, from_far, from_z = (refs[i * N_W : (i + 1) * N_W] for i in range(4))
    refs = refs[4 * N_W :]
    tall, wide, turned_a, gq, ev, d_side, n_turned, rows_a, rows_b, tall_w, wide_w = refs[:11]
    q_pre, w_turned, span, states, back = refs[11:16]
    load_sem, tall_sem, wide_sem, c_send, c_recv, n_send, n_recv, z_send, z_recv = refs[16:25]
    s_send, s_recv, o_send, o_recv = refs[25:]
    rows, width = rows_a.shape
    half = rows // 2
    y, x, c, f, t = place()
    core, along_x, along_y, along_z = peers_of(f, t)
    all_ = slice(None)

    keys = {}

    def load(key, source, target):
        index = keys.setdefault(key, len(keys))
        return pltpu.make_async_copy(source, target, load_sem.at[index])

    def pair_columns(i):
        return slice(i * 2 * HEAD_DIM, (i + 1) * 2 * HEAD_DIM)

    def by_pairs(key, source, place_):
        return [load((key, i), source.at[:, pair_columns(i)], q_pre.at[place_, i]) for i in range(4)]

    lane_pair = [slice(0, 2 * HEAD_DIM), slice(2 * HEAD_DIM, 4 * HEAD_DIM)]
    loads = {
        "cot": by_pairs("cot", out_grad, 0),
        "tokens": by_pairs("tokens", tokens, 0),
        "a": [load("a", a_in, turned_a)],
        "g": [load("g", inp["g"], gq)],
        "e": [load("e", inp["e"], ev)],
        "n2": [load("n2", inp["n2t"], n_turned)],
        "n1": [load("n1", inp["n1t"], n_turned)],
        "y1": [load("y1", inp["y1"], rows_a)],
        "o": [load("o", inp["o"], rows_a)],
        "w": [load("w", inp["wt"], w_turned)],
        "qp": [load("qp", inp["qp"], q_pre.at[0])],
        "kp": [load("kp", inp["kp"], q_pre.at[1])],
        "q": [load("q", inp["q"], gq.at[:, :, lane_pair[0]])],
        "k": [load("k", inp["k"], gq.at[:, :, lane_pair[1]])],
        "v": [load("v", inp["v"], ev.at[:, :, lane_pair[0]])],
        "up": [load("up", inp["up"], turned_a.at[:, :rows, lane_pair[1]])],
        "out": [load("out", rows_b, d_tokens)],
    }

    def start(*names):
        for name in names:
            for copy in loads[name]:
                copy.start()

    def wait(*names):
        for name in names:
            for copy in loads[name]:
                copy.wait()

    def tile(w, i, slot):
        if w in (4, 7):
            depth = kept[w].shape[4]
            return pltpu.make_async_copy(
                kept[w].at[:, :, :, i], tall_w.at[slot, :, :, :, :depth], tall_sem.at[slot]
            )
        lanes = kept[w].shape[5]
        return pltpu.make_async_copy(
            kept[w].at[:, :, :, i], wide_w.at[slot, :, :, :, :, :lanes], wide_sem.at[slot]
        )

    def over_tiles(w, use, lo=0, hi=4):
        tile(w, lo, lo % 2).start()

        def step(i, carry):
            slot = lax.rem(i, 2)

            @pl.when(i < hi - 1)
            def _():
                tile(w, i + 1, 1 - slot).start()

            tile(w, i, slot).wait()
            use(i, slot)
            return carry

        lax.fori_loop(lo, hi, step, 0)

    pieces = [(w, h) for w in range(N_W) for h in range(2)]

    def remote(src, dst, send, recv, peer):
        return pltpu.make_async_remote_copy(
            src_ref=src, dst_ref=dst, send_sem=send, recv_sem=recv, device_id=peer, device_id_type=MESH
        )

    def rows_of(p):
        w, h = pieces[p]
        part = grads[w].shape[0] // 2
        return pl.ds(h * part, part)

    def ring_of(w):
        return (tall, 0) if w in (4, 7) else (wide, 1)

    def core_copy(w, i):
        ring, kind = ring_of(w)
        depth, lanes = grads[w].shape
        return remote(
            ring.at[lax.rem(i, 2), :, :, :depth, :lanes],
            mine[w].at[:, :, i],
            c_send.at[kind, lax.rem(i, 2)],
            c_recv.at[w, i],
            core,
        )

    def near_copy(p):
        (w, h), part = pieces[p], rows_of(p)
        src = mine[w].at[1 - y, :, :, part] if h == 0 else mine[w].at[:, 1 - x, :, part]
        return remote(
            src,
            from_near[w].at[:, :, part],
            n_send.at[p, 0],
            n_recv.at[p, 0],
            along_y if h == 0 else along_x,
        )

    def far_copy(p):
        (w, h), part = pieces[p], rows_of(p)
        src = mine[w].at[y, 1 - x, :, part] if h == 0 else mine[w].at[1 - y, x, :, part]
        return remote(
            src,
            from_far[w].at[:, part],
            n_send.at[p, 1],
            n_recv.at[p, 1],
            along_x if h == 0 else along_y,
        )

    def z_copy(p, d):
        w, part = pieces[p][0], rows_of(p)
        return remote(
            mine[w].at[y, x, (t + d + 1) % 4, part],
            from_z[w].at[d, part],
            z_send.at[p, d],
            z_recv.at[p, d],
            along_z[d],
        )

    def far_first(p, d, a, source):
        w, part = pieces[p][0], rows_of(p)
        dst = from_near[w].at[d, 2 * a : 2 * a + 2] if d < 2 else from_far[w].at[2 * a : 2 * a + 2]
        return remote(
            mine[w].at[a, :, source, part],
            dst.at[:, part],
            o_send.at[2 * d + a],
            o_recv.at[2 * d + a],
            along_z[d],
        )

    def then_near(p, k):
        w, part = pieces[p][0], rows_of(p)
        if k == 0:
            src, dst = mine[w].at[1 - y, :, t, part], from_z[w].at[0:2, part]
        else:
            src, dst = mine[w].at[y, 1 - x, t, part], from_z[w].at[2, part]
        return remote(src, dst, o_send.at[6 + k], o_recv.at[6 + k], (along_y, along_x)[k])

    def plus(into, *terms):
        total = into[...].astype(jnp.float32)
        for term in terms:
            total = total + term[...].astype(jnp.float32)
        return total

    def add(steps, target, other):
        def step(i, carry):
            into, term = target(i), other(i)
            into[...] = (into[...].astype(jnp.float32) + term[...].astype(jnp.float32)).astype(
                jnp.bfloat16
            )
            return carry

        lax.fori_loop(0, steps, step, 0)

    def after_near(p):
        (w, h), part = pieces[p], rows_of(p)
        near_copy(p).wait_recv()
        if h == 0:
            into = lambda i: mine[w].at[y, i // 4, i % 4, part]
        else:
            into = lambda i: mine[w].at[i // 4, x, i % 4, part]
        add(8, into, lambda i: from_near[w].at[i // 4, i % 4, part])

    def after_far(p):
        w, part = pieces[p][0], rows_of(p)
        far_copy(p).wait_recv()
        add(4, lambda i: mine[w].at[y, x, i, part], lambda i: from_far[w].at[i, part])

    def after_z(p):
        w, part = pieces[p][0], rows_of(p)
        for d in range(3):
            z_copy(p, d).wait_recv()
        result = mine[w][y, x, t, part].astype(jnp.float32)
        for d in range(3):
            result = result + from_z[w][d, part].astype(jnp.float32)
        grads[w][part] = result

    used = {0: None, 1: None}

    def gradient(w, own, value):
        ring, kind = ring_of(w)
        depth, lanes = grads[w].shape

        def blocks(i):
            for q in range(2):
                result = value(i, (c if own else 1 - c), slice(2 * q * HEAD_DIM, (2 * q + 2) * HEAD_DIM))
                for b in range(2):
                    if kind == 1:
                        yield q, b, result[b * depth : (b + 1) * depth]
                    else:
                        yield q, b, result[:, b * lanes : (b + 1) * lanes]

        def run():
            if not own:
                before = used[kind]
                used[kind] = w

                def step(i, carry):
                    if before is not None:

                        @pl.when(i < 2)
                        def _():
                            core_copy(before, i + 2).wait_send()

                    @pl.when(i >= 2)
                    def _():
                        core_copy(w, i - 2).wait_send()

                    slot = lax.rem(i, 2)
                    for a, b, part in blocks(i):
                        ring[slot, a, b, :depth, :lanes] = part.astype(jnp.bfloat16)
                    core_copy(w, i).start()
                    return carry

                lax.fori_loop(0, 4, step, 0)
            else:

                def step(i, carry):
                    core_copy(w, i).wait_recv()
                    for a, b, part in blocks(i):
                        mine[w][a, b, i] = (mine[w][a, b, i].astype(jnp.float32) + part).astype(
                            jnp.bfloat16
                        )
                    return carry

                lax.fori_loop(0, 4, step, 0)

        return run

    ends, first, offsets, segments = row_tables(lengths, t, rows)
    steps_f = offsets.astype(jnp.float32)
    seg_before = scalar_segment(first - 1, ends)
    seg_after = scalar_segment(first + rows, ends)
    seg_first = scalar_segment(first, ends)

    def lanes_of(j, base=0):
        return slice(base + j * HEAD_DIM, base + (j + 1) * HEAD_DIM)

    def rate_of(h):
        return inp["r8"][pl.ds(h, 1), :]

    def over_rows(use):
        def step(i, carry):
            use(pl.ds(pl.multiple_of(i * BAND, BAND), BAND))
            return carry

        lax.fori_loop(0, rows // BAND, step, 0)

    def begin():
        start("cot", "a", "e", "g", "n2", "y1", "w")
        fill_span(span, ends, first)
        live = jnp.where(segments < SLOTS - 1, 1.0, 0.0)
        wait("cot")
        for i in range(4):
            for s in range(2):
                part = q_pre[0, i, :, lanes_of(s)].astype(jnp.float32) * live
                d_side[s, :, lanes_of(i)] = part.astype(jnp.bfloat16)
        start("qp", "kp")
        wait("a")

    def expand(lo, hi):
        def use(i, slot):
            def band(b, carry):
                part = pl.ds(pl.multiple_of(b * half, half), half)
                d_hidden = sum(
                    dot_nt(
                        d_side[s, part],
                        jnp.concatenate([tall_w[slot, j // 2, j % 2, s] for j in range(4)], axis=1),
                    )
                    for s in range(2)
                )
                lift, gate = ev[i, part].astype(jnp.float32), gq[i, part].astype(jnp.float32)
                ev[i, part] = (d_hidden * lift).astype(jnp.bfloat16)
                gq[i, part] = (d_hidden * gate).astype(jnp.bfloat16)
                return carry

            lax.fori_loop(0, 2, band, 0)

        def run():
            if lo == 0:
                wait("e", "g")
            over_tiles(7, use, lo, hi)
            if hi == 4:
                wait("n2")

        return run

    def through(w, source, target, clear):
        def run():
            if clear:
                target[...] = jnp.zeros_like(target)
            lanes = kept[w].shape[5]

            def use(i, slot):
                for j in range(4):
                    part = wide_w[slot, j // 2, j % 2, :, :, :lanes].reshape(2 * HEAD_DIM, lanes)
                    target[:, pair_columns(j)] += dot_nt(source(i), part)

            over_tiles(w, use)

        return run

    def middle_back():
        start("v", "q", "k")
        wait("y1")

        def use(part):
            values = rows_a[part, :]
            cot = jnp.concatenate(
                [d_side[j % 2, part, lanes_of(j // 2)].astype(jnp.float32) for j in range(8)], axis=1
            )
            result = cot + norm_back(values, rms_scale(values), rows_b[part, :])
            rows_b[part, :] = result
            for j in range(8):
                d_side[j % 2, part, lanes_of(j // 2)] = result[:, lanes_of(j)].astype(jnp.bfloat16)

        over_rows(use)
        start("o")
        wait("w")

    def mixed_back():
        wait("o", "up")

        def use(i, slot):
            def band(b, carry):
                part = pl.ds(pl.multiple_of(b * half, half), half)
                d_mixed = sum(
                    dot_nt(
                        d_side[s, part],
                        jnp.concatenate(
                            [tall_w[slot, j // 2, j % 2, s, : 2 * HEAD_DIM] for j in range(4)], axis=1
                        ),
                    )
                    for s in range(2)
                )
                for j in range(2):
                    columns = pl.ds(pl.multiple_of((2 * i + j) * HEAD_DIM, HEAD_DIM), HEAD_DIM)
                    attn = rows_a[part, columns]
                    scale = rms_scale(attn, head_floor)
                    normed = attn * scale
                    pre = turned_a[i, part, lanes_of(j, 2 * HEAD_DIM)].astype(jnp.float32)
                    grad_ = d_mixed[:, lanes_of(j)]
                    turned_a[i, part, lanes_of(j)] = (grad_ * normed * slope_of(pre)).astype(
                        jnp.bfloat16
                    )
                    d_attn = norm_back(attn, scale, grad_ * swish_of(pre))
                    ev[i, part, lanes_of(j, 2 * HEAD_DIM)] = d_attn.astype(jnp.bfloat16)
                return carry

            lax.fori_loop(0, 2, band, 0)

        over_tiles(4, use)
        wait("n1", "q")

    def make_states():
        def pair(i, carry):
            for j in range(2):
                rate = rate_of(2 * i + j)[:, :HEAD_DIM]
                from_start = jnp.where(segments == seg_first, jnp.exp(-steps_f * rate), 0.0)
                scaled = (gq[i, :, lanes_of(j)].astype(jnp.float32) * from_start).astype(jnp.bfloat16)
                states[t, 2 * i + j] = dot_tn(scaled, ev[i, :, lanes_of(j, 2 * HEAD_DIM)]).astype(
                    jnp.bfloat16
                )
            return carry

        lax.fori_loop(0, 4, pair, 0)

    def state_copy(d, source):
        ref = states.at[source]
        return remote(ref, ref, s_send.at[d], s_recv.at[d], along_z[d])

    def send_states():
        for d in range(3):
            state_copy(d, t).start()

    def receive_states():
        for d in range(3):
            state_copy(d, (t + 3 - d) % 4).wait_recv()

    def sum_states():
        wait("v", "k", "qp", "kp")

        def head(h, carry):
            rate = rate_of(h)[:, :HEAD_DIM]
            result = jnp.zeros((HEAD_DIM, HEAD_DIM), jnp.float32)
            for j in range(1, 4):
                reach = jnp.where((j > t) & (scalar_segment(j * rows, ends) == seg_after), 1.0, 0.0)
                distance = jnp.maximum(j - t - 1, 0).astype(jnp.float32) * rows
                weight = reach * jnp.exp(-rate * distance)
                result = result + weight * states[j, h].astype(jnp.float32)
            back[h] = result.astype(jnp.bfloat16)
            return carry

        lax.fori_loop(0, 8, head, 0)

    def attend_back(h, carry):
        cos, sin = inp["cos"][...], inp["sin"][...]
        i, j = h // 2, lax.rem(h, 2)
        low_lanes = pl.ds(pl.multiple_of(j * HEAD_DIM, HEAD_DIM), HEAD_DIM)
        high_lanes = pl.ds(pl.multiple_of((2 + j) * HEAD_DIM, HEAD_DIM), HEAD_DIM)
        rate = rate_of(h)
        short = rate[:, :HEAD_DIM]
        key, value = gq[i, :, high_lanes], ev[i, :, low_lanes]
        state_in, state_back = inp["st"][h], back[h]
        out_of = jnp.where(segments == seg_after, jnp.exp(-(rows - steps_f) * short), 0.0)
        d_value = out_of * dot(key, state_back)
        d_key = out_of * dot_nt(value, state_back)
        d_query = []
        for b in range(2):
            part = slice(b * half, (b + 1) * half)
            keys = (b + 1) * half
            query = gq[i, part, low_lanes]
            grad = ev[i, part, high_lanes]
            decay = jnp.exp(-span[part, :keys] * rate[:, :keys])
            weights = (dot_nt(query, key[:keys]) * decay).astype(jnp.bfloat16)
            d_raw = (dot_nt(grad, value[:keys]) * decay).astype(jnp.bfloat16)
            into = jnp.where(
                segments[part] == seg_before, jnp.exp(-(steps_f[part] + 1.0) * short), 0.0
            )
            d_query.append(dot(d_raw, key[:keys]) + into * dot_nt(grad, state_in))
            add_value, add_key = dot_tn(weights, grad), dot_tn(d_raw, query)
            if b == 0:
                d_value = jnp.concatenate([d_value[:half] + add_value, d_value[half:]], axis=0)
                d_key = jnp.concatenate([d_key[:half] + add_key, d_key[half:]], axis=0)
            else:
                d_value, d_key = d_value + add_value, d_key + add_key
        d_query = jnp.concatenate(d_query, axis=0)
        pre_query = q_pre[0, i, :, low_lanes].astype(jnp.float32)
        pre_key = q_pre[1, i, :, low_lanes].astype(jnp.float32)
        gq[i, :, low_lanes] = (slope_of(pre_query) * turn_back(d_query, cos, sin)).astype(
            jnp.bfloat16
        )
        gq[i, :, high_lanes] = (
            slope_of(pre_key) * turn_back(d_key, cos, sin)
        ).astype(jnp.bfloat16)
        ev[i, :, low_lanes] = d_value.astype(jnp.bfloat16)
        return carry

    def close():
        wait("tokens")

        def use(part):
            values = jnp.concatenate([q_pre[0, i, part, :] for i in range(4)], axis=1)
            values = values.astype(jnp.float32)
            rows_b[part, :] += norm_back(values, rms_scale(values), rows_a[part, :])

        over_rows(use)
        start("out")

    low_pair, high_pair = slice(0, 2 * HEAD_DIM), slice(2 * HEAD_DIM, 4 * HEAD_DIM)
    sources = {
        0: lambda i: gq[i, :, low_pair],
        1: lambda i: gq[i, :, high_pair],
        2: lambda i: ev[i, :, low_pair],
        3: lambda i: turned_a[i, :rows, low_pair],
        5: lambda i: ev[i],
        6: lambda i: gq[i],
    }

    def grad(w, own):
        if w == 7:
            value = lambda i, s, half_: dot(turned_a[i], d_side[s, :, half_])
        elif w == 4:
            value = lambda i, s, half_: dot(w_turned[i], d_side[s, :, half_])
        else:
            value = lambda i, s, half_: dot(n_turned[s, half_], sources[w](i))
        return gradient(w, own, value)

    def attend_pairs(lo, hi):
        return lambda: (lax.fori_loop(2 * lo, 2 * hi, attend_back, 0), None)[1]

    work = [
        (3.0, begin, None),
        (2.5, grad(7, False), None),
        (3.0, expand(0, 2), None),
        (3.0, grad(7, True), 7),
        (3.0, expand(2, 4), None),
        (2.5, grad(5, False), None),
        (0.1, lambda: start("up"), None),
        (2.5, grad(6, False), None),
        (3.0, grad(5, True), 5),
        (3.0, grad(6, True), 6),
        (0.1, lambda: start("n1"), None),
        (5.0, through(5, sources[5], rows_b, True), None),
        (5.0, through(6, sources[6], rows_b, False), None),
        (3.0, middle_back, None),
        (1.0, grad(4, False), None),
        (6.0, mixed_back, None),
        (2.0, make_states, -1),
        (1.0, grad(3, False), None),
        (1.2, grad(4, True), 4),
        (1.2, grad(3, True), 3),
        (2.0, through(3, sources[3], rows_a, True), None),
        (1.0, sum_states, None),
        (4.0, attend_pairs(0, 1), None),
        (4.0, attend_pairs(1, 2), None),
        (4.0, attend_pairs(2, 3), None),
        (4.0, attend_pairs(3, 4), None),
        (1.0, grad(2, False), None),
        (1.0, grad(0, False), None),
        (1.0, grad(1, False), None),
        (1.2, grad(2, True), 2),
        (1.2, grad(0, True), 0),
        (1.2, grad(1, True), 1),
        (0.1, lambda: start("tokens"), None),
        (2.0, through(2, sources[2], rows_a, False), None),
        (2.0, through(0, sources[0], rows_a, False), None),
        (2.0, through(1, sources[1], rows_a, False), None),
        (2.0, close, None),
    ]
    meet([core, along_x, along_y, *along_z])

    def after(name):
        stage, p = name
        if stage == "st":
            return [("z", 4 * STATE_BYTES, send_states, receive_states, ("sr", 0))]
        if stage == "sr":
            return []
        if stage == "grad":
            return [first_send(2 * p + h) for h in range(2)]
        (w, h), part = pieces[p], rows_of(p)
        size = grads[w].size
        route = SUMS[w][h]
        if stage == "near":
            link = "x" if route == "a" else "y"
            return [(link, 4 * size, far_copy(p).start, lambda: after_far(p), ("far", p))]
        if stage == "far":

            def send():
                for d in range(3):
                    z_copy(p, d).start()

            return [("z", 4 * size, send, lambda: after_z(p), ("z", p))]
        if stage == "c0":

            def receive_y():
                then_near(p, 0).wait_recv()
                for b in range(2):
                    into = mine[w].at[y, b, t, part]
                    into[...] = plus(into, from_z[w].at[b, part]).astype(jnp.bfloat16)

            return [("y", 2 * size, then_near(p, 0).start, receive_y, ("c1", p))]
        if stage == "c1":

            def receive_x():
                then_near(p, 1).wait_recv()
                grads[w][part] = plus(mine[w].at[y, x, t, part], from_z[w].at[2, part])

            return [("x", size, then_near(p, 1).start, receive_x, ("c2", p))]
        return []

    def first_send(p):
        (w, h), part = pieces[p], rows_of(p)
        size = grads[w].size
        if SUMS[w][h] == "c":

            def send():
                for d in range(3):
                    for a in range(2):
                        far_first(p, d, a, (t + d + 1) % 4).start()

            def receive():
                for d in range(3):
                    for a in range(2):
                        far_first(p, d, a, (t + d + 1) % 4).wait_recv()
                for i in range(4):
                    into = mine[w].at[i // 2, i % 2, t, part]
                    into[...] = plus(
                        into,
                        from_near[w].at[0, i, part],
                        from_near[w].at[1, i, part],
                        from_far[w].at[i, part],
                    ).astype(jnp.bfloat16)

            return ("z", 16 * size, send, receive, ("c0", p))
        link = "y" if SUMS[w][h] == "a" else "x"
        return (link, 8 * size, near_copy(p).start, lambda: after_near(p), ("near", p))

    arrange(
        [
            (
                took,
                run,
                {("sr", 0)} if run is sum_states else set(),
                ("st", 0) if done == -1 else None if done is None else ("grad", done),
            )
            for took, run, done in work
        ],
        [],
        after,
    )
    for kind in range(2):
        for i in range(2, 4):
            core_copy(used[kind], i).wait_send()
    for p in range(len(pieces)):
        if SUMS[pieces[p][0]][pieces[p][1]] == "c":
            for d in range(3):
                for a in range(2):
                    far_first(p, d, a, (t + d + 1) % 4).wait_send()
            then_near(p, 0).wait_send()
            then_near(p, 1).wait_send()
        else:
            near_copy(p).wait_send()
            far_copy(p).wait_send()
            for d in range(3):
                z_copy(p, d).wait_send()
    for d in range(3):
        state_copy(d, t).wait_send()
    wait("out")


def backward(kept, a_turned, saved, cos, sin, tokens, out_grad, lengths):
    rows, width = tokens.shape
    low, wide = jnp.bfloat16, jnp.float32
    units = a_turned.shape[1]
    pair = width // 4
    shards = [w.shape[4:] for w in kept]
    dma = pltpu.SemaphoreType.DMA
    anywhere, in_vmem, in_smem = (
        pl.BlockSpec(memory_space=m) for m in (pl.ANY, pltpu.VMEM, pltpu.SMEM)
    )
    pieces = 2 * N_W

    def buffers(*lead):
        return [pltpu.VMEM((*lead, *s), low) for s in shards]

    outs = pl.pallas_call(
        backward_kernel,
        name="backward_and_scatter",
        out_shape=[jax.ShapeDtypeStruct(s, wide) for s in shards]
        + [jax.ShapeDtypeStruct((rows, width), wide)],
        in_specs=[anywhere] * (N_W + 1 + len(BWD_ANY))
        + [in_vmem] * len(BWD_VMEM)
        + [anywhere, anywhere, in_smem],
        out_specs=[in_vmem] * N_W + [anywhere],
        scratch_shapes=[
            *buffers(2, 2, 4),
            *buffers(2, 4),
            *buffers(4),
            *buffers(3),
            pltpu.VMEM((2, 2, 2, units, HEAD_DIM), low),
            pltpu.VMEM((2, 2, 2, HEAD_DIM, units), low),
            pltpu.VMEM((4, units, rows), low),
            pltpu.VMEM((4, rows, units), low),
            pltpu.VMEM((4, rows, units), low),
            pltpu.VMEM((2, rows, width // 2), low),
            pltpu.VMEM((2, width // 2, rows), low),
            pltpu.VMEM((rows, width), wide),
            pltpu.VMEM((rows, width), wide),
            pltpu.VMEM((2, 2, 2, 2, units, HEAD_DIM), low),
            pltpu.VMEM((2, 2, 2, 2, HEAD_DIM, units), low),
            pltpu.VMEM((2, 4, rows, pair), low),
            pltpu.VMEM((4, pair, rows), low),
            pltpu.VMEM((rows, rows), wide),
            pltpu.VMEM((4, width // HEAD_DIM, HEAD_DIM, HEAD_DIM), low),
            pltpu.VMEM((width // HEAD_DIM, HEAD_DIM, HEAD_DIM), low),
            dma((24,)),
            dma((2,)),
            dma((2,)),
            dma((2, 2)),
            dma((N_W, 4)),
            dma((pieces, 2)),
            dma((pieces, 2)),
            dma((pieces, 3)),
            dma((pieces, 3)),
            dma((3,)),
            dma((3,)),
            dma((8,)),
            dma((8,)),
        ],
        compiler_params=pltpu.CompilerParams(
            collective_id=1, has_side_effects=True, vmem_limit_bytes=VMEM_BYTES
        ),
    )(
        *kept,
        a_turned,
        *[saved[name] for name in BWD_ANY],
        saved["st"],
        saved["r8"],
        cos,
        sin,
        tokens,
        out_grad,
        lengths,
    )
    return outs[:N_W], outs[N_W]


def hand_out_kernel(turned, *refs):
    count = (len(refs) - 2 - len(turned)) // 3
    ins, outs, bufs = (refs[i * count : (i + 1) * count] for i in range(3))
    flipped, (load_sem, store_sem) = refs[3 * count : -2], refs[-2:]
    loads = [pltpu.make_async_copy(ins[i], bufs[i], load_sem.at[i]) for i in range(count)]
    order = [*turned, *(i for i in range(count) if i not in turned)]
    stores = []
    for i in order:
        loads[i].start()
    for i in order:
        loads[i].wait()
        source = bufs[i]
        if i in turned:
            source = flipped[turned.index(i)]
            source[...] = bufs[i][...].T
        stores.append(pltpu.make_async_copy(source, outs[i], store_sem.at[i]))
        stores[-1].start()
    for store in stores:
        store.wait()


def hand_out(arrays, turned):
    anywhere = pl.BlockSpec(memory_space=pl.ANY)
    shapes = [a.shape[::-1] if i in turned else a.shape for i, a in enumerate(arrays)]
    outs = pl.pallas_call(
        functools.partial(hand_out_kernel, turned),
        name="hand_out",
        out_shape=[jax.ShapeDtypeStruct(s, a.dtype) for s, a in zip(shapes, arrays)],
        in_specs=[anywhere] * len(arrays),
        out_specs=[anywhere] * len(arrays),
        scratch_shapes=[
            *[pltpu.VMEM(a.shape, a.dtype) for a in arrays],
            *[pltpu.VMEM(shapes[i], arrays[i].dtype) for i in turned],
            pltpu.SemaphoreType.DMA((len(arrays),)),
            pltpu.SemaphoreType.DMA((len(arrays),)),
        ],
    )(*arrays)
    return [out.T if i in turned else out for i, out in enumerate(outs)]


def body_by_kernels(
    tokens,
    lengths,
    rates,
    w_query,
    w_key,
    w_value,
    w_update,
    w_output,
    w_gate,
    w_up,
    w_down,
    out_grad,
):
    rows = tokens.shape[0]
    ends = jnp.cumsum(lengths[0], dtype=jnp.int32)
    places = lax.axis_index("tp") * rows + jnp.arange(rows, dtype=jnp.int32)
    segments = segment_of(places, ends)
    slots = jnp.arange(SLOTS, dtype=jnp.int32)
    starts = jnp.sum(jnp.where(segments[:, None] == slots, ends - lengths[0], 0), axis=1)
    positions = (places - starts).astype(jnp.float32)
    frequency = 10000.0 ** (-2.0 * jnp.arange(HEAD_DIM // 2, dtype=jnp.float32) / HEAD_DIM)
    turned = positions[:, None] * frequency[None, :]
    cos_half, sin_half = jnp.cos(turned), jnp.sin(turned)
    cos = jnp.concatenate([cos_half, cos_half], axis=1)
    sin = jnp.concatenate([-sin_half, sin_half], axis=1)
    shards = (w_query, w_key, w_value, w_update, w_output, w_gate.T, w_up.T, w_down)
    kept, a_turned, saved = forward(shards, tokens, cos, sin, lengths, rates)
    grads, d_tokens = backward(kept, a_turned, saved, cos, sin, tokens, out_grad, lengths)
    return tuple(hand_out([saved["res"], d_tokens, *grads], (7, 8)))


def body(
    tokens,
    lengths,
    rates,
    w_query,
    w_key,
    w_value,
    w_update,
    w_output,
    w_gate,
    w_up,
    w_down,
    out_grad,
):
    tp_count = lax.axis_size("tp")
    tp_index = lax.axis_index("tp")
    rows, width = tokens.shape
    head_width = HEAD_DIM
    all_rates = lax.all_gather(rates, "tp", axis=0, tiled=True)
    heads = all_rates.shape[0]
    ends = jnp.cumsum(lengths[0], dtype=jnp.int32)
    first = tp_index * rows
    places = first + jnp.arange(rows, dtype=jnp.int32)
    segments = segment_of(places, ends)
    starts = ends - lengths[0]
    slots = jnp.arange(SLOTS, dtype=jnp.int32)
    positions = (
        places - jnp.sum(jnp.where(segments[:, None] == slots, starts, 0), axis=1)
    ).astype(jnp.float32)
    live = (segments < SLOTS - 1).astype(jnp.float32)
    frequency = 10000.0 ** (-2.0 * jnp.arange(head_width // 2, dtype=jnp.float32) / head_width)
    turned = positions[:, None] * frequency[None, :]
    cos_table, sin_table = jnp.cos(turned)[:, None, :], jnp.sin(turned)[:, None, :]

    gaps = places[:, None] - places[None, :]
    allowed = (segments[:, None] == segments[None, :]) & (gaps >= 0)
    spans = jnp.maximum(gaps, 0).astype(jnp.float32)
    decay = jnp.where(
        allowed[None], jnp.exp(-all_rates[:, None, None] * spans[None]), 0.0
    )
    blocks = jnp.arange(tp_count, dtype=jnp.int32)
    seg_before = segment_of(first - 1, ends)
    seg_after = segment_of(first + rows, ends)
    seg_last = segment_of(blocks * rows + rows - 1, ends)
    seg_first = segment_of(blocks * rows, ends)
    offsets = jnp.arange(rows, dtype=jnp.float32)

    def row_decay(distance, mask):
        return jnp.where(mask[:, None], jnp.exp(-distance[:, None] * all_rates[None]), 0.0)[
            :, :, None
        ]

    to_end = row_decay(rows - 1 - offsets, segments == segments[rows - 1])
    from_start = row_decay(offsets, segments == segments[0])
    into = row_decay(offsets + 1.0, segments == seg_before)
    out_of = row_decay(rows - offsets, segments == seg_after)

    def block_weights(mask, distance):
        distance = jnp.maximum(distance, 0).astype(jnp.float32)
        return jnp.where(mask[:, None], jnp.exp(-distance[:, None] * all_rates[None]), 0.0)

    before_weights = block_weights(
        (blocks < tp_index) & (seg_last == seg_before), (tp_index - blocks - 1) * rows
    )
    after_weights = block_weights(
        (blocks > tp_index) & (seg_first == seg_after), (blocks - tp_index - 1) * rows
    )

    tokens_f = tokens.astype(jnp.float32)
    scale1 = rms_scale(tokens_f)
    normed1 = (tokens_f * scale1).astype(jnp.bfloat16)
    shards = (w_query, w_key, w_value, w_update, w_output, w_gate, w_up, w_down)
    inner = (True, True, True, True, False, True, True, False)
    full = [
        gather_full(w, "fsdp", "tp") if rows_first else gather_full(w, "tp", "fsdp")
        for w, rows_first in zip(shards, inner)
    ]
    (
        query_full,
        key_full,
        value_full,
        update_full,
        output_full,
        gate_full,
        up_full,
        down_full,
    ) = full
    shape_heads = (rows, heads, head_width)
    query_pre = mm(normed1, query_full)
    key_pre = mm(normed1, key_full)
    value_rows = mm(normed1, value_full).astype(jnp.bfloat16).reshape(shape_heads)
    update_pre = mm(normed1, update_full)
    query = rotate(swish(query_pre).reshape(shape_heads), cos_table, sin_table).astype(jnp.bfloat16)
    key_rows = rotate(swish(key_pre).reshape(shape_heads), cos_table, sin_table).astype(
        jnp.bfloat16
    )
    update = swish(update_pre)
    key_state = heads_dot(
        "shc,shd->hcd", (key_rows * to_end).astype(jnp.bfloat16), value_rows
    ).astype(jnp.bfloat16)
    key_states = lax.all_gather(key_state, "tp", axis=0, tiled=False)
    state_in = jnp.sum(
        key_states.astype(jnp.float32) * before_weights[:, :, None, None], axis=0
    ).astype(jnp.bfloat16)
    weights = (heads_dot("thc,shc->hts", query, key_rows) * decay).astype(jnp.bfloat16)
    attn = heads_dot("hts,shd->thd", weights, value_rows) + into * heads_dot(
        "thc,hcd->thd", query, state_in
    )
    scale_attn = rms_scale(attn, head_floor)
    normed_attn = (attn * scale_attn).reshape(rows, width)
    mixed = (normed_attn * update).astype(jnp.bfloat16)
    middle = tokens_f + mm(mixed, output_full)
    scale2 = rms_scale(middle)
    normed2 = (middle * scale2).astype(jnp.bfloat16)
    gate_rows = mm(normed2, gate_full)
    up_rows = mm(normed2, up_full)
    hidden = (gate_rows * up_rows).astype(jnp.bfloat16)
    result = (middle + mm(hidden, down_full)).astype(jnp.bfloat16)

    cotangent = out_grad.astype(jnp.float32) * live[:, None]
    cot_rows = cotangent.astype(jnp.bfloat16)
    grad_down = mm_inner(hidden, cot_rows)
    d_hidden = mm_trans(cot_rows, down_full)
    d_gate = (d_hidden * up_rows).astype(jnp.bfloat16)
    d_up = (d_hidden * gate_rows).astype(jnp.bfloat16)
    grad_gate = mm_inner(normed2, d_gate)
    grad_up = mm_inner(normed2, d_up)
    d_normed2 = mm_trans(d_gate, gate_full) + mm_trans(d_up, up_full)
    d_middle = cotangent + norm_back(middle, scale2, d_normed2)
    mid_rows = d_middle.astype(jnp.bfloat16)
    d_mixed = mm_trans(mid_rows, output_full)
    grad_output = mm_inner(mixed, mid_rows)
    d_update_pre = (d_mixed * normed_attn * swish_slope(update_pre)).astype(jnp.bfloat16)
    d_attn = norm_back(attn, scale_attn, (d_mixed * update).reshape(shape_heads)).astype(
        jnp.bfloat16
    )
    query_state = heads_dot(
        "thc,thd->hcd", (query * from_start).astype(jnp.bfloat16), d_attn
    ).astype(jnp.bfloat16)
    query_states = lax.all_gather(query_state, "tp", axis=0, tiled=False)
    state_back = jnp.sum(
        query_states.astype(jnp.float32) * after_weights[:, :, None, None], axis=0
    ).astype(jnp.bfloat16)
    d_raw = (heads_dot("thd,shd->hts", d_attn, value_rows) * decay).astype(jnp.bfloat16)
    d_value = heads_dot("hts,thd->shd", weights, d_attn) + out_of * heads_dot(
        "shc,hcd->shd", key_rows, state_back
    )
    d_query = heads_dot("hts,shc->thc", d_raw, key_rows) + into * heads_dot(
        "thd,hcd->thc", d_attn, state_in
    )
    d_key = heads_dot("hts,thc->shc", d_raw, query) + out_of * heads_dot(
        "shd,hcd->shc", value_rows, state_back
    )
    d_query_pre = (
        swish_slope(query_pre) * rotate_back(d_query, cos_table, sin_table).reshape(rows, width)
    ).astype(jnp.bfloat16)
    d_key_pre = (
        swish_slope(key_pre) * rotate_back(d_key, cos_table, sin_table).reshape(rows, width)
    ).astype(jnp.bfloat16)
    d_value_pre = d_value.reshape(rows, width).astype(jnp.bfloat16)
    grads = [mm_inner(normed1, d) for d in (d_query_pre, d_key_pre, d_value_pre, d_update_pre)]
    d_normed1 = (
        mm_trans(d_query_pre, query_full)
        + mm_trans(d_key_pre, key_full)
        + mm_trans(d_value_pre, value_full)
        + mm_trans(d_update_pre, update_full)
    )
    d_tokens = d_middle + norm_back(tokens_f, scale1, d_normed1)
    grads = (*grads, grad_output, grad_gate, grad_up, grad_down)
    grads = [
        scatter_grad(g, "fsdp", "tp") if rows_first else scatter_grad(g, "tp", "fsdp")
        for g, rows_first in zip(grads, inner)
    ]
    return (result, d_tokens, *grads)


def solution(mesh):
    rows = P(AXES, None)
    inner, outer = P("fsdp", "tp"), P("tp", "fsdp")
    by_kernels = mesh.shape["fsdp"] == 8 and mesh.shape["tp"] == 4
    return jax.shard_map(
        body_by_kernels if by_kernels else body,
        mesh=mesh,
        in_specs=(
            rows,
            P("fsdp", None),
            P("tp"),
            inner,
            inner,
            inner,
            inner,
            outer,
            inner,
            inner,
            outer,
            rows,
        ),
        out_specs=(rows, rows, inner, inner, inner, inner, outer, inner, inner, outer),
        check_vma=False,
    )
```
